32 devices in a mesh: slab: 2 (over y), tile: 4 (over z), view: 4 (over x, core).
Axes of the slice: x: 2, y: 2, z: 4, core: 2. Of those that a mesh axis runs over, the one named last changes fastest.
Arguments:
- recorded: float32 [4, 96, 32, 1024], P('view', 'tile', 'slab'), parts along dimension 2, may hold values from 0.5 to 2
- psf_taps: float32 [4, 3, 15], P('view'), may hold values from 0.2 to 1
- estimate: float32 [96, 32, 1024], P('tile', 'slab'), parts along dimension 1, may hold values from 0.5 to 2
Outputs:
- joined: float32 [96, 32, 1024], P('tile', 'slab'), parts along dimension 1
The draws below stay inside these ranges and needn't reach their ends.
There are 2 independent parts, one for each index of `slab`. The reference program is written for one: setup_inputs(seed, part) draws one part's arguments, and reference() takes and returns one part's arrays. A program takes and returns all parts, laid end to end along the dimension named above; an argument that names none is the same for every part. Nothing has to cross between parts.
All inputs are finite; a program needn't handle non-finite values.
Results may differ from the reference program's by a relative error of at most 0.00002.
Values sent between devices are 32-bit elements; how exact they have to be, the bound alone decides.
No kernel may reach another device: no remote copies, remote signals or barrier semaphores. Data moves between devices by JAX's collectives and lax.ppermute only.
A program may use at most 64 MiB of HBM per device.

```python
import math
import jax
import jax.numpy as jnp
from jax import lax

NZ = 16
NY = 1024
RADIUS = 7
ITERS = 2
TAPS = 15
VIEWS = 4
NX = 96


def steps_of(key, extent, split, smallest, top_value):
    loudness = 1.0
    for position, shards_of in split:
        steps = jax.random.uniform(jax.random.fold_in(jax.random.fold_in(key, 6), position), (shards_of,), jnp.float32, smallest / len(split), top_value / len(split))
        loudness = loudness * jnp.repeat(jnp.exp(steps), extent[position] // shards_of).reshape((-1,) + (1,) * (len(extent) - 1 - position))
    return loudness


def setup_inputs(seed: int = 0, part: int = 0) -> dict:
    streams_of = jax.random.split(jax.random.key(seed), 4)
    part_keys = jax.random.split(jax.random.fold_in(streams_of[3], part), 4)
    recorded = jnp.clip(0.5 + 1.5 * jax.random.uniform(part_keys[0], (VIEWS, NX, NZ, NY), jnp.float32) ** steps_of(part_keys[0], (VIEWS, NX, NZ, NY), ((0, 4), (1, 4)), -0.2, 0.2), 0.5, 2.0)
    psf_taps = jnp.clip(jnp.exp(math.log(1.0) - 1.609438 * jax.random.uniform(streams_of[1], (VIEWS, 3, TAPS), jnp.float32) ** steps_of(streams_of[1], (VIEWS, 3, TAPS), ((0, 4),), -0.2, 0.2)), 0.2, 1.0)
    estimate = jnp.clip(0.5 + 1.5 * jax.random.uniform(part_keys[2], (NX, NZ, NY), jnp.float32) ** steps_of(part_keys[2], (NX, NZ, NY), ((0, 4),), -0.2, 0.2), 0.5, 2.0)
    return dict(recorded=recorded, psf_taps=psf_taps, estimate=estimate)


def valid_along(padded, kernel_row, axis_num, mirrored):
    length_out = padded.shape[axis_num] - 2 * RADIUS
    summed = jnp.zeros(padded.shape[:axis_num] + (length_out,) + padded.shape[axis_num + 1:], jnp.float32)
    for offset in range(2 * RADIUS + 1):
        weight = kernel_row[2 * RADIUS - offset] if mirrored else kernel_row[offset]
        summed = summed + weight * lax.slice_in_dim(padded, offset, offset + length_out, axis=axis_num)
    return summed


def along(values_in, kernel_row, axis_num, mirrored):
    widths = [(0, 0)] * values_in.ndim
    widths[axis_num] = (RADIUS, RADIUS)
    return valid_along(jnp.pad(values_in, widths), kernel_row, axis_num, mirrored)


def blur(values_in, kernel_view, mirrored):
    result = along(values_in, kernel_view[0], 0, mirrored)
    result = along(result, kernel_view[1], 1, mirrored)
    return along(result, kernel_view[2], 2, mirrored)


def reference(recorded, psf_taps, estimate):
    kernel = psf_taps / jnp.sum(psf_taps, axis=2, keepdims=True)
    for iteration in range(ITERS):
        log_total = jnp.zeros(estimate.shape, jnp.float32)
        for view_num in range(VIEWS):
            blurred = blur(estimate, kernel[view_num], False)
            quotient = recorded[view_num] / blurred
            correction = blur(quotient, kernel[view_num], True)
            log_total = log_total + jnp.log(correction)
        estimate = estimate * jnp.exp(log_total / VIEWS)
    return estimate
```

```python
import functools

import jax
import jax.numpy as jnp
from jax import lax
from jax.experimental import pallas as pl
from jax.experimental.pallas import tpu as pltpu
from jax.sharding import PartitionSpec as P

RADIUS = 7
ITERS = 2
TAPS = 2 * RADIUS + 1
LANES = 128
ROWS = 256
BF = jnp.bfloat16
F32 = jnp.float32
VMEM = pl.BlockSpec(memory_space=pltpu.VMEM)
SMEM = pl.BlockSpec(memory_space=pltpu.SMEM)
PARAMS = pltpu.CompilerParams(vmem_limit_bytes=60 * 1024 * 1024)


def halves(value):
    high = value.astype(BF)
    return high, (value - high.astype(F32)).astype(BF)


def dot(a, b):
    return jnp.dot(a, b, preferred_element_type=F32)


def dot3(a, b):
    return dot(a[0], b[0]) + (dot(a[1], b[0]) + dot(a[0], b[1]))


def operators_kernel(nz, kern, th, tl, wh, wl):
    planes = ROWS // nz
    i = lax.broadcasted_iota(jnp.int32, (2 * ROWS, ROWS), 0)
    o = lax.broadcasted_iota(jnp.int32, (2 * ROWS, ROWS), 1)
    shift_y = i - o - (LANES - RADIUS)
    row = lax.broadcasted_iota(jnp.int32, (ROWS, 2 * ROWS), 0)
    col = lax.broadcasted_iota(jnp.int32, (ROWS, 2 * ROWS), 1)
    shift_x = col // nz - row // nz
    shift_z = col % nz - row % nz + RADIUS
    for mirrored in range(2):
        ty = jnp.zeros((2 * ROWS, ROWS), F32)
        kx = jnp.zeros((ROWS, 2 * ROWS), F32)
        kz = jnp.zeros((ROWS, 2 * ROWS), F32)
        for k in range(TAPS):
            tap = TAPS - 1 - k if mirrored else k
            kx = jnp.where(shift_x == k, kern[0, tap], kx)
            kz = jnp.where(shift_z == k, kern[1, tap], kz)
            ty = jnp.where(shift_y == k, kern[2, tap], ty)
        th[mirrored], tl[mirrored] = halves(ty)
        wh[mirrored], wl[mirrored] = halves(kx * kz)


def operators(kern, nz):
    t = jax.ShapeDtypeStruct((2, 2 * ROWS, ROWS), BF)
    w = jax.ShapeDtypeStruct((2, ROWS, 2 * ROWS), BF)
    return pl.pallas_call(
        functools.partial(operators_kernel, nz),
        out_shape=(t, t, w, w),
        in_specs=[SMEM],
        out_specs=(VMEM,) * 4,
        compiler_params=PARAMS,
        name="operators",
    )(kern)


def blur_y(x, th, tl, store):
    width = x.shape[1]
    xh, xl = halves(x)
    for o0 in range(0, width, ROWS):
        size = min(ROWS, width - o0)
        k0, k1 = max(0, o0 - LANES), min(width, o0 + size + LANES)
        t0 = k0 - (o0 - LANES)
        rows = slice(t0, t0 + k1 - k0)
        t = (th[rows, :size], tl[rows, :size])
        store(o0, size, dot3((xh[:, k0:k1], xl[:, k0:k1]), t))


def blur_xz(dh, dl, wh, wl, nz, planes_out, store):
    width = dh.shape[1]
    step = ROWS // nz
    for p0 in range(0, planes_out, step):
        planes = min(step, planes_out - p0)
        m = planes * nz
        k = min(2 * ROWS, (planes_out + 2 * RADIUS - p0) * nz)
        for o0 in range(0, width, ROWS):
            size = min(ROWS, width - o0)
            d = (
                dh[p0 * nz : p0 * nz + k, o0 : o0 + size],
                dl[p0 * nz : p0 * nz + k, o0 : o0 + size],
            )
            store(p0 * nz, m, o0, size, dot3((wh[:m, :k], wl[:m, :k]), d))


def to_halves(dh, dl, r0, n):
    def store(o0, size, value):
        h, l = halves(value)
        dh[r0 : r0 + n, o0 : o0 + size] = h
        dl[r0 : r0 + n, o0 : o0 + size] = l

    return store


def chunks(rows, step=128):
    return [(r, min(step, rows - r)) for r in range(0, rows, step)]


def own_kernel(est, th, tl, dh, dl):
    for r0, n in chunks(est.shape[0]):
        blur_y(est[r0 : r0 + n, :], th.at[0], tl.at[0], to_halves(dh, dl, r0, n))


def own_blur_y(est, ops):
    out = jax.ShapeDtypeStruct(est.shape, BF)
    return pl.pallas_call(
        own_kernel,
        out_shape=(out, out),
        in_specs=[VMEM] * 3,
        out_specs=(VMEM, VMEM),
        compiler_params=PARAMS,
        name="own_blur_y",
    )(est, ops[0], ops[1])


def forward_kernel(nz, core, mine, other, oh, ol, th, tl, wh, wl, blurred, rims, dh, dl):
    width = oh.shape[1]
    half = nz // 2
    rim = mine.shape[1]
    c = core[0]
    a = pl.multiple_of(c * half, half)
    b = pl.multiple_of((1 - c) * half, half)
    for side in range(2):
        rims[side, :, pl.ds(a, half), :] = mine[side]
        rims[side, :, pl.ds(b, half), :] = other[side]
    own = oh.shape[0]
    for side in range(2):
        base = 0 if side == 0 else rim * nz + own
        flat = rims[side].reshape(rim * nz, width)
        for r0, n in chunks(rim * nz, 112):
            blur_y(flat[r0 : r0 + n, :], th.at[0], tl.at[0], to_halves(dh, dl, base + r0, n))
    dh[rim * nz : rim * nz + own, :] = oh[...]
    dl[rim * nz : rim * nz + own, :] = ol[...]

    def store(r0, m, o0, size, value):
        blurred[r0 : r0 + m, o0 : o0 + size] = value

    blur_xz(dh, dl, wh.at[0], wl.at[0], nz, blurred.shape[0] // nz, store)


def forward(core, mine, other, own, ops, nz):
    rim = mine.shape[1]
    rows, width = own[0].shape
    total = rows + 2 * rim * nz
    return pl.pallas_call(
        functools.partial(forward_kernel, nz),
        out_shape=jax.ShapeDtypeStruct((total - 2 * RADIUS * nz, width), F32),
        in_specs=[SMEM] + [VMEM] * 8,
        out_specs=VMEM,
        scratch_shapes=[
            pltpu.VMEM((2, rim, nz, width), F32),
            pltpu.VMEM((total, width), BF),
            pltpu.VMEM((total, width), BF),
        ],
        compiler_params=PARAMS,
        name="forward",
    )(core, mine, other, own[0], own[1], *ops)


def adjoint_kernel(nz, rim_rows, blurred, before, own, after, th, tl, wh, wl, added, out, dh, dl):
    rows = own.shape[0]
    parts = ((before, 0, rim_rows), (own, rim_rows, rows), (after, rim_rows + rows, rim_rows))
    for ref, base, count in parts:
        for r0, n in chunks(count):
            q = ref[r0 : r0 + n, :] / blurred[base + r0 : base + r0 + n, :]
            blur_y(q, th.at[1], tl.at[1], to_halves(dh, dl, base + r0, n))

    def store(r0, m, o0, size, value):
        log = jnp.log(value)
        if added is not None:
            log = log + added[r0 : r0 + m, o0 : o0 + size]
        out[r0 : r0 + m, o0 : o0 + size] = log

    blur_xz(dh, dl, wh.at[1], wl.at[1], nz, rows // nz, store)


def adjoint(blurred, before, own, after, ops, added, nz):
    rows, width = own.shape
    args = [blurred, before, own, after, *ops]
    kernel = functools.partial(adjoint_kernel, nz, before.shape[0])
    if added is None:
        body = lambda *refs: kernel(*refs[:8], None, *refs[8:])
    else:
        body = kernel
        args.append(added)
    return pl.pallas_call(
        body,
        out_shape=jax.ShapeDtypeStruct((rows, width), F32),
        in_specs=[VMEM] * len(args),
        out_specs=VMEM,
        scratch_shapes=[pltpu.VMEM(blurred.shape, BF), pltpu.VMEM(blurred.shape, BF)],
        compiler_params=PARAMS,
        name="adjoint",
    )(*args)


def local(recorded, psf_taps, estimate):
    views = lax.axis_size("view")
    cores = 2
    chips = views // cores
    tiles = lax.axis_size("tile")
    nx, nz, ny = estimate.shape
    half = nz // 2
    place = lax.axis_index("view")
    chip, core = place // cores, place % cores
    core_arr = core.astype(jnp.int32).reshape(1)

    part = ny // chips
    width = min(ny, part + (LANES if chips <= 2 else 2 * LANES))

    def start_of(c):
        return jnp.clip(c * part - LANES, 0, ny - width)

    start = start_of(chip)

    def window(values, of):
        return lax.dynamic_slice_in_dim(values, start_of(of), width, axis=2)

    def swap_core(values):
        pairs = [(v, v ^ 1) for v in range(views)]
        return lax.ppermute(values, "view", pairs)

    def to_chip(values, r):
        pairs = [(v, (v + r * cores) % views) for v in range(views)]
        return lax.ppermute(values, "view", pairs)

    up = [(t, t + 1) for t in range(tiles - 1)]
    down = [(t + 1, t) for t in range(tiles - 1)]

    def rims(first, last):
        return lax.ppermute(last, "tile", up), lax.ppermute(first, "tile", down)

    def estimate_rims(est):
        sel = lax.dynamic_slice_in_dim(est, core * half, half, axis=1)
        mine = jnp.stack(rims(sel[: 2 * RADIUS], sel[nx - 2 * RADIUS :]))
        return mine, swap_core(mine)

    recorded = recorded[0]
    est = window(estimate, chip)
    est_rims = estimate_rims(est)

    kern = psf_taps[0] / jnp.sum(psf_taps[0], axis=1, keepdims=True)
    kerns = [kern] + [to_chip(kern, r) for r in range(1, chips)]

    own = window(recorded, chip)
    record = [(own, *rims(own[:RADIUS], own[nx - RADIUS :]))]
    for r in range(1, chips):
        sent = window(recorded, (chip + r) % chips)
        edges = to_chip(jnp.concatenate([sent[:RADIUS], sent[nx - RADIUS :]]), r)
        middle = to_chip(sent[RADIUS : nx - RADIUS], r)
        first, last = edges[:RADIUS], edges[RADIUS:]
        record.append((jnp.concatenate([first, middle, last]), *rims(first, last)))

    ops = [operators(k, nz) for k in kerns]
    flat = lambda a: a.reshape(-1, a.shape[-1])

    for iteration in range(ITERS):
        if iteration:
            est_rims = estimate_rims(est)
        total = None
        owns = [own_blur_y(flat(est), op[:2]) for op in ops]
        for rec, op, done in zip(record, ops, owns):
            blurred = forward(core_arr, *est_rims, done, op, nz)
            total = adjoint(blurred, flat(rec[1]), flat(rec[0]), flat(rec[2]), op, total, nz)
        if iteration < ITERS - 1:
            total = (total + swap_core(total)).reshape(est.shape)
            est = est * jnp.exp(total / views)

    offset = chip * part - start
    total = lax.dynamic_slice_in_dim(total.reshape(est.shape), offset, part, axis=2)
    est = lax.dynamic_slice_in_dim(est, offset, part, axis=2)
    pick = lambda a, c: lax.dynamic_slice_in_dim(a, c * half, half, axis=1)
    total = pick(total, core) + swap_core(pick(total, 1 - core))
    est = pick(est, core) * jnp.exp(total / views)
    parts = jnp.stack([est] + [to_chip(est, r) for r in range(1, chips)])
    others = swap_core(parts)
    joined = jnp.where(
        core == 0, jnp.concatenate([parts, others], 2), jnp.concatenate([others, parts], 2)
    )
    out = jnp.zeros((nx, nz, ny), F32)
    for r in range(chips):
        at = ((chip - r) % chips) * part
        out = lax.dynamic_update_slice_in_dim(out, joined[r], at, axis=2)
    return out


def solution(mesh):
    in_specs = (P("view", "tile", "slab", None), P("view", None, None), P("tile", "slab", None))
    out_specs = P("tile", "slab", None)
    return jax.shard_map(local, mesh=mesh, in_specs=in_specs, out_specs=out_specs, check_vma=False)
```

```python
import functools

import jax
import jax.numpy as jnp
from jax import lax
from jax.experimental import pallas as pl
from jax.experimental.pallas import tpu as pltpu
from jax.sharding import PartitionSpec as P

RADIUS = 7
ITERS = 2
TAPS = 2 * RADIUS + 1
LANES = 128
ROWS = 256
BF = jnp.bfloat16
F32 = jnp.float32
VMEM = pl.BlockSpec(memory_space=pltpu.VMEM)
SMEM = pl.BlockSpec(memory_space=pltpu.SMEM)
PARAMS = pltpu.CompilerParams(vmem_limit_bytes=20 * 1024 * 1024)


def halves(value):
    high = value.astype(BF)
    return high, (value - high.astype(F32)).astype(BF)


def dot(a, b):
    return jnp.dot(a, b, preferred_element_type=F32)


def dot3(a, b):
    return dot(a[0], b[0]) + (dot(a[1], b[0]) + dot(a[0], b[1]))


def operators_kernel(nz, kern, th, tl, wh, wl):
    planes = ROWS // nz
    i = lax.broadcasted_iota(jnp.int32, (2 * ROWS, ROWS), 0)
    o = lax.broadcasted_iota(jnp.int32, (2 * ROWS, ROWS), 1)
    shift_y = i - o - (LANES - RADIUS)
    row = lax.broadcasted_iota(jnp.int32, (ROWS, 2 * ROWS), 0)
    col = lax.broadcasted_iota(jnp.int32, (ROWS, 2 * ROWS), 1)
    shift_x = col // nz - row // nz
    shift_z = col % nz - row % nz + RADIUS
    for mirrored in range(2):
        ty = jnp.zeros((2 * ROWS, ROWS), F32)
        kx = jnp.zeros((ROWS, 2 * ROWS), F32)
        kz = jnp.zeros((ROWS, 2 * ROWS), F32)
        for k in range(TAPS):
            tap = TAPS - 1 - k if mirrored else k
            kx = jnp.where(shift_x == k, kern[0, tap], kx)
            kz = jnp.where(shift_z == k, kern[1, tap], kz)
            ty = jnp.where(shift_y == k, kern[2, tap], ty)
        th[mirrored], tl[mirrored] = halves(ty)
        wh[mirrored], wl[mirrored] = halves(kx * kz)


def operators(kern, nz):
    t = jax.ShapeDtypeStruct((2, 2 * ROWS, ROWS), BF)
    w = jax.ShapeDtypeStruct((2, ROWS, 2 * ROWS), BF)
    return pl.pallas_call(
        functools.partial(operators_kernel, nz),
        out_shape=(t, t, w, w),
        in_specs=[SMEM],
        out_specs=(VMEM,) * 4,
        compiler_params=PARAMS,
        name="operators",
    )(kern)


def blur_y(x, th, tl, store):
    width = x.shape[1]
    xh, xl = halves(x)
    for o0 in range(0, width, ROWS):
        size = min(ROWS, width - o0)
        k0, k1 = max(0, o0 - LANES), min(width, o0 + size + LANES)
        t0 = k0 - (o0 - LANES)
        rows = slice(t0, t0 + k1 - k0)
        t = (th[rows, :size], tl[rows, :size])
        store(o0, size, dot3((xh[:, k0:k1], xl[:, k0:k1]), t))


def blur_xz(dh, dl, wh, wl, nz, planes_out, store):
    width = dh.shape[1]
    step = ROWS // nz
    for p0 in range(0, planes_out, step):
        planes = min(step, planes_out - p0)
        m = planes * nz
        k = min(2 * ROWS, (planes_out + 2 * RADIUS - p0) * nz)
        for o0 in range(0, width, ROWS):
            size = min(ROWS, width - o0)
            d = (
                dh[p0 * nz : p0 * nz + k, o0 : o0 + size],
                dl[p0 * nz : p0 * nz + k, o0 : o0 + size],
            )
            store(p0 * nz, m, o0, size, dot3((wh[:m, :k], wl[:m, :k]), d))


def to_halves(dh, dl, r0, n):
    def store(o0, size, value):
        h, l = halves(value)
        dh[r0 : r0 + n, o0 : o0 + size] = h
        dl[r0 : r0 + n, o0 : o0 + size] = l

    return store


def chunks(rows, step=128):
    return [(r, min(step, rows - r)) for r in range(0, rows, step)]


def own_kernel(est, th, tl, dh, dl):
    for r0, n in chunks(est.shape[0]):
        blur_y(est[r0 : r0 + n, :], th.at[0], tl.at[0], to_halves(dh, dl, r0, n))


def own_blur_y(est, ops):
    out = jax.ShapeDtypeStruct(est.shape, BF)
    return pl.pallas_call(
        own_kernel,
        out_shape=(out, out),
        in_specs=[VMEM] * 3,
        out_specs=(VMEM, VMEM),
        compiler_params=PARAMS,
        name="own_blur_y",
    )(est, ops[0], ops[1])


def forward_kernel(nz, core, mine, other, oh, ol, th, tl, wh, wl, blurred, rims, dh, dl):
    width = oh.shape[1]
    half = nz // 2
    rim = mine.shape[1]
    c = core[0]
    a = pl.multiple_of(c * half, half)
    b = pl.multiple_of((1 - c) * half, half)
    for side in range(2):
        rims[side, :, pl.ds(a, half), :] = mine[side]
        rims[side, :, pl.ds(b, half), :] = other[side]
    own = oh.shape[0]
    for side in range(2):
        base = 0 if side == 0 else rim * nz + own
        flat = rims[side].reshape(rim * nz, width)
        for r0, n in chunks(rim * nz, 112):
            blur_y(flat[r0 : r0 + n, :], th.at[0], tl.at[0], to_halves(dh, dl, base + r0, n))
    dh[rim * nz : rim * nz + own, :] = oh[...]
    dl[rim * nz : rim * nz + own, :] = ol[...]

    def store(r0, m, o0, size, value):
        blurred[r0 : r0 + m, o0 : o0 + size] = value

    blur_xz(dh, dl, wh.at[0], wl.at[0], nz, blurred.shape[0] // nz, store)


def forward(core, mine, other, own, ops, nz):
    rim = mine.shape[1]
    rows, width = own[0].shape
    total = rows + 2 * rim * nz
    return pl.pallas_call(
        functools.partial(forward_kernel, nz),
        out_shape=jax.ShapeDtypeStruct((total - 2 * RADIUS * nz, width), F32),
        in_specs=[SMEM] + [VMEM] * 8,
        out_specs=VMEM,
        scratch_shapes=[
            pltpu.VMEM((2, rim, nz, width), F32),
            pltpu.VMEM((total, width), BF),
            pltpu.VMEM((total, width), BF),
        ],
        compiler_params=PARAMS,
        name="forward",
    )(core, mine, other, own[0], own[1], *ops)


def adjoint_kernel(nz, rim_rows, blurred, before, own, after, th, tl, wh, wl, added, out, dh, dl):
    rows = own.shape[0]
    parts = ((before, 0, rim_rows), (own, rim_rows, rows), (after, rim_rows + rows, rim_rows))
    for ref, base, count in parts:
        for r0, n in chunks(count):
            q = ref[r0 : r0 + n, :] / blurred[base + r0 : base + r0 + n, :]
            blur_y(q, th.at[1], tl.at[1], to_halves(dh, dl, base + r0, n))

    def store(r0, m, o0, size, value):
        log = jnp.log(value)
        if added is not None:
            log = log + added[r0 : r0 + m, o0 : o0 + size]
        out[r0 : r0 + m, o0 : o0 + size] = log

    blur_xz(dh, dl, wh.at[1], wl.at[1], nz, rows // nz, store)


def adjoint(blurred, before, own, after, ops, added, nz):
    rows, width = own.shape
    args = [blurred, before, own, after, *ops]
    kernel = functools.partial(adjoint_kernel, nz, before.shape[0])
    if added is None:
        body = lambda *refs: kernel(*refs[:8], None, *refs[8:])
    else:
        body = kernel
        args.append(added)
    return pl.pallas_call(
        body,
        out_shape=jax.ShapeDtypeStruct((rows, width), F32),
        in_specs=[VMEM] * len(args),
        out_specs=VMEM,
        scratch_shapes=[pltpu.VMEM(blurred.shape, BF), pltpu.VMEM(blurred.shape, BF)],
        compiler_params=PARAMS,
        name="adjoint",
    )(*args)


def local(recorded, psf_taps, estimate):
    views = lax.axis_size("view")
    cores = 2
    chips = views // cores
    tiles = lax.axis_size("tile")
    nx, nz, ny = estimate.shape
    half = nz // 2
    place = lax.axis_index("view")
    chip, core = place // cores, place % cores
    core_arr = core.astype(jnp.int32).reshape(1)

    part = ny // chips
    width = min(ny, part + (LANES if chips <= 2 else 2 * LANES))

    def start_of(c):
        return jnp.clip(c * part - LANES, 0, ny - width)

    start = start_of(chip)

    def window(values, of):
        return lax.dynamic_slice_in_dim(values, start_of(of), width, axis=2)

    def swap_core(values):
        pairs = [(v, v ^ 1) for v in range(views)]
        return lax.ppermute(values, "view", pairs)

    def to_chip(values, r):
        pairs = [(v, (v + r * cores) % views) for v in range(views)]
        return lax.ppermute(values, "view", pairs)

    up = [(t, t + 1) for t in range(tiles - 1)]
    down = [(t + 1, t) for t in range(tiles - 1)]

    def rims(first, last):
        return lax.ppermute(last, "tile", up), lax.ppermute(first, "tile", down)

    def estimate_rims(est):
        sel = lax.dynamic_slice_in_dim(est, core * half, half, axis=1)
        mine = jnp.stack(rims(sel[: 2 * RADIUS], sel[nx - 2 * RADIUS :]))
        return mine, swap_core(mine)

    recorded = recorded[0]
    est = window(estimate, chip)
    est_rims = estimate_rims(est)

    kern = psf_taps[0] / jnp.sum(psf_taps[0], axis=1, keepdims=True)
    kerns = [kern] + [to_chip(kern, r) for r in range(1, chips)]

    own = window(recorded, chip)
    record = [(own, *rims(own[:RADIUS], own[nx - RADIUS :]))]
    for r in range(1, chips):
        sent = window(recorded, (chip + r) % chips)
        edges = to_chip(jnp.concatenate([sent[:RADIUS], sent[nx - RADIUS :]]), r)
        middle = to_chip(sent[RADIUS : nx - RADIUS], r)
        first, last = edges[:RADIUS], edges[RADIUS:]
        record.append((jnp.concatenate([first, middle, last]), *rims(first, last)))

    ops = [operators(k, nz) for k in kerns]
    flat = lambda a: a.reshape(-1, a.shape[-1])

    for iteration in range(ITERS):
        if iteration:
            est_rims = estimate_rims(est)
        total = None
        owns = [own_blur_y(flat(est), op[:2]) for op in ops]
        for rec, op, done in zip(record, ops, owns):
            blurred = forward(core_arr, *est_rims, done, op, nz)
            total = adjoint(blurred, flat(rec[1]), flat(rec[0]), flat(rec[2]), op, total, nz)
        if iteration < ITERS - 1:
            total = (total + swap_core(total)).reshape(est.shape)
            est = est * jnp.exp(total / views)

    offset = chip * part - start
    total = lax.dynamic_slice_in_dim(total.reshape(est.shape), offset, part, axis=2)
    est = lax.dynamic_slice_in_dim(est, offset, part, axis=2)
    pick = lambda a, c: lax.dynamic_slice_in_dim(a, c * half, half, axis=1)
    total = pick(total, core) + swap_core(pick(total, 1 - core))
    est = pick(est, core) * jnp.exp(total / views)
    parts = jnp.stack([est] + [to_chip(est, r) for r in range(1, chips)])
    others = swap_core(parts)
    joined = jnp.where(
        core == 0, jnp.concatenate([parts, others], 2), jnp.concatenate([others, parts], 2)
    )
    out = jnp.zeros((nx, nz, ny), F32)
    for r in range(chips):
        at = ((chip - r) % chips) * part
        out = lax.dynamic_update_slice_in_dim(out, joined[r], at, axis=2)
    return out


def solution(mesh):
    in_specs = (P("view", "tile", "slab", None), P("view", None, None), P("tile", "slab", None))
    out_specs = P("tile", "slab", None)
    return jax.shard_map(local, mesh=mesh, in_specs=in_specs, out_specs=out_specs, check_vma=False)
```

```python
import functools
from typing import NamedTuple

import jax
import jax.numpy as jnp
from jax import lax
from jax.experimental import pallas as pl
from jax.experimental.pallas import tpu as pltpu
from jax.sharding import PartitionSpec as P


RADIUS = 7
ITERS = 2
TAPS = 2 * RADIUS + 1
LANES = 128
ROWS = 256
BF = jnp.bfloat16
F32 = jnp.float32
VMEM = pl.BlockSpec(memory_space=pltpu.VMEM)
SMEM = pl.BlockSpec(memory_space=pltpu.SMEM)
ANY = pl.BlockSpec(memory_space=pl.ANY)
PARAMS = pltpu.CompilerParams(vmem_limit_bytes=20 * 1024 * 1024)


def halves(value):
    high = value.astype(BF)
    return high, (value - high.astype(F32)).astype(BF)


def dot(a, b):
    return jnp.dot(a, b, preferred_element_type=F32)


def dot3(a, b):
    return dot(a[0], b[0]) + (dot(a[1], b[0]) + dot(a[0], b[1]))


class Split(NamedTuple):
    chips: int
    cores: int
    part: int
    width: int
    ny: int
    half: int

    def start(self, chip):
        place = jnp.clip(chip * self.part - LANES, 0, self.ny - self.width)
        return pl.multiple_of(place, LANES)

    def here(self):
        place = lax.axis_index("view")
        return place // self.cores, lax.rem(place, self.cores)

    def inner(self):
        chip, _ = self.here()
        return pl.multiple_of(chip * self.part - self.start(chip), LANES)

    def rows(self, core):
        return pl.ds(pl.multiple_of(core * self.half, self.half), self.half)


def cut_kernel(split, moves, ahead, *refs):
    source, outs, sem = refs[0], refs[1:-1], refs[-1]
    chip, core = split.here()
    lanes = pl.ds(split.start(lax.rem(chip + ahead, split.chips)), split.width)
    copies = []
    for out, (x0, at, n, by_core) in moves:
        z = split.rows(core) if by_core else slice(None)
        copies.append(
            pltpu.make_async_copy(
                source.at[x0 : x0 + n, z, lanes], outs[out].at[at : at + n], sem.at[len(copies)]
            )
        )
        copies[-1].start()
    for copy in copies:
        copy.wait()


def cut(source, split, ahead, outs):
    moves, shapes = [], []
    for index, ranges in enumerate(outs):
        at = 0
        for x0, n, by_core in ranges:
            moves.append((index, (x0, at, n, by_core)))
            at += n
        nz = split.half if ranges[0][2] else source.shape[1]
        shapes.append(jax.ShapeDtypeStruct((at, nz, split.width), F32))
    return pl.pallas_call(
        functools.partial(cut_kernel, split, tuple(moves), ahead),
        out_shape=tuple(shapes),
        in_specs=[ANY],
        out_specs=(VMEM,) * len(shapes),
        scratch_shapes=[pltpu.SemaphoreType.DMA((len(moves),))],
        compiler_params=PARAMS,
        name="cut",
    )(source)


def update_kernel(split, views, mine, sibling, est, out, first, last):
    _, core = split.here()
    out[...] = est[...] * jnp.exp((mine[...] + sibling[...]) / views)
    rim = first.shape[0]
    first[...] = out[:rim, split.rows(core), :]
    last[...] = out[out.shape[0] - rim :, split.rows(core), :]


def update(split, views, mine, sibling, est):
    rim = jax.ShapeDtypeStruct((2 * RADIUS, split.half, split.width), F32)
    return pl.pallas_call(
        functools.partial(update_kernel, split, views),
        out_shape=(jax.ShapeDtypeStruct(est.shape, F32), rim, rim),
        in_specs=[VMEM] * 3,
        out_specs=(VMEM,) * 3,
        compiler_params=PARAMS,
        name="update",
    )(mine, sibling, est)


def finish_kernel(split, views, mine, sibling, est, out):
    _, core = split.here()
    old = est[:, split.rows(core), pl.ds(split.inner(), split.part)]
    out[...] = old * jnp.exp((mine[...] + sibling[...]) / views)


def finish(split, views, mine, sibling, est):
    return pl.pallas_call(
        functools.partial(finish_kernel, split, views),
        out_shape=jax.ShapeDtypeStruct(mine.shape, F32),
        in_specs=[VMEM] * 3,
        out_specs=VMEM,
        compiler_params=PARAMS,
        name="finish",
    )(mine, sibling, est)


def operators_kernel(nz, kern, th, tl, wh, wl):
    planes = ROWS // nz
    band = LANES + 3 * 8
    first = LANES - 8
    i = lax.broadcasted_iota(jnp.int32, (band, LANES), 0) + first
    o = lax.broadcasted_iota(jnp.int32, (band, LANES), 1)
    shift_y = i - o - (LANES - RADIUS)
    row = lax.broadcasted_iota(jnp.int32, (nz, 2 * ROWS), 0)
    col = lax.broadcasted_iota(jnp.int32, (nz, 2 * ROWS), 1)
    shift_x = col // nz
    shift_z = col % nz - row + RADIUS
    th[...] = jnp.zeros_like(th)
    tl[...] = jnp.zeros_like(tl)
    for mirrored in range(2):
        ty = jnp.zeros((band, LANES), F32)
        kx = jnp.zeros((nz, 2 * ROWS), F32)
        kz = jnp.zeros((nz, 2 * ROWS), F32)
        for k in range(TAPS):
            tap = TAPS - 1 - k if mirrored else k
            kx = jnp.where(shift_x == k, kern[0, tap], kx)
            kz = jnp.where(shift_z == k, kern[1, tap], kz)
            ty = jnp.where(shift_y == k, kern[2, tap], ty)
        high, low = halves(ty)
        for c0 in range(0, ROWS, LANES):
            rows = slice(first + c0, first + c0 + band)
            th[mirrored, rows, c0 : c0 + LANES] = high
            tl[mirrored, rows, c0 : c0 + LANES] = low
        strip = kx * kz
        for p in range(planes):
            moved = pltpu.roll(strip, p * nz, 1) if p else strip
            rows = slice(p * nz, (p + 1) * nz)
            wh[mirrored, rows, :], wl[mirrored, rows, :] = halves(moved)


def operators(kern, nz):
    t = jax.ShapeDtypeStruct((2, 2 * ROWS, ROWS), BF)
    w = jax.ShapeDtypeStruct((2, ROWS, 2 * ROWS), BF)
    return pl.pallas_call(
        functools.partial(operators_kernel, nz),
        out_shape=(t, t, w, w),
        in_specs=[SMEM],
        out_specs=(VMEM,) * 4,
        compiler_params=PARAMS,
        name="operators",
    )(kern)


def blur_y(x, th, tl, store):
    width = x.shape[1]
    xh, xl = halves(x)
    for o0 in range(0, width, ROWS):
        size = min(ROWS, width - o0)
        k0, k1 = max(0, o0 - LANES), min(width, o0 + size + LANES)
        t0 = k0 - (o0 - LANES)
        rows = slice(t0, t0 + k1 - k0)
        t = (th[rows, :size], tl[rows, :size])
        store(o0, size, dot3((xh[:, k0:k1], xl[:, k0:k1]), t))


def blur_xz(dh, dl, wh, wl, nz, planes_out, store):
    width = dh.shape[1]
    step = ROWS // nz
    for p0 in range(0, planes_out, step):
        planes = min(step, planes_out - p0)
        m = planes * nz
        k = min(2 * ROWS, (planes_out + 2 * RADIUS - p0) * nz)
        for o0 in range(0, width, ROWS):
            size = min(ROWS, width - o0)
            d = (
                dh[p0 * nz : p0 * nz + k, o0 : o0 + size],
                dl[p0 * nz : p0 * nz + k, o0 : o0 + size],
            )
            store(p0 * nz, m, o0, size, dot3((wh[:m, :k], wl[:m, :k]), d))


def to_halves(dh, dl, r0, n):
    def store(o0, size, value):
        h, l = halves(value)
        dh[r0 : r0 + n, o0 : o0 + size] = h
        dl[r0 : r0 + n, o0 : o0 + size] = l

    return store


def chunks(rows, step=128):
    return [(r, min(step, rows - r)) for r in range(0, rows, step)]


def own_kernel(est, th, tl, dh, dl):
    for r0, n in chunks(est.shape[0]):
        blur_y(est[r0 : r0 + n, :], th.at[0], tl.at[0], to_halves(dh, dl, r0, n))


def own_blur_y(est, ops):
    out = jax.ShapeDtypeStruct(est.shape, BF)
    return pl.pallas_call(
        own_kernel,
        out_shape=(out, out),
        in_specs=[VMEM] * 3,
        out_specs=(VMEM, VMEM),
        compiler_params=PARAMS,
        name="own_blur_y",
    )(est, ops[0], ops[1])


def forward_kernel(nz, split, m0, s0, m1, s1, oh, ol, th, tl, wh, wl, blurred, rims, dh, dl):
    width = oh.shape[1]
    rim = m0.shape[0]
    own = oh.shape[0]
    _, core = split.here()
    for side, (mine, sibling) in enumerate(((m0, s0), (m1, s1))):
        rims[side, :, split.rows(core), :] = mine[...]
        rims[side, :, split.rows(1 - core), :] = sibling[...]
    for side in range(2):
        base = 0 if side == 0 else rim * nz + own
        flat = rims[side].reshape(rim * nz, width)
        for r0, n in chunks(rim * nz, 112):
            blur_y(flat[r0 : r0 + n, :], th.at[0], tl.at[0], to_halves(dh, dl, base + r0, n))
    dh[rim * nz : rim * nz + own, :] = oh[...]
    dl[rim * nz : rim * nz + own, :] = ol[...]

    def store(r0, m, o0, size, value):
        blurred[r0 : r0 + m, o0 : o0 + size] = value

    blur_xz(dh, dl, wh.at[0], wl.at[0], nz, blurred.shape[0] // nz, store)


def forward(split, rims, own, ops, nz):
    rim = rims[0].shape[0]
    rows, width = own[0].shape
    total = rows + 2 * rim * nz
    return pl.pallas_call(
        functools.partial(forward_kernel, nz, split),
        out_shape=jax.ShapeDtypeStruct((total - 2 * RADIUS * nz, width), F32),
        in_specs=[VMEM] * 10,
        out_specs=VMEM,
        scratch_shapes=[
            pltpu.VMEM((2, rim, nz, width), F32),
            pltpu.VMEM((total, width), BF),
            pltpu.VMEM((total, width), BF),
        ],
        compiler_params=PARAMS,
        name="forward",
    )(*rims, own[0], own[1], *ops)


def adjoint_kernel(nz, pieces, inputs, has_added, last, *refs):
    blurred, refs = refs[0], refs[1:]
    record, refs = refs[:inputs], refs[inputs:]
    th, tl, wh, wl = refs[:4]
    refs = refs[4:]
    if has_added:
        added, refs = refs[0], refs[1:]
    if last is not None:
        keep, send, refs = refs[0], refs[1], refs[2:]
    out, dh, dl = refs
    base = 0
    for which, start, count in pieces:
        for r0, n in chunks(count):
            rows = slice(base + r0, base + r0 + n)
            q = record[which][start + r0 : start + r0 + n, :] / blurred[rows, :]
            blur_y(q, th.at[1], tl.at[1], to_halves(dh, dl, base + r0, n))
        base += count

    def store(r0, m, o0, size, value):
        log = jnp.log(value)
        planes = slice(r0 // nz, (r0 + m) // nz)
        log = log.reshape(m // nz, nz, size)
        if has_added:
            log = log + added[planes, :, o0 : o0 + size]
        out[planes, :, o0 : o0 + size] = log

    blur_xz(dh, dl, wh.at[1], wl.at[1], nz, out.shape[0], store)
    if last is not None:
        _, core = last.here()
        lanes = pl.ds(last.inner(), last.part)
        keep[...] = out[:, last.rows(core), lanes]
        send[...] = out[:, last.rows(1 - core), lanes]


def adjoint(blurred, record, pieces, ops, added, nz, last=None):
    rows, width = blurred.shape
    args = [blurred, *record, *ops] + ([] if added is None else [added])
    full = (rows // nz - 2 * RADIUS, nz, width)
    shape = jax.ShapeDtypeStruct(full, F32)
    scratch = [pltpu.VMEM(blurred.shape, BF), pltpu.VMEM(blurred.shape, BF)]
    if last is not None:
        shape = (jax.ShapeDtypeStruct((full[0], last.half, last.part), F32),) * 2
        scratch = [pltpu.VMEM(full, F32)] + scratch
    return pl.pallas_call(
        functools.partial(adjoint_kernel, nz, pieces, len(record), added is not None, last),
        out_shape=shape,
        in_specs=[VMEM] * len(args),
        out_specs=VMEM if last is None else (VMEM, VMEM),
        scratch_shapes=scratch,
        compiler_params=PARAMS,
        name="adjoint",
    )(*args)


def join_kernel(split, *refs):
    mine, out = refs[:-1], refs[-1]
    chip, core = split.here()
    for r in range(split.chips):
        owner = lax.rem(chip + split.chips - r, split.chips)
        lanes = pl.ds(pl.multiple_of(owner * split.part, LANES), split.part)
        out[:, split.rows(core), lanes] = mine[r][...]
        out[:, split.rows(1 - core), lanes] = mine[split.chips + r][...]


def join(split, mine, others, nz):
    return pl.pallas_call(
        functools.partial(join_kernel, split),
        out_shape=jax.ShapeDtypeStruct((mine[0].shape[0], nz, split.ny), F32),
        in_specs=[VMEM] * (2 * len(mine)),
        out_specs=VMEM,
        compiler_params=PARAMS,
        name="join",
    )(*mine, *others)


def steps(recorded, psf_taps, estimate):
    views = lax.axis_size("view")
    tiles = lax.axis_size("tile")
    nx, nz, ny = estimate.shape
    cores = 2
    chips = views // cores
    part = ny // chips
    width = min(ny, part + (LANES if chips <= 2 else 2 * LANES))
    split = Split(chips, cores, part, width, ny, nz // cores)
    assert 2 * RADIUS * ITERS <= LANES and nx >= 2 * RADIUS
    flat = lambda a: a.reshape(-1, a.shape[-1])

    def swap_core(values):
        pairs = [(v, v ^ 1) for v in range(views)]
        return lax.ppermute(values, "view", pairs)

    def to_chip(values, r):
        pairs = [(v, (v + r * cores) % views) for v in range(views)]
        return lax.ppermute(values, "view", pairs)

    up = [(t, t + 1) for t in range(tiles - 1)]
    down = [(t + 1, t) for t in range(tiles - 1)]

    def rims(first, last):
        before = lax.ppermute(last, "tile", up)
        after = lax.ppermute(first, "tile", down)
        return before, after

    def estimate_rims(first, last):
        before, after = rims(first, last)
        return (before, swap_core(before), after, swap_core(after))

    recorded = recorded[0]
    kern = psf_taps[0] / jnp.sum(psf_taps[0], axis=1, keepdims=True)
    kerns = [kern] + [to_chip(kern, r) for r in range(1, chips)]

    rim, body = RADIUS * nz, (nx - 2 * RADIUS) * nz
    edges, middles = [None], [None]
    for r in range(1, chips):
        (both,) = cut(
            recorded, split, r, [((0, RADIUS, False), (nx - RADIUS, RADIUS, False))]
        )
        edges.append(to_chip(both, r))
        (inside,) = cut(recorded, split, r, [((RADIUS, nx - 2 * RADIUS, False),)])
        middles.append(to_chip(inside, r))

    est, first, last = cut(
        estimate,
        split,
        0,
        [
            ((0, nx, False),),
            ((0, 2 * RADIUS, True),),
            ((nx - 2 * RADIUS, 2 * RADIUS, True),),
        ],
    )
    est_rims = estimate_rims(first, last)

    own, first, last = cut(
        recorded,
        split,
        0,
        [((0, nx, False),), ((0, RADIUS, False),), ((nx - RADIUS, RADIUS, False),)],
    )
    before, after = rims(first, last)
    record = [tuple(flat(a) for a in (before, own, after))]
    pieces = [((0, 0, rim), (1, 0, 2 * rim + body), (2, 0, rim))]
    for r in range(1, chips):
        before, after = rims(edges[r][:RADIUS], edges[r][RADIUS:])
        record.append(tuple(flat(a) for a in (before, edges[r], middles[r], after)))
        pieces.append(((0, 0, rim), (1, 0, rim), (2, 0, body), (1, rim, rim), (3, 0, rim)))

    ops = []
    for k in kerns:
        ops.append(operators(k, nz))

    for iteration in range(ITERS):
        final = iteration == ITERS - 1
        total = None
        owns = []
        for r in range(chips):
            owns.append(own_blur_y(flat(est), ops[r][:2]))
        for r in range(chips):
            blurred = forward(split, est_rims, owns[r], ops[r], nz)
            end = split if final and r == chips - 1 else None
            total = adjoint(blurred, record[r], pieces[r], ops[r], total, nz, end)
        if not final:
            sibling = swap_core(total)
            est, first, last = update(split, views, total, sibling, est)
            est_rims = estimate_rims(first, last)

    keep, send = total
    est = finish(split, views, keep, swap_core(send), est)
    parts = [est] + [to_chip(est, r) for r in range(1, chips)]
    others = [swap_core(p) for p in parts]
    return join(split, parts, others, nz)


def solution(mesh):
    in_specs = (P("view", "tile", "slab", None), P("view", None, None), P("tile", "slab", None))
    out_specs = P("tile", "slab", None)
    return jax.shard_map(steps, mesh=mesh, in_specs=in_specs, out_specs=out_specs, check_vma=False)
```

```python
import functools
from typing import NamedTuple

import jax
import jax.numpy as jnp
from jax import lax
from jax.experimental import pallas as pl
from jax.experimental.pallas import tpu as pltpu
from jax.sharding import PartitionSpec as P


RADIUS = 7
ITERS = 2
TAPS = 2 * RADIUS + 1
LANES = 128
ROWS = 256
BF = jnp.bfloat16
F32 = jnp.float32
VMEM = pl.BlockSpec(memory_space=pltpu.VMEM)
SMEM = pl.BlockSpec(memory_space=pltpu.SMEM)
ANY = pl.BlockSpec(memory_space=pltpu.HBM)
PARAMS = pltpu.CompilerParams(vmem_limit_bytes=20 * 1024 * 1024)


def halves(value):
    high = value.astype(BF)
    return high, (value - high.astype(F32)).astype(BF)


def dot(a, b):
    return jnp.dot(a, b, preferred_element_type=F32)


class Split(NamedTuple):
    chips: int
    cores: int
    part: int
    width: int
    ny: int
    half: int

    def start(self, chip):
        place = jnp.clip(chip * self.part - LANES, 0, self.ny - self.width)
        return pl.multiple_of(place, LANES)

    def here(self):
        place = lax.axis_index("view")
        return place // self.cores, lax.rem(place, self.cores)

    def inner(self):
        chip, _ = self.here()
        return pl.multiple_of(chip * self.part - self.start(chip), LANES)

    def odd(self):
        return lax.rem(lax.axis_index("tile"), 2)

    def rows(self, core):
        return pl.ds(pl.multiple_of(core * self.half, self.half), self.half)


def cut_kernel(split, moves, ahead, *refs):
    source, outs, sem = refs[0], refs[1:-1], refs[-1]
    chip, core = split.here()
    lanes = pl.ds(split.start(lax.rem(chip + ahead, split.chips)), split.width)
    copies = []
    for out, at, even, odd, n, whose in moves:
        x0 = even if even == odd else jnp.where(split.odd() == 1, odd, even)
        z = slice(None) if whose is None else split.rows(core if whose == 0 else 1 - core)
        copies.append(
            pltpu.make_async_copy(
                source.at[pl.ds(x0, n), z, lanes],
                outs[out].at[pl.ds(at, n)],
                sem.at[len(copies)],
            )
        )
        copies[-1].start()
    for copy in copies:
        copy.wait()


def cut(source, split, ahead, outs):
    moves, shapes = [], []
    for index, ranges in enumerate(outs):
        at = 0
        for even, odd, n, whose in ranges:
            moves.append((index, at, even, odd, n, whose))
            at += n
        nz = source.shape[1] if ranges[0][3] is None else split.half
        shapes.append(jax.ShapeDtypeStruct((at, nz, split.width), F32))
    return pl.pallas_call(
        functools.partial(cut_kernel, split, tuple(moves), ahead),
        out_shape=tuple(shapes),
        in_specs=[ANY],
        out_specs=(VMEM,) * len(shapes),
        scratch_shapes=[pltpu.SemaphoreType.DMA((len(moves),))],
        compiler_params=PARAMS,
        name="cut",
    )(source)


def update_kernel(split, views, mine, sibling, est, out, pair_a, pair_b):
    out[...] = est[...] * jnp.exp((mine[...] + sibling[...]) / views)
    rim = pair_a.shape[0]
    top = out.shape[0] - rim
    odd = split.odd()
    pair_a[...] = out[pl.ds((1 - odd) * top, rim)]
    pair_b[...] = out[pl.ds(odd * top, rim)]


def update(split, views, mine, sibling, est):
    rim = jax.ShapeDtypeStruct((2 * RADIUS, split.half, split.width), F32)
    return pl.pallas_call(
        functools.partial(update_kernel, split, views),
        out_shape=(jax.ShapeDtypeStruct(est.shape, F32), rim, rim),
        in_specs=[VMEM] * 3,
        out_specs=(VMEM,) * 3,
        compiler_params=PARAMS,
        name="update",
    )(mine, sibling, est)


def finish_kernel(split, views, mine, sibling, est, out):
    old = est[:, :, pl.ds(split.inner(), split.part)]
    out[...] = old * jnp.exp((mine[...] + sibling[...]) / views)


def finish(split, views, mine, sibling, est):
    return pl.pallas_call(
        functools.partial(finish_kernel, split, views),
        out_shape=jax.ShapeDtypeStruct(mine.shape, F32),
        in_specs=[VMEM] * 3,
        out_specs=VMEM,
        compiler_params=PARAMS,
        name="finish",
    )(mine, sibling, est)


def operators_kernel(nz, taps, t, w, th, tl):
    planes = ROWS // nz
    band = LANES + 3 * 8
    first = LANES - 8
    i = lax.broadcasted_iota(jnp.int32, (band, LANES), 0) + first
    o = lax.broadcasted_iota(jnp.int32, (band, LANES), 1)
    shift_y = i - o - (LANES - RADIUS)
    row = lax.broadcasted_iota(jnp.int32, (nz, 2 * ROWS), 0)
    col = lax.broadcasted_iota(jnp.int32, (nz, 2 * ROWS), 1)
    shift_x = col // nz
    shift_z = col % nz - row + RADIUS
    sums = []
    for d in range(3):
        value = taps[d, 0]
        for k in range(1, TAPS):
            value = value + taps[d, k]
        sums.append(value)
    th[...] = jnp.zeros_like(th)
    tl[...] = jnp.zeros_like(tl)
    half = LANES // 2
    for mirrored in range(2):
        ty = jnp.zeros((band, LANES), F32)
        kx = jnp.zeros((nz, 2 * ROWS), F32)
        kz = jnp.zeros((nz, 2 * ROWS), F32)
        for k in range(TAPS):
            tap = TAPS - 1 - k if mirrored else k
            kx = jnp.where(shift_x == k, taps[0, tap], kx)
            kz = jnp.where(shift_z == k, taps[1, tap], kz)
            ty = jnp.where(shift_y == k, taps[2, tap], ty)
        kx = kx / sums[0]
        kz = kz / sums[1]
        ty = ty / sums[2]
        high, low = halves(ty)
        for c0 in range(0, ROWS, LANES):
            rows = slice(first + c0, first + c0 + band)
            th[rows, c0 : c0 + LANES] = high
            tl[rows, c0 : c0 + LANES] = low
        inside = slice(LANES, LANES + ROWS)
        right, left = slice(LANES + ROWS, LANES + ROWS + half), slice(half, LANES)
        t[mirrored, 0] = th[inside, :]
        t[mirrored, 1] = tl[inside, :]
        for at in (0, LANES):
            t[mirrored, 2, at : at + half] = th[right, :]
            t[mirrored, 2, at + half : at + LANES] = th[left, :]
        t[mirrored, 3, :half] = tl[right, :]
        t[mirrored, 3, half:LANES] = tl[left, :]
        t[mirrored, 3, LANES:] = jnp.zeros((ROWS - LANES, ROWS), BF)
        t[mirrored, 4, :, :LANES] = th[:ROWS, :LANES]
        t[mirrored, 4, :, LANES:] = tl[:ROWS, :LANES]
        strip = kx * kz
        for p in range(planes):
            moved = pltpu.roll(strip, p * nz, 1) if p else strip
            rows = slice(p * nz, (p + 1) * nz)
            w[mirrored, 0, rows, :], w[mirrored, 1, rows, :] = halves(moved)


def operators(taps, nz):
    return pl.pallas_call(
        functools.partial(operators_kernel, nz),
        out_shape=(
            jax.ShapeDtypeStruct((2, 5, ROWS, ROWS), BF),
            jax.ShapeDtypeStruct((2, 2, ROWS, 2 * ROWS), BF),
        ),
        in_specs=[SMEM],
        out_specs=(VMEM,) * 2,
        scratch_shapes=[pltpu.VMEM((2 * ROWS, ROWS), BF)] * 2,
        compiler_params=PARAMS,
        name="operators",
    )(taps)


def blur_y(x, t, store):
    n, width = x.shape
    xh, xl = halves(x)
    right = lax.broadcasted_iota(jnp.int32, (n, LANES), 1) < LANES // 2
    for o0 in range(0, width, ROWS):
        size = min(ROWS, width - o0)
        if size == ROWS:
            end = o0 + ROWS
            at = slice(o0, end)
            out = dot(xh[:, at], t[0]) + (dot(xl[:, at], t[0]) + dot(xh[:, at], t[1]))
            none = jnp.zeros((n, LANES), F32)
            corner = jnp.where(
                right,
                x[:, end : end + LANES] if end < width else none,
                x[:, o0 - LANES : o0] if o0 else none,
            )
            ch, cl = halves(corner)
            out = out + (dot(jnp.concatenate([ch, cl], 1), t[2]) + dot(ch, t[3, :LANES]))
        else:
            at = slice(o0 - LANES, o0 + LANES)
            both = dot(xh[:, at], t[4])
            out = both[:, :LANES] + (both[:, LANES:] + dot(xl[:, at], t[4, :, :LANES]))
        store(o0, size, out)


def blur_xz(dh, dl, w, nz, planes_out, store):
    width = dh.shape[1]
    step = ROWS // nz
    for p0 in range(0, planes_out, step):
        planes = min(step, planes_out - p0)
        m = planes * nz
        k = min(2 * ROWS, (planes_out + 2 * RADIUS - p0) * nz)
        rows = slice(p0 * nz, p0 * nz + k)
        wh, wl = w[0, :m, :k], w[1, :m, :k]
        for o0 in range(0, width, ROWS):
            size = min(ROWS, width - o0)
            at = slice(o0, o0 + size)
            if size == ROWS:
                out = dot(wh, dh[rows, at]) + (dot(wl, dh[rows, at]) + dot(wh, dl[rows, at]))
            else:
                both = dot(wh, jnp.concatenate([dh[rows, at], dl[rows, at]], 1))
                out = both[:, :size] + (both[:, size:] + dot(wl, dh[rows, at]))
            store(p0 * nz, m, o0, size, out)


def to_halves(dh, dl, rows):
    def store(o0, size, value):
        h, l = halves(value)
        dh[rows, o0 : o0 + size] = h
        dl[rows, o0 : o0 + size] = l

    return store


def chunks(rows, step=128):
    return [(r, min(step, rows - r)) for r in range(0, rows, step)]


def own_kernel(split, mine, sibling, t, dh, dl, est):
    _, core = split.here()
    est[:, split.rows(core), :] = mine[...]
    est[:, split.rows(1 - core), :] = sibling[...]
    planes, nz, width = est.shape
    step = LANES // nz
    for p in range(0, planes, step):
        n = min(step, planes - p)
        rows = slice(p * nz, (p + n) * nz)
        x = est[p : p + n].reshape(n * nz, width)
        blur_y(x, t.at[0], to_halves(dh, dl, rows))


def own_blur_y(split, mine, sibling, t):
    planes, half, width = mine.shape
    nz = half * split.cores
    out = jax.ShapeDtypeStruct((planes * nz, width), BF)
    return pl.pallas_call(
        functools.partial(own_kernel, split),
        out_shape=(out, out),
        in_specs=[VMEM] * 3,
        out_specs=(VMEM, VMEM),
        scratch_shapes=[pltpu.VMEM((planes, nz, width), F32)],
        compiler_params=PARAMS,
        name="own_blur_y",
    )(mine, sibling, t)


def forward_kernel(nz, split, ma, sa, mb, sb, oh, ol, t, w, blurred, rims, dh, dl):
    width = oh.shape[1]
    rim = ma.shape[0]
    own = oh.shape[0]
    _, core = split.here()
    odd = split.odd()
    for side, mine, sibling in ((1 - odd, ma, sa), (odd, mb, sb)):
        rims[side, :, split.rows(core), :] = mine[...]
        rims[side, :, split.rows(1 - core), :] = sibling[...]
    for side in range(2):
        base = 0 if side == 0 else rim * nz + own
        flat = rims[side].reshape(rim * nz, width)
        for r0, n in chunks(rim * nz, 112):
            rows = slice(base + r0, base + r0 + n)
            blur_y(flat[r0 : r0 + n, :], t.at[0], to_halves(dh, dl, rows))
    dh[rim * nz : rim * nz + own, :] = oh[...]
    dl[rim * nz : rim * nz + own, :] = ol[...]

    def store(r0, m, o0, size, value):
        blurred[r0 : r0 + m, o0 : o0 + size] = value

    blur_xz(dh, dl, w.at[0], nz, blurred.shape[0] // nz, store)


def forward(split, rims, own, ops, nz):
    rim = rims[0].shape[0]
    rows, width = own[0].shape
    total = rows + 2 * rim * nz
    return pl.pallas_call(
        functools.partial(forward_kernel, nz, split),
        out_shape=jax.ShapeDtypeStruct((total - 2 * RADIUS * nz, width), F32),
        in_specs=[VMEM] * 8,
        out_specs=VMEM,
        scratch_shapes=[
            pltpu.VMEM((2, rim, nz, width), F32),
            pltpu.VMEM((total, width), BF),
            pltpu.VMEM((total, width), BF),
        ],
        compiler_params=PARAMS,
        name="forward",
    )(*rims, own[0], own[1], *ops)


def adjoint_kernel(nz, split, pieces, inputs, has_added, ends, *refs):
    blurred, refs = refs[0], refs[1:]
    record, refs = refs[:inputs], refs[inputs:]
    t, w, refs = refs[0], refs[1], refs[2:]
    if has_added:
        added, refs = refs[0], refs[1:]
    if ends is not None:
        keep, send, refs = refs[0], refs[1], refs[2:]
    out, dh, dl = refs
    odd = split.odd()
    for which, start, count, even_base, odd_base in pieces:
        if even_base == odd_base:
            base = even_base
        else:
            base = pl.multiple_of(jnp.where(odd == 1, odd_base, even_base), nz)
        for r0, n in chunks(count):
            rows = pl.ds(base + r0, n)
            q = record[which][start + r0 : start + r0 + n, :] / blurred[rows, :]
            blur_y(q, t.at[1], to_halves(dh, dl, rows))

    def store(r0, m, o0, size, value):
        log = jnp.log(value)
        planes = slice(r0 // nz, (r0 + m) // nz)
        log = log.reshape(m // nz, nz, size)
        if has_added:
            log = log + added[planes, :, o0 : o0 + size]
        out[planes, :, o0 : o0 + size] = log

    blur_xz(dh, dl, w.at[1], nz, out.shape[0], store)
    if ends is not None:
        _, core = split.here()
        lanes = slice(None) if ends == split.width else pl.ds(split.inner(), ends)
        keep[...] = out[:, split.rows(core), lanes]
        send[...] = out[:, split.rows(1 - core), lanes]


def adjoint(split, blurred, record, pieces, ops, added, nz, ends=None):
    rows, width = blurred.shape
    args = [blurred, *record, *ops] + ([] if added is None else [added])
    full = (rows // nz - 2 * RADIUS, nz, width)
    shape = jax.ShapeDtypeStruct(full, F32)
    scratch = [pltpu.VMEM(blurred.shape, BF), pltpu.VMEM(blurred.shape, BF)]
    if ends is not None:
        shape = (jax.ShapeDtypeStruct((full[0], split.half, ends), F32),) * 2
        scratch = [pltpu.VMEM(full, F32)] + scratch
    kernel = functools.partial(
        adjoint_kernel, nz, split, pieces, len(record), added is not None, ends
    )
    return pl.pallas_call(
        kernel,
        out_shape=shape,
        in_specs=[VMEM] * len(args),
        out_specs=VMEM if ends is None else (VMEM, VMEM),
        scratch_shapes=scratch,
        compiler_params=PARAMS,
        name="adjoint",
    )(*args)


def join_kernel(split, *refs):
    mine, out = refs[:-1], refs[-1]
    chip, core = split.here()
    for r in range(split.chips):
        owner = lax.rem(chip + split.chips - r, split.chips)
        lanes = pl.ds(pl.multiple_of(owner * split.part, LANES), split.part)
        out[:, split.rows(core), lanes] = mine[r][...]
        out[:, split.rows(1 - core), lanes] = mine[split.chips + r][...]


def join(split, mine, others, nz):
    return pl.pallas_call(
        functools.partial(join_kernel, split),
        out_shape=jax.ShapeDtypeStruct((mine[0].shape[0], nz, split.ny), F32),
        in_specs=[VMEM] * (2 * len(mine)),
        out_specs=VMEM,
        compiler_params=PARAMS,
        name="join",
    )(*mine, *others)


def steps(recorded, psf_taps, estimate):
    views = lax.axis_size("view")
    tiles = lax.axis_size("tile")
    nx, nz, ny = estimate.shape
    cores = 2
    chips = views // cores
    part = ny // chips
    width = min(ny, part + (LANES if chips <= 2 else 2 * LANES))
    split = Split(chips, cores, part, width, ny, nz // cores)
    assert 2 * RADIUS * ITERS <= LANES and nx >= 2 * RADIUS
    flat = lambda a: a.reshape(-1, a.shape[-1])

    def swap_core(values):
        pairs = [(v, v ^ 1) for v in range(views)]
        return lax.ppermute(values, "view", pairs)

    def to_chip(values, r):
        pairs = [(v, (v + r * cores) % views) for v in range(views)]
        return lax.ppermute(values, "view", pairs)

    next_a = [(t, t ^ 1) for t in range(tiles) if t ^ 1 < tiles]
    next_b = [(t, ((t + 1) ^ 1) - 1) for t in range(1, tiles)]
    next_b = [(t, u) for t, u in next_b if u < tiles]

    def pair_up(a, b):
        b = lax.ppermute(b, "tile", next_b)
        a = lax.ppermute(a, "tile", next_a)
        return a, b

    def estimate_rims(a, b):
        a, b = pair_up(a, b)
        return a, swap_core(a), b, swap_core(b)

    recorded = recorded[0]
    taps = [psf_taps[0]] + [to_chip(psf_taps[0], r) for r in range(1, chips)]

    def to_a(n, whose=None):
        return (nx - n, 0, n, whose)

    def to_b(n, whose=None):
        return (0, nx - n, n, whose)

    rim, body = RADIUS * nz, (nx - 2 * RADIUS) * nz
    end = 2 * rim + body
    edges, middles = [None], [None]
    for r in range(1, chips):
        (both,) = cut(recorded, split, r, [(to_a(RADIUS), to_b(RADIUS))])
        edges.append(to_chip(both, r))
        inside = (RADIUS, RADIUS, nx - 2 * RADIUS, None)
        (inside,) = cut(recorded, split, r, [(inside,)])
        middles.append(to_chip(inside, r))

    est, est_sibling, pair_a, pair_b = cut(
        estimate,
        split,
        0,
        [
            ((0, 0, nx, 0),),
            ((0, 0, nx, 1),),
            (to_a(2 * RADIUS, 0),),
            (to_b(2 * RADIUS, 0),),
        ],
    )
    est_rims = estimate_rims(pair_a, pair_b)

    own, pair_a, pair_b = cut(
        recorded, split, 0, [((0, 0, nx, None),), (to_a(RADIUS),), (to_b(RADIUS),)]
    )
    pair_a, pair_b = pair_up(pair_a, pair_b)
    record = [tuple(flat(a) for a in (pair_a, own, pair_b))]
    outer_a, outer_b = (0, 0, rim, rim + end, 0), (2, 0, rim, 0, rim + end)
    pieces = [((1, 0, end, rim, rim), outer_a, outer_b)]
    for r in range(1, chips):
        pair_a, pair_b = pair_up(edges[r][:RADIUS], edges[r][RADIUS:])
        record.append(tuple(flat(a) for a in (pair_a, edges[r], pair_b, middles[r])))
        inner_a = (1, 0, rim, end, rim)
        inner_b = (1, rim, rim, rim, end)
        pieces.append((inner_a, inner_b, (3, 0, body, 2 * rim, 2 * rim), outer_a, outer_b))

    ops = []
    for k in taps:
        ops.append(operators(k, nz))

    for iteration in range(ITERS):
        final = iteration == ITERS - 1
        total = None
        owns = []
        for r in range(chips):
            owns.append(own_blur_y(split, est, est_sibling, ops[r][0]))
        for r in range(chips):
            blurred = forward(split, est_rims, owns[r], ops[r], nz)
            ends = (part if final else width) if r == chips - 1 else None
            total = adjoint(split, blurred, record[r], pieces[r], ops[r], total, nz, ends)
        keep, send = total
        sibling = swap_core(send)
        if not final:
            est, pair_a, pair_b = update(split, views, keep, sibling, est)
            est_rims = estimate_rims(pair_a, pair_b)
            est_sibling = swap_core(est)

    est = finish(split, views, keep, sibling, est)
    parts = [est] + [to_chip(est, r) for r in range(1, chips)]
    others = [swap_core(p) for p in parts]
    return join(split, parts, others, nz)


def solution(mesh):
    in_specs = (P("view", "tile", "slab", None), P("view", None, None), P("tile", "slab", None))
    out_specs = P("tile", "slab", None)
    return jax.shard_map(steps, mesh=mesh, in_specs=in_specs, out_specs=out_specs, check_vma=False)
```

```python
import functools
from typing import NamedTuple

import jax
import jax.numpy as jnp
from jax import lax
from jax.experimental import pallas as pl
from jax.experimental.pallas import tpu as pltpu
from jax.sharding import PartitionSpec as P


RADIUS = 7
ITERS = 2
TAPS = 2 * RADIUS + 1
LANES = 128
ROWS = 256
BF = jnp.bfloat16
F32 = jnp.float32
VMEM = pl.BlockSpec(memory_space=pltpu.VMEM)
SMEM = pl.BlockSpec(memory_space=pltpu.SMEM)
ANY = pl.BlockSpec(memory_space=pltpu.HBM)
PARAMS = pltpu.CompilerParams(vmem_limit_bytes=20 * 1024 * 1024)


def halves(value):
    high = value.astype(BF)
    return high, (value - high.astype(F32)).astype(BF)


def dot(a, b):
    return jnp.dot(a, b, preferred_element_type=F32)


class Split(NamedTuple):
    chips: int
    cores: int
    part: int
    width: int
    ny: int
    half: int

    def start(self, chip):
        place = jnp.clip(chip * self.part - LANES, 0, self.ny - self.width)
        return pl.multiple_of(place, LANES)

    def here(self):
        place = lax.axis_index("view")
        return place // self.cores, lax.rem(place, self.cores)

    def inner(self):
        chip, _ = self.here()
        return pl.multiple_of(chip * self.part - self.start(chip), LANES)

    def odd(self):
        return lax.rem(lax.axis_index("tile"), 2)

    def side(self, mine):
        _, core = self.here()
        own = 1 - lax.rem(self.odd() + core, 2)
        return own if mine else 1 - own

    def rows(self, core):
        return pl.ds(pl.multiple_of(core * self.half, self.half), self.half)


def cut_kernel(split, sources, moves, *refs):
    outs, sem = refs[sources:-1], refs[-1]
    chip, _ = split.here()
    copies = []
    for source, ahead, out, at, even, odd, n, by_core in moves:
        lanes = pl.ds(split.start(lax.rem(chip + ahead, split.chips)), split.width)
        which = 1 - split.side(True) if by_core else split.odd()
        x0 = even if even == odd else jnp.where(which == 1, odd, even)
        copies.append(
            pltpu.make_async_copy(
                refs[source].at[pl.ds(x0, n), :, lanes],
                outs[out].at[pl.ds(at, n)],
                sem.at[len(copies)],
            )
        )
        copies[-1].start()
    for copy in copies:
        copy.wait()


def cut(sources, split, outs):
    moves, shapes = [], []
    for index, (source, ahead, ranges) in enumerate(outs):
        at = 0
        for even, odd, n, by_core in ranges:
            moves.append((source, ahead, index, at, even, odd, n, by_core))
            at += n
        shapes.append(jax.ShapeDtypeStruct((at, sources[source].shape[1], split.width), F32))
    return pl.pallas_call(
        functools.partial(cut_kernel, split, len(sources), tuple(moves)),
        out_shape=tuple(shapes),
        in_specs=[ANY] * len(sources),
        out_specs=(VMEM,) * len(shapes),
        scratch_shapes=[pltpu.SemaphoreType.DMA((len(moves),))],
        compiler_params=PARAMS,
        name="cut",
    )(*sources)


def update_kernel(split, views, planes, *refs):
    est, out, rim = refs[-3:]
    for c, (p0, p1) in enumerate(planes):
        total = refs[2 * c][...] + refs[2 * c + 1][...]
        out[p0:p1] = est[p0:p1] * jnp.exp(total / views)
    n = rim.shape[0]
    rim[...] = out[pl.ds(split.side(True) * (out.shape[0] - n), n)]


def update(split, views, planes, sums, est):
    return pl.pallas_call(
        functools.partial(update_kernel, split, views, planes),
        out_shape=(
            jax.ShapeDtypeStruct(est.shape, F32),
            jax.ShapeDtypeStruct((2 * RADIUS, *est.shape[1:]), F32),
        ),
        in_specs=[VMEM] * (len(sums) + 1),
        out_specs=(VMEM,) * 2,
        compiler_params=PARAMS,
        name="update",
    )(*sums, est)


def finish_kernel(split, views, planes, mine, sibling, est, out):
    _, core = split.here()
    old = est[planes[0] : planes[1], split.rows(core), pl.ds(split.inner(), split.part)]
    out[...] = old * jnp.exp((mine[...] + sibling[...]) / views)


def finish(split, views, planes, mine, sibling, est):
    return pl.pallas_call(
        functools.partial(finish_kernel, split, views, planes),
        out_shape=jax.ShapeDtypeStruct(mine.shape, F32),
        in_specs=[VMEM] * 3,
        out_specs=VMEM,
        compiler_params=PARAMS,
        name="finish",
    )(mine, sibling, est)


def operators_kernel(nz, taps, t, w, wr, th, tl):
    planes = ROWS // nz
    band = LANES + 3 * 8
    first = LANES - 8
    i = lax.broadcasted_iota(jnp.int32, (band, LANES), 0) + first
    o = lax.broadcasted_iota(jnp.int32, (band, LANES), 1)
    shift_y = i - o - (LANES - RADIUS)
    row = lax.broadcasted_iota(jnp.int32, (nz, 2 * ROWS), 0)
    col = lax.broadcasted_iota(jnp.int32, (nz, 2 * ROWS), 1)
    shift_x = col // nz
    shift_z = col % nz - row + RADIUS
    sums = []
    for d in range(3):
        value = taps[0, d, 0]
        for k in range(1, TAPS):
            value = value + taps[0, d, k]
        sums.append(value)
    th[...] = jnp.zeros_like(th)
    tl[...] = jnp.zeros_like(tl)
    half = LANES // 2
    for mirrored in range(2):
        ty = jnp.zeros((band, LANES), F32)
        kx = jnp.zeros((nz, 2 * ROWS), F32)
        kz = jnp.zeros((nz, 2 * ROWS), F32)
        for k in range(TAPS):
            tap = TAPS - 1 - k if mirrored else k
            kx = jnp.where(shift_x == k, taps[0, 0, tap], kx)
            kz = jnp.where(shift_z == k, taps[0, 1, tap], kz)
            ty = jnp.where(shift_y == k, taps[0, 2, tap], ty)
        kx = kx / sums[0]
        kz = kz / sums[1]
        ty = ty / sums[2]
        high, low = halves(ty)
        for c0 in range(0, ROWS, LANES):
            rows = slice(first + c0, first + c0 + band)
            th[rows, c0 : c0 + LANES] = high
            tl[rows, c0 : c0 + LANES] = low
        inside = slice(LANES, LANES + ROWS)
        right, left = slice(LANES + ROWS, LANES + ROWS + half), slice(half, LANES)
        t[mirrored, 0] = th[inside, :]
        t[mirrored, 1] = tl[inside, :]
        for at in (0, LANES):
            t[mirrored, 2, at : at + half] = th[right, :]
            t[mirrored, 2, at + half : at + LANES] = th[left, :]
        t[mirrored, 3, :half] = tl[right, :]
        t[mirrored, 3, half:LANES] = tl[left, :]
        t[mirrored, 3, LANES:] = jnp.zeros((ROWS - LANES, ROWS), BF)
        t[mirrored, 4, :, :LANES] = th[:ROWS, :LANES]
        t[mirrored, 4, :, LANES:] = tl[:ROWS, :LANES]
        strip = kx * kz
        for p in range(planes):
            moved = pltpu.roll(strip, p * nz, 1) if p else strip
            rows = slice(p * nz, (p + 1) * nz)
            w[mirrored, 0, rows, :], w[mirrored, 1, rows, :] = halves(moved)
            if not mirrored:
                wr[0, 0, rows, :], wr[0, 1, rows, :] = halves(moved[:, :ROWS])
                back = (p - 2 * RADIUS) * nz % (2 * ROWS)
                moved = pltpu.roll(strip, back, 1)[:, :ROWS] if back else strip[:, :ROWS]
                wr[1, 0, rows, :], wr[1, 1, rows, :] = halves(moved)


def operators(taps, nz):
    return pl.pallas_call(
        functools.partial(operators_kernel, nz),
        out_shape=(
            jax.ShapeDtypeStruct((2, 5, ROWS, ROWS), BF),
            jax.ShapeDtypeStruct((2, 2, ROWS, 2 * ROWS), BF),
            jax.ShapeDtypeStruct((2, 2, ROWS, ROWS), BF),
        ),
        in_specs=[SMEM],
        out_specs=(VMEM,) * 3,
        scratch_shapes=[pltpu.VMEM((2 * ROWS, ROWS), BF)] * 2,
        compiler_params=PARAMS,
        name="operators",
    )(taps)


def blur_y(x, t, store):
    n, width = x.shape
    xh, xl = halves(x)
    right = lax.broadcasted_iota(jnp.int32, (n, LANES), 1) < LANES // 2
    for o0 in range(0, width, ROWS):
        size = min(ROWS, width - o0)
        if size == ROWS:
            end = o0 + ROWS
            at = slice(o0, end)
            out = dot(xh[:, at], t[0]) + (dot(xl[:, at], t[0]) + dot(xh[:, at], t[1]))
            none = jnp.zeros((n, LANES), F32)
            corner = jnp.where(
                right,
                x[:, end : end + LANES] if end < width else none,
                x[:, o0 - LANES : o0] if o0 else none,
            )
            ch, cl = halves(corner)
            out = out + (dot(jnp.concatenate([ch, cl], 1), t[2]) + dot(ch, t[3, :LANES]))
        else:
            at = slice(o0 - LANES, o0 + LANES)
            both = dot(xh[:, at], t[4])
            out = both[:, :LANES] + (both[:, LANES:] + dot(xl[:, at], t[4, :, :LANES]))
        store(o0, size, out)


def product(w, dh, dl, rows, store):
    wh, wl = w
    width = dh.shape[1]
    for o0 in range(0, width, ROWS):
        size = min(ROWS, width - o0)
        at = slice(o0, o0 + size)
        if size == ROWS:
            out = dot(wh, dh[rows, at]) + (dot(wl, dh[rows, at]) + dot(wh, dl[rows, at]))
        else:
            both = dot(wh, jnp.concatenate([dh[rows, at], dl[rows, at]], 1))
            out = both[:, :size] + (both[:, size:] + dot(wl, dh[rows, at]))
        store(o0, size, out)


def blur_xz(dh, dl, w, nz, planes_out, store):
    step = ROWS // nz
    for p0 in range(0, planes_out, step):
        m = min(step, planes_out - p0) * nz
        k = min(2 * ROWS, (planes_out + 2 * RADIUS - p0) * nz)
        rows = slice(p0 * nz, p0 * nz + k)
        put = functools.partial(store, p0 * nz, m)
        product((w[0, :m, :k], w[1, :m, :k]), dh, dl, rows, put)


def to_halves(dh, dl, rows):
    def store(o0, size, value):
        h, l = halves(value)
        dh[rows, o0 : o0 + size] = h
        dl[rows, o0 : o0 + size] = l

    return store


def chunks(rows, step=128):
    return [(r, min(step, rows - r)) for r in range(0, rows, step)]


def own_kernel(est, t, w, wr, blurred, dh, dl):
    planes, nz, width = est.shape
    step = LANES // nz
    for p in range(0, planes, step):
        n = min(step, planes - p)
        x = est[p : p + n].reshape(n * nz, width)
        blur_y(x, t.at[0], to_halves(dh, dl, slice(p * nz, (p + n) * nz)))
    total = planes + 2 * RADIUS
    step = ROWS // nz
    for p0 in range(0, total, step):
        out = min(step, total - p0)
        first = max(0, p0 - 2 * RADIUS)
        last = min(planes, p0 + out)
        k = (last - first) * nz
        m = out * nz
        if p0 < 2 * RADIUS:
            assert p0 == 0
            block = wr[1, 0, :m, :k], wr[1, 1, :m, :k]
        else:
            first = p0 - 2 * RADIUS
            block = w[0, 0, :m, :k], w[0, 1, :m, :k]

        def store(o0, size, value):
            blurred[p0 * nz : p0 * nz + m, o0 : o0 + size] = value

        product(block, dh, dl, slice(first * nz, last * nz), store)


def own_share(est, ops):
    planes, nz, width = est.shape
    t, w, wr = ops
    half = pltpu.VMEM((planes * nz, width), BF)
    return pl.pallas_call(
        own_kernel,
        out_shape=jax.ShapeDtypeStruct(((planes + 2 * RADIUS) * nz, width), F32),
        in_specs=[VMEM] * 4,
        out_specs=VMEM,
        scratch_shapes=[half, half],
        compiler_params=PARAMS,
        name="own_share",
    )(est, t, w, wr)


def rim_kernel(split, mine, before, rim, t, wr, blurred, dh, dl):
    planes, nz, width = rim.shape
    n = planes * nz
    side = split.side(mine)
    flat = rim[...].reshape(n, width)
    for r0, count in chunks(n, 112):
        blur_y(flat[r0 : r0 + count, :], t.at[0], to_halves(dh, dl, slice(r0, r0 + count)))
    rows = pl.ds(pl.multiple_of(side * (blurred.shape[0] - n), nz), n)

    def store(o0, size, value):
        blurred[rows, o0 : o0 + size] = before[rows, o0 : o0 + size] + value

    product((wr[side, 0, :n, :n], wr[side, 1, :n, :n]), dh, dl, slice(0, n), store)


def rim_share(split, mine, before, rim, ops):
    planes, nz, width = rim.shape
    half = pltpu.VMEM((planes * nz, width), BF)
    return pl.pallas_call(
        functools.partial(rim_kernel, split, mine),
        out_shape=jax.ShapeDtypeStruct(before.shape, F32),
        in_specs=[VMEM] * 4,
        out_specs=VMEM,
        scratch_shapes=[half, half],
        input_output_aliases={0: 0},
        compiler_params=PARAMS,
        name="rim_share",
    )(before, rim, ops[0], ops[2])


class Piece(NamedTuple):
    at: int
    rows: int
    odd: int
    odd_start: int
    even: int
    even_start: int

    def load(self, refs, odd, r0, n):
        if self.odd != self.even:
            a = refs[self.odd][self.odd_start + r0 : self.odd_start + r0 + n, :]
            b = refs[self.even][self.even_start + r0 : self.even_start + r0 + n, :]
            return jnp.where(odd == 1, a, b)
        start = self.even_start
        if self.odd_start != self.even_start:
            start = jnp.where(odd == 1, self.odd_start, self.even_start)
            start = pl.multiple_of(start, 8)
        return refs[self.odd][pl.ds(start + r0, n), :]


class Span(NamedTuple):
    planes: tuple
    blurred: tuple
    handed: bool
    hands_on: bool


def adjoint_kernel(nz, split, pieces, inputs, span, has_added, ends, *refs):
    refs = list(refs)
    take = lambda n: [refs.pop(0) for _ in range(n)]
    (blurred,), record, (t, w) = take(1), take(inputs), take(2)
    (added,) = take(1) if has_added else (None,)
    handed = take(2) if span.handed else None
    keep, send = take(2) if ends is not None else (None, None)
    (out,) = take(1) if ends is None else (None,)
    hands_on = take(2) if span.hands_on else None
    (out,) = take(1) if ends is not None else (out,)
    dh, dl = refs
    odd = split.odd()
    p0, p1 = span.planes
    base = p0 * nz
    q0, q1 = span.blurred[0] * nz, span.blurred[1] * nz
    if handed is not None:
        dh[: q0 - base, :] = handed[0][...]
        dl[: q0 - base, :] = handed[1][...]
    for piece in pieces:
        lo, hi = max(q0, piece.at), min(q1, piece.at + piece.rows)
        for r0, n in chunks(max(0, hi - lo)):
            at = lo + r0
            q = piece.load(record, odd, at - piece.at, n) / blurred[at : at + n, :]
            blur_y(q, t.at[1], to_halves(dh, dl, slice(at - base, at - base + n)))
    if hands_on is not None:
        hands_on[0][...] = dh[(p1 - p0) * nz :, :]
        hands_on[1][...] = dl[(p1 - p0) * nz :, :]

    def store(r0, m, o0, size, value):
        log = jnp.log(value)
        planes = slice(r0 // nz, (r0 + m) // nz)
        log = log.reshape(m // nz, nz, size)
        if has_added:
            log = log + added[planes, :, o0 : o0 + size]
        out[planes, :, o0 : o0 + size] = log

    blur_xz(dh, dl, w.at[1], nz, p1 - p0, store)
    if ends is not None:
        _, core = split.here()
        lanes = slice(None) if ends == split.width else pl.ds(split.inner(), ends)
        keep[...] = out[:, split.rows(core), lanes]
        send[...] = out[:, split.rows(1 - core), lanes]


def adjoint(split, blurred, record, pieces, ops, span, added, handed, nz, ends=None):
    width = blurred.shape[1]
    planes = span.planes[1] - span.planes[0]
    args = [blurred, *record, *ops[:2]] + ([] if added is None else [added])
    args += [] if handed is None else list(handed)
    rows = (planes + 2 * RADIUS) * nz
    full = (planes, nz, width)
    shapes = [jax.ShapeDtypeStruct(full, F32)]
    scratch = [pltpu.VMEM((rows, width), BF), pltpu.VMEM((rows, width), BF)]
    if ends is not None:
        shapes = [jax.ShapeDtypeStruct((planes, split.half, ends), F32)] * 2
        scratch = [pltpu.VMEM(full, F32)] + scratch
    if span.hands_on:
        shapes += [jax.ShapeDtypeStruct((2 * RADIUS * nz, width), BF)] * 2
    kernel = functools.partial(
        adjoint_kernel, nz, split, pieces, len(record), span, added is not None, ends
    )
    out = pl.pallas_call(
        kernel,
        out_shape=tuple(shapes),
        in_specs=[VMEM] * len(args),
        out_specs=(VMEM,) * len(shapes),
        scratch_shapes=scratch,
        compiler_params=PARAMS,
        name="adjoint",
    )(*args)
    total = out[0] if ends is None else out[:2]
    return total, (out[-2:] if span.hands_on else None)


def spans(nx, count):
    out, done = [], 0
    for c in range(count):
        p0, p1 = c * nx // count, (c + 1) * nx // count
        q1 = p1 + 2 * RADIUS
        out.append(Span((p0, p1), (done, q1), c > 0, c < count - 1))
        done = q1
    return out


def join_kernel(split, planes, *refs):
    parts, out = refs[:-1], refs[-1]
    chip, core = split.here()
    for c, (p0, p1) in enumerate(planes):
        for r in range(split.chips):
            owner = lax.rem(chip + split.chips - r, split.chips)
            lanes = pl.ds(pl.multiple_of(owner * split.part, LANES), split.part)
            mine, sibling = parts[2 * (c * split.chips + r) : 2 * (c * split.chips + r) + 2]
            out[p0:p1, split.rows(core), lanes] = mine[...]
            out[p0:p1, split.rows(1 - core), lanes] = sibling[...]


def join(split, planes, parts, nx, nz):
    return pl.pallas_call(
        functools.partial(join_kernel, split, planes),
        out_shape=jax.ShapeDtypeStruct((nx, nz, split.ny), F32),
        in_specs=[VMEM] * len(parts),
        out_specs=VMEM,
        compiler_params=PARAMS,
        name="join",
    )(*parts)


def steps(recorded, psf_taps, estimate):
    views = lax.axis_size("view")
    tiles = lax.axis_size("tile")
    nx, nz, ny = estimate.shape
    cores = 2
    chips = views // cores
    part = ny // chips
    width = min(ny, part + (LANES if chips <= 2 else 2 * LANES))
    split = Split(chips, cores, part, width, ny, nz // cores)
    assert 2 * RADIUS * ITERS <= LANES and nx >= 2 * RADIUS
    flat = lambda a: a.reshape(-1, a.shape[-1])

    def swap_core(values):
        pairs = [(v, v ^ 1) for v in range(views)]
        return lax.ppermute(values, "view", pairs)

    def to_chip(values, r):
        pairs = [(v, (v + r * cores) % views) for v in range(views)]
        return lax.ppermute(values, "view", pairs)

    next_a = [(t, t ^ 1) for t in range(tiles) if t ^ 1 < tiles]
    next_b = [(t, ((t + 1) ^ 1) - 1) for t in range(1, tiles)]
    next_b = [(t, u) for t, u in next_b if u < tiles]

    def pair_up(a, b):
        b = lax.ppermute(b, "tile", next_b)
        a = lax.ppermute(a, "tile", next_a)
        return a, b

    both = []
    for v in range(views):
        both += [(t * views + v, u * views + v) for t, u in (next_b if v % cores else next_a)]

    def estimate_rims(values):
        mine = lax.ppermute(values, ("tile", "view"), both)
        return mine, swap_core(mine)

    recorded = recorded[0]
    taps = [psf_taps] + [to_chip(psf_taps, r) for r in range(1, chips)]

    def to_a(n, by_core=False):
        return (nx - n, 0, n, by_core)

    def to_b(n):
        return (0, nx - n, n, False)

    rim, body = RADIUS * nz, (nx - 2 * RADIUS) * nz
    end = 2 * rim + body
    outs = []
    for r in range(1, chips):
        outs.append((0, r, (to_a(RADIUS), to_b(RADIUS))))
        outs.append((0, r, ((RADIUS, RADIUS, nx - 2 * RADIUS, False),)))
    outs += [(0, 0, ((0, 0, nx, False),)), (0, 0, (to_a(RADIUS),)), (0, 0, (to_b(RADIUS),))]
    outs += [(1, 0, ((0, 0, nx, False),)), (1, 0, (to_a(2 * RADIUS, True),))]
    cuts = cut((recorded, estimate), split, outs)
    own, own_a, own_b, est, est_rim = cuts[2 * (chips - 1) :]

    edges, middles = [None], [None]
    for r in range(1, chips):
        edges.append(to_chip(cuts[2 * r - 2], r))
        middles.append(to_chip(cuts[2 * r - 1], r))
    rims = estimate_rims(est_rim)
    own_a, own_b = pair_up(own_a, own_b)

    record = [tuple(flat(a) for a in (own_a, own_b, own))]
    before, after = Piece(0, rim, 0, 0, 1, 0), Piece(rim + end, rim, 1, 0, 0, 0)
    pieces = [(before, Piece(rim, end, 2, 0, 2, 0), after)]
    for r in range(1, chips):
        pair_a, pair_b = pair_up(edges[r][:RADIUS], edges[r][RADIUS:])
        record.append(tuple(flat(a) for a in (pair_a, pair_b, edges[r], middles[r])))
        first = Piece(rim, rim, 2, 0, 2, rim)
        inner = Piece(2 * rim, body, 3, 0, 3, 0)
        last = Piece(2 * rim + body, rim, 2, rim, 2, 0)
        pieces.append((before, first, inner, last, after))

    ops = []
    for k in taps:
        ops.append(operators(k, nz))

    for iteration in range(ITERS):
        final = iteration == ITERS - 1
        blurred = []
        for r in range(chips):
            blurred.append(own_share(est, ops[r]))
        for mine in (True, False):
            for r in range(chips):
                rim_planes = rims[0] if mine else rims[1]
                blurred[r] = rim_share(split, mine, blurred[r], rim_planes, ops[r])
        plan = spans(nx, 2)
        handed = [None] * chips
        sums = []
        for span in plan:
            total = None
            for r in range(chips):
                ends = part if final and r == chips - 1 else None
                total, handed[r] = adjoint(
                    split,
                    blurred[r],
                    record[r],
                    pieces[r],
                    ops[r],
                    span,
                    total,
                    handed[r],
                    nz,
                    ends,
                )
            keep, send = total if final else (total, total)
            sums.append((keep, swap_core(send)))
        if not final:
            planes = [span.planes for span in plan]
            est, est_rim = update(split, views, planes, sum(sums, ()), est)
            rims = estimate_rims(est_rim)

    parts = []
    for span, pair in zip(plan, sums):
        done = finish(split, views, span.planes, *pair, est)
        for r in range(chips):
            mine = to_chip(done, r) if r else done
            parts += [mine, swap_core(mine)]
    return join(split, [span.planes for span in plan], parts, nx, nz)


def solution(mesh):
    in_specs = (P("view", "tile", "slab", None), P("view", None, None), P("tile", "slab", None))
    out_specs = P("tile", "slab", None)
    return jax.shard_map(steps, mesh=mesh, in_specs=in_specs, out_specs=out_specs, check_vma=False)
```

```python
import functools
from typing import NamedTuple

import jax
import jax.numpy as jnp
from jax import lax
from jax.experimental import pallas as pl
from jax.experimental.pallas import tpu as pltpu
from jax.sharding import PartitionSpec as P


RADIUS = 7
ITERS = 2
TAPS = 2 * RADIUS + 1
LANES = 128
ROWS = 256
BF = jnp.bfloat16
F32 = jnp.float32
VMEM = pl.BlockSpec(memory_space=pltpu.VMEM)
SMEM = pl.BlockSpec(memory_space=pltpu.SMEM)
ANY = pl.BlockSpec(memory_space=pltpu.HBM)
PARAMS = pltpu.CompilerParams(vmem_limit_bytes=20 * 1024 * 1024)


def halves(value):
    high = value.astype(BF)
    return high, (value - high.astype(F32)).astype(BF)


def dot(a, b):
    return jnp.dot(a, b, preferred_element_type=F32)


class Split(NamedTuple):
    chips: int
    cores: int
    part: int
    width: int
    ny: int
    half: int

    def start(self, chip):
        place = jnp.clip(chip * self.part - LANES, 0, self.ny - self.width)
        return pl.multiple_of(place, LANES)

    def here(self):
        place = lax.axis_index("view")
        return place // self.cores, lax.rem(place, self.cores)

    def inner(self):
        chip, _ = self.here()
        return pl.multiple_of(chip * self.part - self.start(chip), LANES)

    def odd(self):
        return lax.rem(lax.axis_index("tile"), 2)

    def side(self, mine):
        _, core = self.here()
        own = 1 - lax.rem(self.odd() + core, 2)
        return own if mine else 1 - own

    def rows(self, core):
        return pl.ds(pl.multiple_of(core * self.half, self.half), self.half)


def cut_kernel(split, sources, moves, *refs):
    outs, sem = refs[sources:-1], refs[-1]
    chip, _ = split.here()
    copies = []
    for source, ahead, out, at, even, odd, n, by_core in moves:
        lanes = pl.ds(split.start(lax.rem(chip + ahead, split.chips)), split.width)
        which = 1 - split.side(True) if by_core else split.odd()
        x0 = even if even == odd else jnp.where(which == 1, odd, even)
        copies.append(
            pltpu.make_async_copy(
                refs[source].at[pl.ds(x0, n), :, lanes],
                outs[out].at[pl.ds(at, n)],
                sem.at[len(copies)],
            )
        )
        copies[-1].start()
    for copy in copies:
        copy.wait()


def cut(sources, split, outs):
    moves, shapes = [], []
    for index, (source, ahead, ranges) in enumerate(outs):
        at = 0
        for even, odd, n, by_core in ranges:
            moves.append((source, ahead, index, at, even, odd, n, by_core))
            at += n
        shapes.append(jax.ShapeDtypeStruct((at, sources[source].shape[1], split.width), F32))
    return pl.pallas_call(
        functools.partial(cut_kernel, split, len(sources), tuple(moves)),
        out_shape=tuple(shapes),
        in_specs=[ANY] * len(sources),
        out_specs=(VMEM,) * len(shapes),
        scratch_shapes=[pltpu.SemaphoreType.DMA((len(moves),))],
        compiler_params=PARAMS,
        name="cut",
    )(*[pltpu.with_memory_space_constraint(a, pltpu.HBM) for a in sources])


def update_kernel(split, views, planes, *refs):
    est, out, rim = refs[-3:]
    for c, (p0, p1) in enumerate(planes):
        total = refs[2 * c][...] + refs[2 * c + 1][...]
        out[p0:p1] = est[p0:p1] * jnp.exp(total / views)
    n = rim.shape[0]
    rim[...] = out[pl.ds(split.side(True) * (out.shape[0] - n), n)]


def update(split, views, planes, sums, est):
    return pl.pallas_call(
        functools.partial(update_kernel, split, views, planes),
        out_shape=(
            jax.ShapeDtypeStruct(est.shape, F32),
            jax.ShapeDtypeStruct((2 * RADIUS, *est.shape[1:]), F32),
        ),
        in_specs=[VMEM] * (len(sums) + 1),
        out_specs=(VMEM,) * 2,
        compiler_params=PARAMS,
        name="update",
    )(*sums, est)


def finish_kernel(split, views, planes, mine, sibling, est, out):
    _, core = split.here()
    old = est[planes[0] : planes[1], split.rows(core), pl.ds(split.inner(), split.part)]
    out[...] = old * jnp.exp((mine[...] + sibling[...]) / views)


def finish(split, views, planes, mine, sibling, est):
    return pl.pallas_call(
        functools.partial(finish_kernel, split, views, planes),
        out_shape=jax.ShapeDtypeStruct(mine.shape, F32),
        in_specs=[VMEM] * 3,
        out_specs=VMEM,
        compiler_params=PARAMS,
        name="finish",
    )(mine, sibling, est)


GROUP = 8


def operators_kernel(nz, taps, t, last, w, wr, full):
    planes = ROWS // nz
    band = LANES + 3 * GROUP
    first = LANES - GROUP
    i = lax.broadcasted_iota(jnp.int32, (band, LANES), 0) + first
    o = lax.broadcasted_iota(jnp.int32, (band, LANES), 1)
    shift_y = i - o - (LANES - RADIUS)
    row = lax.broadcasted_iota(jnp.int32, (nz, 2 * ROWS), 0)
    col = lax.broadcasted_iota(jnp.int32, (nz, 2 * ROWS), 1)
    shift_x = col // nz
    shift_z = col % nz - row + RADIUS
    sums = []
    for d in range(3):
        value = taps[0, d, 0]
        for k in range(1, TAPS):
            value = value + taps[0, d, k]
        sums.append(value)
    full[...] = jnp.zeros_like(full)
    for mirrored in range(2):
        ty = jnp.zeros((band, LANES), F32)
        kx = jnp.zeros((nz, 2 * ROWS), F32)
        kz = jnp.zeros((nz, 2 * ROWS), F32)
        for k in range(TAPS):
            tap = TAPS - 1 - k if mirrored else k
            kx = jnp.where(shift_x == k, taps[0, 0, tap], kx)
            kz = jnp.where(shift_z == k, taps[0, 1, tap], kz)
            ty = jnp.where(shift_y == k, taps[0, 2, tap], ty)
        kx = kx / sums[0]
        kz = kz / sums[1]
        ty = ty / sums[2]
        for c0 in range(0, ROWS, LANES):
            full[first + c0 : first + c0 + band, c0 : c0 + LANES] = ty
        high, low = halves(full[LANES : LANES + ROWS, :])
        t[mirrored, :ROWS] = high
        t[mirrored, ROWS : 2 * ROWS] = high
        t[mirrored, 2 * ROWS : 3 * ROWS] = low
        right = full[LANES + ROWS : LANES + ROWS + GROUP, :]
        left = full[LANES - GROUP : LANES, :]
        right_high, left_high = right.astype(BF).astype(F32), left.astype(BF).astype(F32)
        none = jnp.zeros((2 * GROUP, ROWS), F32)
        corners = [
            right_high,
            none,
            left_high,
            right_high,
            none,
            left - left_high,
            right - right_high,
            none,
            none,
            none,
            left_high,
        ]
        t[mirrored, 3 * ROWS :] = jnp.concatenate(corners, 0).astype(BF)
        high, low = halves(full[:ROWS, :LANES])
        last[mirrored, :, :LANES] = high
        last[mirrored, :, LANES:] = low
        strip = kx * kz
        for p in range(planes):
            moved = pltpu.roll(strip, p * nz, 1) if p else strip
            rows = slice(p * nz, (p + 1) * nz)
            w[mirrored, 0, rows, :], w[mirrored, 1, rows, :] = halves(moved)
            if not mirrored:
                wr[0, 0, rows, :], wr[0, 1, rows, :] = halves(moved[:, :ROWS])
                back = (p - 2 * RADIUS) * nz % (2 * ROWS)
                moved = pltpu.roll(strip, back, 1)[:, :ROWS] if back else strip[:, :ROWS]
                wr[1, 0, rows, :], wr[1, 1, rows, :] = halves(moved)


class Operators(NamedTuple):
    t: jax.Array
    last: jax.Array
    w: jax.Array
    wr: jax.Array


def operators(taps, nz):
    out = pl.pallas_call(
        functools.partial(operators_kernel, nz),
        out_shape=(
            jax.ShapeDtypeStruct((2, 3 * ROWS + LANES, ROWS), BF),
            jax.ShapeDtypeStruct((2, ROWS, ROWS), BF),
            jax.ShapeDtypeStruct((2, 2, ROWS, 2 * ROWS), BF),
            jax.ShapeDtypeStruct((2, 2, ROWS, ROWS), BF),
        ),
        in_specs=[SMEM],
        out_specs=(VMEM,) * 4,
        scratch_shapes=[pltpu.VMEM((2 * ROWS, ROWS), F32)],
        compiler_params=PARAMS,
        name="operators",
    )(taps)
    return Operators(*out)


def blur_y(x, t, last, store):
    n, width = x.shape
    xh, xl = halves(x)
    lane = lax.broadcasted_iota(jnp.int32, (n, LANES), 1)
    for o0 in range(0, width, ROWS):
        size = min(ROWS, width - o0)
        if size == ROWS:
            end = o0 + ROWS
            at = slice(o0, end)
            corner = jnp.zeros((n, LANES), F32)
            if end < width:
                corner = jnp.where(lane < GROUP, x[:, end : end + LANES], corner)
            if o0:
                corner = jnp.where(lane >= LANES - GROUP, x[:, o0 - LANES : o0], corner)
            high = corner.astype(BF).astype(F32)
            low = pltpu.roll(corner - high, LANES // 4, 1)
            corner = (high + low + pltpu.roll(high, LANES // 2, 1)).astype(BF)
            out = dot(jnp.concatenate([xh[:, at], xl[:, at], xh[:, at], corner], 1), t[...])
        else:
            at = slice(o0 - LANES, o0 + LANES)
            both = dot(xh[:, at], last[...])
            out = both[:, :LANES] + (both[:, LANES:] + dot(xl[:, at], last[:, :LANES]))
        store(o0, size, out)


def product(w, dh, dl, rows, store):
    wh, wl = w
    width = dh.shape[1]
    for o0 in range(0, width, ROWS):
        size = min(ROWS, width - o0)
        at = slice(o0, o0 + size)
        if size == ROWS:
            out = dot(wh, dh[rows, at]) + (dot(wl, dh[rows, at]) + dot(wh, dl[rows, at]))
        else:
            both = dot(wh, jnp.concatenate([dh[rows, at], dl[rows, at]], 1))
            out = both[:, :size] + (both[:, size:] + dot(wl, dh[rows, at]))
        store(o0, size, out)


def blur_xz(dh, dl, w, nz, planes_out, store):
    step = ROWS // nz
    for p0 in range(0, planes_out, step):
        m = min(step, planes_out - p0) * nz
        k = min(2 * ROWS, (planes_out + 2 * RADIUS - p0) * nz)
        rows = slice(p0 * nz, p0 * nz + k)
        put = functools.partial(store, p0 * nz, m)
        product((w[0, :m, :k], w[1, :m, :k]), dh, dl, rows, put)


def to_halves(dh, dl, rows):
    def store(o0, size, value):
        h, l = halves(value)
        dh[rows, o0 : o0 + size] = h
        dl[rows, o0 : o0 + size] = l

    return store


def chunks(rows, step=128):
    return [(r, min(step, rows - r)) for r in range(0, rows, step)]


def own_kernel(est, t, last, w, wr, blurred, dh, dl):
    planes, nz, width = est.shape
    step = LANES // nz
    for p in range(0, planes, step):
        n = min(step, planes - p)
        x = est[p : p + n].reshape(n * nz, width)
        blur_y(x, t.at[0], last.at[0], to_halves(dh, dl, slice(p * nz, (p + n) * nz)))
    total = planes + 2 * RADIUS
    step = ROWS // nz
    for p0 in range(0, total, step):
        out = min(step, total - p0)
        first = max(0, p0 - 2 * RADIUS)
        stop = min(planes, p0 + out)
        k = (stop - first) * nz
        m = out * nz
        if p0 < 2 * RADIUS:
            assert p0 == 0
            block = wr[1, 0, :m, :k], wr[1, 1, :m, :k]
        else:
            first = p0 - 2 * RADIUS
            block = w[0, 0, :m, :k], w[0, 1, :m, :k]

        def store(o0, size, value):
            blurred[p0 * nz : p0 * nz + m, o0 : o0 + size] = value

        product(block, dh, dl, slice(first * nz, stop * nz), store)


def own_share(est, ops):
    planes, nz, width = est.shape
    half = pltpu.VMEM((planes * nz, width), BF)
    return pl.pallas_call(
        own_kernel,
        out_shape=jax.ShapeDtypeStruct(((planes + 2 * RADIUS) * nz, width), F32),
        in_specs=[VMEM] * 5,
        out_specs=VMEM,
        scratch_shapes=[half, half],
        compiler_params=PARAMS,
        name="own_share",
    )(est, *ops)


def rim_kernel(split, mine, before, rim, t, last, wr, blurred, dh, dl):
    planes, nz, width = rim.shape
    n = planes * nz
    side = split.side(mine)
    flat = rim[...].reshape(n, width)
    for r0, count in chunks(n, 112):
        rows = slice(r0, r0 + count)
        blur_y(flat[rows, :], t.at[0], last.at[0], to_halves(dh, dl, rows))
    rows = pl.ds(pl.multiple_of(side * (blurred.shape[0] - n), nz), n)

    def store(o0, size, value):
        blurred[rows, o0 : o0 + size] = before[rows, o0 : o0 + size] + value

    product((wr[side, 0, :n, :n], wr[side, 1, :n, :n]), dh, dl, slice(0, n), store)


def rim_share(split, mine, before, rim, ops):
    planes, nz, width = rim.shape
    half = pltpu.VMEM((planes * nz, width), BF)
    return pl.pallas_call(
        functools.partial(rim_kernel, split, mine),
        out_shape=jax.ShapeDtypeStruct(before.shape, F32),
        in_specs=[VMEM] * 5,
        out_specs=VMEM,
        scratch_shapes=[half, half],
        input_output_aliases={0: 0},
        compiler_params=PARAMS,
        name="rim_share",
    )(before, rim, ops.t, ops.last, ops.wr)


class Piece(NamedTuple):
    at: int
    rows: int
    odd: int
    odd_start: int
    even: int
    even_start: int

    def load(self, refs, odd, r0, n):
        if self.odd != self.even:
            a = refs[self.odd][self.odd_start + r0 : self.odd_start + r0 + n, :]
            b = refs[self.even][self.even_start + r0 : self.even_start + r0 + n, :]
            return jnp.where(odd == 1, a, b)
        start = self.even_start
        if self.odd_start != self.even_start:
            start = jnp.where(odd == 1, self.odd_start, self.even_start)
            start = pl.multiple_of(start, 8)
        return refs[self.odd][pl.ds(start + r0, n), :]


class Span(NamedTuple):
    planes: tuple
    blurred: tuple
    handed: bool
    hands_on: bool


def adjoint_kernel(nz, split, pieces, inputs, span, has_added, ends, *refs):
    refs = list(refs)
    take = lambda n: [refs.pop(0) for _ in range(n)]
    (blurred,), record, (t, last, w) = take(1), take(inputs), take(3)
    (added,) = take(1) if has_added else (None,)
    handed = take(2) if span.handed else None
    keep, send = take(2) if ends is not None else (None, None)
    (out,) = take(1) if ends is None else (None,)
    hands_on = take(2) if span.hands_on else None
    (out,) = take(1) if ends is not None else (out,)
    dh, dl = refs
    odd = split.odd()
    p0, p1 = span.planes
    base = p0 * nz
    q0, q1 = span.blurred[0] * nz, span.blurred[1] * nz
    if handed is not None:
        dh[: q0 - base, :] = handed[0][...]
        dl[: q0 - base, :] = handed[1][...]
    for piece in pieces:
        lo, hi = max(q0, piece.at), min(q1, piece.at + piece.rows)
        for r0, n in chunks(max(0, hi - lo)):
            at = lo + r0
            q = piece.load(record, odd, at - piece.at, n) / blurred[at : at + n, :]
            rows = slice(at - base, at - base + n)
            blur_y(q, t.at[1], last.at[1], to_halves(dh, dl, rows))
    if hands_on is not None:
        hands_on[0][...] = dh[(p1 - p0) * nz :, :]
        hands_on[1][...] = dl[(p1 - p0) * nz :, :]

    def store(r0, m, o0, size, value):
        log = jnp.log(value)
        planes = slice(r0 // nz, (r0 + m) // nz)
        log = log.reshape(m // nz, nz, size)
        if has_added:
            log = log + added[planes, :, o0 : o0 + size]
        out[planes, :, o0 : o0 + size] = log

    blur_xz(dh, dl, w.at[1], nz, p1 - p0, store)
    if ends is not None:
        _, core = split.here()
        lanes = slice(None) if ends == split.width else pl.ds(split.inner(), ends)
        keep[...] = out[:, split.rows(core), lanes]
        send[...] = out[:, split.rows(1 - core), lanes]


def adjoint(split, blurred, record, pieces, ops, span, added, handed, nz, ends=None):
    width = blurred.shape[1]
    planes = span.planes[1] - span.planes[0]
    args = [blurred, *record, *ops[:3]] + ([] if added is None else [added])
    args += [] if handed is None else list(handed)
    rows = (planes + 2 * RADIUS) * nz
    full = (planes, nz, width)
    shapes = [jax.ShapeDtypeStruct(full, F32)]
    scratch = [pltpu.VMEM((rows, width), BF), pltpu.VMEM((rows, width), BF)]
    if ends is not None:
        shapes = [jax.ShapeDtypeStruct((planes, split.half, ends), F32)] * 2
        scratch = [pltpu.VMEM(full, F32)] + scratch
    if span.hands_on:
        shapes += [jax.ShapeDtypeStruct((2 * RADIUS * nz, width), BF)] * 2
    kernel = functools.partial(
        adjoint_kernel, nz, split, pieces, len(record), span, added is not None, ends
    )
    out = pl.pallas_call(
        kernel,
        out_shape=tuple(shapes),
        in_specs=[VMEM] * len(args),
        out_specs=(VMEM,) * len(shapes),
        scratch_shapes=scratch,
        compiler_params=PARAMS,
        name="adjoint",
    )(*args)
    total = out[0] if ends is None else out[:2]
    return total, (out[-2:] if span.hands_on else None)


def spans(nx, count):
    out, done = [], 0
    for c in range(count):
        p0, p1 = c * nx // count, (c + 1) * nx // count
        q1 = p1 + 2 * RADIUS
        out.append(Span((p0, p1), (done, q1), c > 0, c < count - 1))
        done = q1
    return out


def join_kernel(split, planes, *refs):
    parts, out, sem = refs[:-2], refs[-2], refs[-1]
    chip, core = split.here()
    copies = []
    for p0, p1 in planes:
        for r in range(split.chips):
            owner = lax.rem(chip + split.chips - r, split.chips)
            lanes = pl.ds(pl.multiple_of(owner * split.part, LANES), split.part)
            for whose in (core, 1 - core):
                to = out.at[p0:p1, split.rows(whose), lanes]
                copies.append(pltpu.make_async_copy(parts[len(copies)], to, sem.at[len(copies)]))
                copies[-1].start()
    for copy in copies:
        copy.wait()


def join(split, planes, parts, nx, nz):
    return pl.pallas_call(
        functools.partial(join_kernel, split, planes),
        out_shape=jax.ShapeDtypeStruct((nx, nz, split.ny), F32),
        in_specs=[VMEM] * len(parts),
        out_specs=ANY,
        scratch_shapes=[pltpu.SemaphoreType.DMA((len(parts),))],
        compiler_params=PARAMS,
        name="join",
    )(*parts)


def steps(recorded, psf_taps, estimate):
    views = lax.axis_size("view")
    tiles = lax.axis_size("tile")
    nx, nz, ny = estimate.shape
    cores = 2
    chips = views // cores
    part = ny // chips
    width = min(ny, part + (LANES if chips <= 2 else 2 * LANES))
    split = Split(chips, cores, part, width, ny, nz // cores)
    assert 2 * RADIUS * ITERS <= LANES and nx >= 2 * RADIUS
    flat = lambda a: a.reshape(-1, a.shape[-1])

    def swap_core(values):
        pairs = [(v, v ^ 1) for v in range(views)]
        return lax.ppermute(values, "view", pairs)

    def to_chip(values, r):
        pairs = [(v, (v + r * cores) % views) for v in range(views)]
        return lax.ppermute(values, "view", pairs)

    next_a = [(t, t ^ 1) for t in range(tiles) if t ^ 1 < tiles]
    next_b = [(t, ((t + 1) ^ 1) - 1) for t in range(1, tiles)]
    next_b = [(t, u) for t, u in next_b if u < tiles]

    def pair_up(a, b):
        b = lax.ppermute(b, "tile", next_b)
        a = lax.ppermute(a, "tile", next_a)
        return a, b

    both = []
    for v in range(views):
        both += [(t * views + v, u * views + v) for t, u in (next_b if v % cores else next_a)]

    def estimate_rims(values):
        mine = lax.ppermute(values, ("tile", "view"), both)
        return mine, swap_core(mine)

    recorded = recorded[0]
    taps = [psf_taps] + [to_chip(psf_taps, r) for r in range(1, chips)]

    def to_a(n, by_core=False):
        return (nx - n, 0, n, by_core)

    def to_b(n):
        return (0, nx - n, n, False)

    rim, body = RADIUS * nz, (nx - 2 * RADIUS) * nz
    end = 2 * rim + body
    outs = []
    for r in range(1, chips):
        outs.append((0, r, (to_a(RADIUS), to_b(RADIUS))))
        outs.append((0, r, ((RADIUS, RADIUS, nx - 2 * RADIUS, False),)))
    outs += [(0, 0, ((0, 0, nx, False),)), (0, 0, (to_a(RADIUS),)), (0, 0, (to_b(RADIUS),))]
    outs += [(1, 0, ((0, 0, nx, False),)), (1, 0, (to_a(2 * RADIUS, True),))]
    cuts = cut((recorded, estimate), split, outs)
    own, own_a, own_b, est, est_rim = cuts[2 * (chips - 1) :]

    edges, middles = [None], [None]
    for r in range(1, chips):
        edges.append(to_chip(cuts[2 * r - 2], r))
        middles.append(to_chip(cuts[2 * r - 1], r))
    rims = estimate_rims(est_rim)
    own_a, own_b = pair_up(own_a, own_b)

    record = [tuple(flat(a) for a in (own_a, own_b, own))]
    before, after = Piece(0, rim, 0, 0, 1, 0), Piece(rim + end, rim, 1, 0, 0, 0)
    pieces = [(before, Piece(rim, end, 2, 0, 2, 0), after)]
    for r in range(1, chips):
        pair_a, pair_b = pair_up(edges[r][:RADIUS], edges[r][RADIUS:])
        record.append(tuple(flat(a) for a in (pair_a, pair_b, edges[r], middles[r])))
        first = Piece(rim, rim, 2, 0, 2, rim)
        inner = Piece(2 * rim, body, 3, 0, 3, 0)
        last = Piece(2 * rim + body, rim, 2, rim, 2, 0)
        pieces.append((before, first, inner, last, after))

    ops = []
    for k in taps:
        ops.append(operators(k, nz))

    for iteration in range(ITERS):
        final = iteration == ITERS - 1
        blurred = []
        for r in range(chips):
            blurred.append(own_share(est, ops[r]))
        for mine in (True, False):
            for r in range(chips):
                rim_planes = rims[0] if mine else rims[1]
                blurred[r] = rim_share(split, mine, blurred[r], rim_planes, ops[r])
        plan = spans(nx, 2)
        handed = [None] * chips
        sums = []
        for span in plan:
            total = None
            for r in range(chips):
                ends = part if final and r == chips - 1 else None
                total, handed[r] = adjoint(
                    split,
                    blurred[r],
                    record[r],
                    pieces[r],
                    ops[r],
                    span,
                    total,
                    handed[r],
                    nz,
                    ends,
                )
            keep, send = total if final else (total, total)
            sums.append((keep, swap_core(send)))
        if not final:
            planes = [span.planes for span in plan]
            est, est_rim = update(split, views, planes, sum(sums, ()), est)
            rims = estimate_rims(est_rim)

    parts = []
    for span, pair in zip(plan, sums):
        done = finish(split, views, span.planes, *pair, est)
        for r in range(chips):
            mine = to_chip(done, r) if r else done
            parts += [mine, swap_core(mine)]
    return join(split, [span.planes for span in plan], parts, nx, nz)


def solution(mesh):
    in_specs = (P("view", "tile", "slab", None), P("view", None, None), P("tile", "slab", None))
    out_specs = P("tile", "slab", None)
    return jax.shard_map(steps, mesh=mesh, in_specs=in_specs, out_specs=out_specs, check_vma=False)
```

```python
import functools
from typing import NamedTuple

import jax
import jax.numpy as jnp
from jax import lax
from jax.experimental import pallas as pl
from jax.experimental.pallas import tpu as pltpu
from jax.sharding import PartitionSpec as P


RADIUS = 7
ITERS = 2
TAPS = 2 * RADIUS + 1
LANES = 128
ROWS = 256
BF = jnp.bfloat16
F32 = jnp.float32
VMEM = pl.BlockSpec(memory_space=pltpu.VMEM)
SMEM = pl.BlockSpec(memory_space=pltpu.SMEM)
ANY = pl.BlockSpec(memory_space=pltpu.HBM)
PARAMS = pltpu.CompilerParams(vmem_limit_bytes=20 * 1024 * 1024)


def halves(value):
    high = value.astype(BF)
    return high, (value - high.astype(F32)).astype(BF)


def dot(a, b):
    return jnp.dot(a, b, preferred_element_type=F32)


class Split(NamedTuple):
    chips: int
    cores: int
    part: int
    width: int
    ny: int
    half: int
    tiles: int

    def start(self, chip):
        place = jnp.clip(chip * self.part - LANES, 0, self.ny - self.width)
        return pl.multiple_of(place, LANES)

    def here(self):
        place = lax.axis_index("view")
        return place // self.cores, lax.rem(place, self.cores)

    def inner(self):
        chip, _ = self.here()
        return pl.multiple_of(chip * self.part - self.start(chip), LANES)

    def odd(self):
        return lax.rem(lax.axis_index("tile"), 2)

    def side(self, mine):
        _, core = self.here()
        own = 1 - lax.rem(self.odd() + core, 2)
        return own if mine else 1 - own

    def inside(self, side):
        tile = lax.axis_index("tile")
        return jnp.where(side == 0, tile > 0, tile < self.tiles - 1).astype(F32)

    def rows(self, core):
        return pl.ds(pl.multiple_of(core * self.half, self.half), self.half)


def cut_kernel(split, sources, moves, *refs):
    outs, sem = refs[sources:-1], refs[-1]
    chip, _ = split.here()
    copies = []
    for source, ahead, out, at, even, odd, n, by_core in moves:
        lanes = pl.ds(split.start(lax.rem(chip + ahead, split.chips)), split.width)
        which = 1 - split.side(True) if by_core else split.odd()
        x0 = even if even == odd else jnp.where(which == 1, odd, even)
        copies.append(
            pltpu.make_async_copy(
                refs[source].at[pl.ds(x0, n), :, lanes],
                outs[out].at[pl.ds(at, n)],
                sem.at[len(copies)],
            )
        )
        copies[-1].start()
    for copy in copies:
        copy.wait()


def cut(sources, split, outs):
    moves, shapes = [], []
    for index, (source, ahead, ranges) in enumerate(outs):
        at = 0
        for even, odd, n, by_core in ranges:
            moves.append((source, ahead, index, at, even, odd, n, by_core))
            at += n
        shapes.append(jax.ShapeDtypeStruct((at, sources[source].shape[1], split.width), F32))
    return pl.pallas_call(
        functools.partial(cut_kernel, split, len(sources), tuple(moves)),
        out_shape=tuple(shapes),
        in_specs=[ANY] * len(sources),
        out_specs=(VMEM,) * len(shapes),
        scratch_shapes=[pltpu.SemaphoreType.DMA((len(moves),))],
        compiler_params=PARAMS,
        name="cut",
    )(*[pltpu.with_memory_space_constraint(a, pltpu.HBM) for a in sources])


def update_kernel(split, views, planes, *refs):
    est, out, rim = refs[-3:]
    for c, (p0, p1) in enumerate(planes):
        total = refs[2 * c][...] + refs[2 * c + 1][...]
        out[p0:p1] = est[p0:p1] * jnp.exp(total / views)
    n = rim.shape[0]
    rim[...] = out[pl.ds(split.side(True) * (out.shape[0] - n), n)]


def update(split, views, planes, sums, est):
    return pl.pallas_call(
        functools.partial(update_kernel, split, views, planes),
        out_shape=(
            jax.ShapeDtypeStruct(est.shape, F32),
            jax.ShapeDtypeStruct((2 * RADIUS, *est.shape[1:]), F32),
        ),
        in_specs=[VMEM] * (len(sums) + 1),
        out_specs=(VMEM,) * 2,
        compiler_params=PARAMS,
        name="update",
    )(*sums, est)


def finish_kernel(split, views, planes, mine, sibling, est, out):
    _, core = split.here()
    old = est[planes[0] : planes[1], split.rows(core), pl.ds(split.inner(), split.part)]
    out[...] = old * jnp.exp((mine[...] + sibling[...]) / views)


def finish(split, views, planes, mine, sibling, est):
    return pl.pallas_call(
        functools.partial(finish_kernel, split, views, planes),
        out_shape=jax.ShapeDtypeStruct(mine.shape, F32),
        in_specs=[VMEM] * 3,
        out_specs=VMEM,
        compiler_params=PARAMS,
        name="finish",
    )(mine, sibling, est)


GROUP = 8


def operators_kernel(nz, taps, t, last, w, wr, full):
    planes = ROWS // nz
    band = LANES + 3 * GROUP
    first = LANES - GROUP
    i = lax.broadcasted_iota(jnp.int32, (band, LANES), 0) + first
    o = lax.broadcasted_iota(jnp.int32, (band, LANES), 1)
    shift_y = i - o - (LANES - RADIUS)
    row = lax.broadcasted_iota(jnp.int32, (nz, 2 * ROWS), 0)
    col = lax.broadcasted_iota(jnp.int32, (nz, 2 * ROWS), 1)
    shift_x = col // nz
    shift_z = col % nz - row + RADIUS
    sums = []
    for d in range(3):
        value = taps[0, d, 0]
        for k in range(1, TAPS):
            value = value + taps[0, d, k]
        sums.append(value)
    full[...] = jnp.zeros_like(full)
    for mirrored in range(2):
        ty = jnp.zeros((band, LANES), F32)
        kx = jnp.zeros((nz, 2 * ROWS), F32)
        kz = jnp.zeros((nz, 2 * ROWS), F32)
        for k in range(TAPS):
            tap = TAPS - 1 - k if mirrored else k
            kx = jnp.where(shift_x == k, taps[0, 0, tap], kx)
            kz = jnp.where(shift_z == k, taps[0, 1, tap], kz)
            ty = jnp.where(shift_y == k, taps[0, 2, tap], ty)
        kx = kx / sums[0]
        kz = kz / sums[1]
        ty = ty / sums[2]
        for c0 in range(0, ROWS, LANES):
            full[first + c0 : first + c0 + band, c0 : c0 + LANES] = ty
        high, low = halves(full[LANES : LANES + ROWS, :])
        t[mirrored, :ROWS] = high
        t[mirrored, ROWS : 2 * ROWS] = high
        t[mirrored, 2 * ROWS : 3 * ROWS] = low
        right = full[LANES + ROWS : LANES + ROWS + GROUP, :]
        left = full[LANES - GROUP : LANES, :]
        right_high, left_high = right.astype(BF).astype(F32), left.astype(BF).astype(F32)
        none = jnp.zeros((2 * GROUP, ROWS), F32)
        corners = [
            right_high,
            none,
            left_high,
            right_high,
            none,
            left - left_high,
            right - right_high,
            none,
            none,
            none,
            left_high,
        ]
        t[mirrored, 3 * ROWS :] = jnp.concatenate(corners, 0).astype(BF)
        high, low = halves(full[:ROWS, :LANES])
        last[mirrored, :, :LANES] = high
        last[mirrored, :, LANES:] = low
        strip = kx * kz
        for p in range(planes):
            moved = pltpu.roll(strip, p * nz, 1) if p else strip
            rows = slice(p * nz, (p + 1) * nz)
            w[mirrored, 0, rows, :], w[mirrored, 1, rows, :] = halves(moved)
            if not mirrored:
                wr[0, 0, rows, :], wr[0, 1, rows, :] = halves(moved[:, :ROWS])
                back = (p - 2 * RADIUS) * nz % (2 * ROWS)
                moved = pltpu.roll(strip, back, 1)[:, :ROWS] if back else strip[:, :ROWS]
                wr[1, 0, rows, :], wr[1, 1, rows, :] = halves(moved)


class Operators(NamedTuple):
    t: jax.Array
    last: jax.Array
    w: jax.Array
    wr: jax.Array


def operators(taps, nz):
    out = pl.pallas_call(
        functools.partial(operators_kernel, nz),
        out_shape=(
            jax.ShapeDtypeStruct((2, 3 * ROWS + LANES, ROWS), BF),
            jax.ShapeDtypeStruct((2, ROWS, ROWS), BF),
            jax.ShapeDtypeStruct((2, 2, ROWS, 2 * ROWS), BF),
            jax.ShapeDtypeStruct((2, 2, ROWS, ROWS), BF),
        ),
        in_specs=[SMEM],
        out_specs=(VMEM,) * 4,
        scratch_shapes=[pltpu.VMEM((2 * ROWS, ROWS), F32)],
        compiler_params=PARAMS,
        name="operators",
    )(taps)
    return Operators(*out)


def blur_y(x, t, last, store):
    n, width = x.shape
    xh, xl = halves(x)
    lane = lax.broadcasted_iota(jnp.int32, (n, LANES), 1)
    for o0 in range(0, width, ROWS):
        size = min(ROWS, width - o0)
        if size == ROWS:
            end = o0 + ROWS
            at = slice(o0, end)
            corner = jnp.zeros((n, LANES), F32)
            if end < width:
                corner = jnp.where(lane < GROUP, x[:, end : end + LANES], corner)
            if o0:
                corner = jnp.where(lane >= LANES - GROUP, x[:, o0 - LANES : o0], corner)
            high = corner.astype(BF).astype(F32)
            low = pltpu.roll(corner - high, LANES // 4, 1)
            corner = (high + low + pltpu.roll(high, LANES // 2, 1)).astype(BF)
            out = dot(jnp.concatenate([xh[:, at], xl[:, at], xh[:, at], corner], 1), t[...])
        else:
            at = slice(o0 - LANES, o0 + LANES)
            both = dot(xh[:, at], last[...])
            out = both[:, :LANES] + (both[:, LANES:] + dot(xl[:, at], last[:, :LANES]))
        store(o0, size, out)


def product(w, dh, dl, rows, store):
    wh, wl = w
    width = dh.shape[1]
    for o0 in range(0, width, ROWS):
        size = min(ROWS, width - o0)
        at = slice(o0, o0 + size)
        if size == ROWS:
            out = dot(wh, dh[rows, at]) + (dot(wl, dh[rows, at]) + dot(wh, dl[rows, at]))
        else:
            both = dot(wh, jnp.concatenate([dh[rows, at], dl[rows, at]], 1))
            out = both[:, :size] + (both[:, size:] + dot(wl, dh[rows, at]))
        store(o0, size, out)


def blur_xz(dh, dl, w, nz, planes_out, store):
    step = ROWS // nz
    for p0 in range(0, planes_out, step):
        m = min(step, planes_out - p0) * nz
        k = min(2 * ROWS, (planes_out + 2 * RADIUS - p0) * nz)
        rows = slice(p0 * nz, p0 * nz + k)
        put = functools.partial(store, p0 * nz, m)
        product((w[0, :m, :k], w[1, :m, :k]), dh, dl, rows, put)


def to_halves(dh, dl, rows):
    def store(o0, size, value):
        h, l = halves(value)
        dh[rows, o0 : o0 + size] = h
        dl[rows, o0 : o0 + size] = l

    return store


def chunks(rows, step=128):
    return [(r, min(step, rows - r)) for r in range(0, rows, step)]


def own_kernel(est, t, last, w, wr, blurred, dh, dl):
    planes, nz, width = est.shape
    step = LANES // nz
    for p in range(0, planes, step):
        n = min(step, planes - p)
        x = est[p : p + n].reshape(n * nz, width)
        blur_y(x, t.at[0], last.at[0], to_halves(dh, dl, slice(p * nz, (p + n) * nz)))
    total = planes + 2 * RADIUS
    step = ROWS // nz
    for p0 in range(0, total, step):
        out = min(step, total - p0)
        first = max(0, p0 - 2 * RADIUS)
        stop = min(planes, p0 + out)
        k = (stop - first) * nz
        m = out * nz
        if p0 < 2 * RADIUS:
            assert p0 == 0
            block = wr[1, 0, :m, :k], wr[1, 1, :m, :k]
        else:
            first = p0 - 2 * RADIUS
            block = w[0, 0, :m, :k], w[0, 1, :m, :k]

        def store(o0, size, value):
            blurred[p0 * nz : p0 * nz + m, o0 : o0 + size] = value

        product(block, dh, dl, slice(first * nz, stop * nz), store)


def own_share(est, ops):
    planes, nz, width = est.shape
    half = pltpu.VMEM((planes * nz, width), BF)
    return pl.pallas_call(
        own_kernel,
        out_shape=jax.ShapeDtypeStruct(((planes + 2 * RADIUS) * nz, width), F32),
        in_specs=[VMEM] * 5,
        out_specs=VMEM,
        scratch_shapes=[half, half],
        compiler_params=PARAMS,
        name="own_share",
    )(est, *ops)


def rim_kernel(split, mine, before, rim, t, last, wr, blurred, dh, dl):
    planes, nz, width = rim.shape
    n = planes * nz
    side = split.side(mine)
    flat = rim[...].reshape(n, width) * split.inside(side)
    for r0, count in chunks(n, 112):
        rows = slice(r0, r0 + count)
        blur_y(flat[rows, :], t.at[0], last.at[0], to_halves(dh, dl, rows))
    rows = pl.ds(pl.multiple_of(side * (blurred.shape[0] - n), nz), n)

    def store(o0, size, value):
        blurred[rows, o0 : o0 + size] = before[rows, o0 : o0 + size] + value

    product((wr[side, 0, :n, :n], wr[side, 1, :n, :n]), dh, dl, slice(0, n), store)


def rim_share(split, mine, before, rim, ops):
    planes, nz, width = rim.shape
    half = pltpu.VMEM((planes * nz, width), BF)
    return pl.pallas_call(
        functools.partial(rim_kernel, split, mine),
        out_shape=jax.ShapeDtypeStruct(before.shape, F32),
        in_specs=[VMEM] * 5,
        out_specs=VMEM,
        scratch_shapes=[half, half],
        input_output_aliases={0: 0},
        compiler_params=PARAMS,
        name="rim_share",
    )(before, rim, ops.t, ops.last, ops.wr)


class Piece(NamedTuple):
    at: int
    rows: int
    odd: int
    odd_start: int
    even: int
    even_start: int
    outside: int | None = None

    def load(self, refs, odd, r0, n):
        if self.odd != self.even:
            a = refs[self.odd][self.odd_start + r0 : self.odd_start + r0 + n, :]
            b = refs[self.even][self.even_start + r0 : self.even_start + r0 + n, :]
            return jnp.where(odd == 1, a, b)
        start = self.even_start
        if self.odd_start != self.even_start:
            start = jnp.where(odd == 1, self.odd_start, self.even_start)
            start = pl.multiple_of(start, 8)
        return refs[self.odd][pl.ds(start + r0, n), :]


class Span(NamedTuple):
    planes: tuple
    blurred: tuple
    handed: bool
    hands_on: bool


def adjoint_kernel(nz, split, pieces, inputs, span, has_added, ends, *refs):
    refs = list(refs)
    take = lambda n: [refs.pop(0) for _ in range(n)]
    (blurred,), record, (t, last, w) = take(1), take(inputs), take(3)
    (added,) = take(1) if has_added else (None,)
    handed = take(2) if span.handed else None
    keep, send = take(2) if ends is not None else (None, None)
    (out,) = take(1) if ends is None else (None,)
    hands_on = take(2) if span.hands_on else None
    (out,) = take(1) if ends is not None else (out,)
    dh, dl = refs
    odd = split.odd()
    p0, p1 = span.planes
    base = p0 * nz
    q0, q1 = span.blurred[0] * nz, span.blurred[1] * nz
    if handed is not None:
        dh[: q0 - base, :] = handed[0][...]
        dl[: q0 - base, :] = handed[1][...]
    for piece in pieces:
        lo, hi = max(q0, piece.at), min(q1, piece.at + piece.rows)
        for r0, n in chunks(max(0, hi - lo)):
            at = lo + r0
            q = piece.load(record, odd, at - piece.at, n)
            if piece.outside is not None:
                q = q * split.inside(piece.outside)
            q = q / blurred[at : at + n, :]
            rows = slice(at - base, at - base + n)
            blur_y(q, t.at[1], last.at[1], to_halves(dh, dl, rows))
    if hands_on is not None:
        hands_on[0][...] = dh[(p1 - p0) * nz :, :]
        hands_on[1][...] = dl[(p1 - p0) * nz :, :]

    def store(r0, m, o0, size, value):
        log = jnp.log(value)
        planes = slice(r0 // nz, (r0 + m) // nz)
        log = log.reshape(m // nz, nz, size)
        if has_added:
            log = log + added[planes, :, o0 : o0 + size]
        out[planes, :, o0 : o0 + size] = log

    blur_xz(dh, dl, w.at[1], nz, p1 - p0, store)
    if ends is not None:
        _, core = split.here()
        lanes = slice(None) if ends == split.width else pl.ds(split.inner(), ends)
        keep[...] = out[:, split.rows(core), lanes]
        send[...] = out[:, split.rows(1 - core), lanes]


def adjoint(split, blurred, record, pieces, ops, span, added, handed, nz, ends=None):
    width = blurred.shape[1]
    planes = span.planes[1] - span.planes[0]
    args = [blurred, *record, *ops[:3]] + ([] if added is None else [added])
    args += [] if handed is None else list(handed)
    rows = (planes + 2 * RADIUS) * nz
    full = (planes, nz, width)
    shapes = [jax.ShapeDtypeStruct(full, F32)]
    scratch = [pltpu.VMEM((rows, width), BF), pltpu.VMEM((rows, width), BF)]
    if ends is not None:
        shapes = [jax.ShapeDtypeStruct((planes, split.half, ends), F32)] * 2
        scratch = [pltpu.VMEM(full, F32)] + scratch
    if span.hands_on:
        shapes += [jax.ShapeDtypeStruct((2 * RADIUS * nz, width), BF)] * 2
    kernel = functools.partial(
        adjoint_kernel, nz, split, pieces, len(record), span, added is not None, ends
    )
    out = pl.pallas_call(
        kernel,
        out_shape=tuple(shapes),
        in_specs=[VMEM] * len(args),
        out_specs=(VMEM,) * len(shapes),
        scratch_shapes=scratch,
        compiler_params=PARAMS,
        name="adjoint",
    )(*args)
    total = out[0] if ends is None else out[:2]
    return total, (out[-2:] if span.hands_on else None)


def spans(nx, count):
    out, done = [], 0
    for c in range(count):
        p0, p1 = c * nx // count, (c + 1) * nx // count
        q1 = p1 + 2 * RADIUS
        out.append(Span((p0, p1), (done, q1), c > 0, c < count - 1))
        done = q1
    return out


def join_kernel(split, planes, *refs):
    parts, out, sem = refs[:-2], refs[-2], refs[-1]
    chip, core = split.here()
    copies = []
    for p0, p1 in planes:
        for r in range(split.chips):
            owner = lax.rem(chip + split.chips - r, split.chips)
            lanes = pl.ds(pl.multiple_of(owner * split.part, LANES), split.part)
            for whose in (core, 1 - core):
                to = out.at[p0:p1, split.rows(whose), lanes]
                copies.append(pltpu.make_async_copy(parts[len(copies)], to, sem.at[len(copies)]))
                copies[-1].start()
    for copy in copies:
        copy.wait()


def join(split, planes, parts, nx, nz):
    return pl.pallas_call(
        functools.partial(join_kernel, split, planes),
        out_shape=jax.ShapeDtypeStruct((nx, nz, split.ny), F32),
        in_specs=[VMEM] * len(parts),
        out_specs=ANY,
        scratch_shapes=[pltpu.SemaphoreType.DMA((len(parts),))],
        compiler_params=PARAMS,
        name="join",
    )(*parts)


def steps(recorded, psf_taps, estimate):
    views = lax.axis_size("view")
    tiles = lax.axis_size("tile")
    nx, nz, ny = estimate.shape
    cores = 2
    chips = views // cores
    part = ny // chips
    width = min(ny, part + (LANES if chips <= 2 else 2 * LANES))
    split = Split(chips, cores, part, width, ny, nz // cores, tiles)
    assert 2 * RADIUS * ITERS <= LANES and nx >= 2 * RADIUS
    flat = lambda a: a.reshape(-1, a.shape[-1])

    def swap_core(values):
        pairs = [(v, v ^ 1) for v in range(views)]
        return lax.ppermute(values, "view", pairs)

    def to_chip(values, r):
        pairs = [(v, (v + r * cores) % views) for v in range(views)]
        return lax.ppermute(values, "view", pairs)

    slabs = lax.axis_size("slab")
    axes = ("slab", "tile", "view")

    def partner(s, t, pair_b):
        u = ((t + 1) ^ 1) - 1 if pair_b else t ^ 1
        return (s, u) if 0 <= u < tiles else (s ^ 1, t)

    def pairs_of(is_b):
        pairs = []
        for s in range(slabs):
            for t in range(tiles):
                for v in range(views):
                    to, u = partner(s, t, is_b(v))
                    if to < slabs:
                        here = (s * tiles + t) * views + v
                        pairs.append((here, (to * tiles + u) * views + v))
        return pairs

    def pair_up(a, b):
        b = lax.ppermute(b, axes, pairs_of(lambda v: True))
        a = lax.ppermute(a, axes, pairs_of(lambda v: False))
        return a, b

    def estimate_rims(values):
        mine = lax.ppermute(values, axes, pairs_of(lambda v: v % cores == 1))
        return mine, swap_core(mine)

    recorded = recorded[0]
    taps = [psf_taps] + [to_chip(psf_taps, r) for r in range(1, chips)]

    def to_a(n, by_core=False):
        return (nx - n, 0, n, by_core)

    def to_b(n):
        return (0, nx - n, n, False)

    rim, body = RADIUS * nz, (nx - 2 * RADIUS) * nz
    end = 2 * rim + body
    outs = []
    for r in range(1, chips):
        outs.append((0, r, (to_a(RADIUS), to_b(RADIUS))))
        outs.append((0, r, ((RADIUS, RADIUS, nx - 2 * RADIUS, False),)))
    outs += [(0, 0, ((0, 0, nx, False),)), (0, 0, (to_a(RADIUS),)), (0, 0, (to_b(RADIUS),))]
    outs += [(1, 0, ((0, 0, nx, False),)), (1, 0, (to_a(2 * RADIUS, True),))]
    cuts = cut((recorded, estimate), split, outs)
    own, own_a, own_b, est, est_rim = cuts[2 * (chips - 1) :]

    edges, middles = [None], [None]
    for r in range(1, chips):
        edges.append(to_chip(cuts[2 * r - 2], r))
        middles.append(to_chip(cuts[2 * r - 1], r))
    rims = estimate_rims(est_rim)
    own_a, own_b = pair_up(own_a, own_b)

    record = [tuple(flat(a) for a in (own_a, own_b, own))]
    before = Piece(0, rim, 0, 0, 1, 0, 0)
    after = Piece(rim + end, rim, 1, 0, 0, 0, 1)
    pieces = [(before, Piece(rim, end, 2, 0, 2, 0), after)]
    for r in range(1, chips):
        pair_a, pair_b = pair_up(edges[r][:RADIUS], edges[r][RADIUS:])
        record.append(tuple(flat(a) for a in (pair_a, pair_b, edges[r], middles[r])))
        first = Piece(rim, rim, 2, 0, 2, rim)
        inner = Piece(2 * rim, body, 3, 0, 3, 0)
        last = Piece(2 * rim + body, rim, 2, rim, 2, 0)
        pieces.append((before, first, inner, last, after))

    ops = []
    for k in taps:
        ops.append(operators(k, nz))

    for iteration in range(ITERS):
        final = iteration == ITERS - 1
        blurred = []
        for r in range(chips):
            blurred.append(own_share(est, ops[r]))
        for mine in (True, False):
            for r in range(chips):
                rim_planes = rims[0] if mine else rims[1]
                blurred[r] = rim_share(split, mine, blurred[r], rim_planes, ops[r])
        plan = spans(nx, 2)
        handed = [None] * chips
        sums = []
        for span in plan:
            total = None
            for r in range(chips):
                ends = part if final and r == chips - 1 else None
                total, handed[r] = adjoint(
                    split,
                    blurred[r],
                    record[r],
                    pieces[r],
                    ops[r],
                    span,
                    total,
                    handed[r],
                    nz,
                    ends,
                )
            keep, send = total if final else (total, total)
            sums.append((keep, swap_core(send)))
        if not final:
            planes = [span.planes for span in plan]
            est, est_rim = update(split, views, planes, sum(sums, ()), est)
            rims = estimate_rims(est_rim)

    parts = []
    for span, pair in zip(plan, sums):
        done = finish(split, views, span.planes, *pair, est)
        for r in range(chips):
            mine = to_chip(done, r) if r else done
            parts += [mine, swap_core(mine)]
    return join(split, [span.planes for span in plan], parts, nx, nz)


def solution(mesh):
    in_specs = (P("view", "tile", "slab", None), P("view", None, None), P("tile", "slab", None))
    out_specs = P("tile", "slab", None)
    return jax.shard_map(steps, mesh=mesh, in_specs=in_specs, out_specs=out_specs, check_vma=False)
```

```python
import functools
from typing import NamedTuple

import jax
import jax.numpy as jnp
from jax import lax
from jax.experimental import pallas as pl
from jax.experimental.pallas import tpu as pltpu
from jax.sharding import PartitionSpec as P


RADIUS = 7
ITERS = 2
TAPS = 2 * RADIUS + 1
LANES = 128
ROWS = 256
BF = jnp.bfloat16
F32 = jnp.float32
VMEM = pl.BlockSpec(memory_space=pltpu.VMEM)
SMEM = pl.BlockSpec(memory_space=pltpu.SMEM)
ANY = pl.BlockSpec(memory_space=pltpu.HBM)
PARAMS = pltpu.CompilerParams(vmem_limit_bytes=20 * 1024 * 1024)


def halves(value):
    high = value.astype(BF)
    return high, (value - high.astype(F32)).astype(BF)


def dot(a, b):
    return jnp.dot(a, b, preferred_element_type=F32)


class Split(NamedTuple):
    chips: int
    cores: int
    part: int
    width: int
    ny: int
    half: int
    tiles: int

    def start(self, chip):
        place = jnp.clip(chip * self.part - LANES, 0, self.ny - self.width)
        return pl.multiple_of(place, LANES)

    def here(self):
        place = lax.axis_index("view")
        return place // self.cores, lax.rem(place, self.cores)

    def inner(self):
        chip, _ = self.here()
        return pl.multiple_of(chip * self.part - self.start(chip), LANES)

    def odd(self):
        return lax.rem(lax.axis_index("tile"), 2)

    def side(self, mine):
        _, core = self.here()
        own = 1 - lax.rem(self.odd() + core, 2)
        return own if mine else 1 - own

    def inside(self, side):
        tile = lax.axis_index("tile")
        return jnp.where(side == 0, tile > 0, tile < self.tiles - 1).astype(F32)

    def rows(self, core):
        return pl.ds(pl.multiple_of(core * self.half, self.half), self.half)


def cut_kernel(split, sources, moves, *refs):
    outs, sem = refs[sources:-1], refs[-1]
    chip, _ = split.here()
    copies = []
    for source, ahead, out, at, even, odd, n, by_core in moves:
        lanes = pl.ds(split.start(lax.rem(chip + ahead, split.chips)), split.width)
        which = 1 - split.side(True) if by_core else split.odd()
        x0 = even if even == odd else jnp.where(which == 1, odd, even)
        copies.append(
            pltpu.make_async_copy(
                refs[source].at[pl.ds(x0, n), :, lanes],
                outs[out].at[pl.ds(at, n)],
                sem.at[len(copies)],
            )
        )
        copies[-1].start()
    for copy in copies:
        copy.wait()


def cut(sources, split, outs):
    moves, shapes = [], []
    for index, (source, ahead, ranges) in enumerate(outs):
        at = 0
        for even, odd, n, by_core in ranges:
            moves.append((source, ahead, index, at, even, odd, n, by_core))
            at += n
        shapes.append(jax.ShapeDtypeStruct((at, sources[source].shape[1], split.width), F32))
    return pl.pallas_call(
        functools.partial(cut_kernel, split, len(sources), tuple(moves)),
        out_shape=tuple(shapes),
        in_specs=[ANY] * len(sources),
        out_specs=(VMEM,) * len(shapes),
        scratch_shapes=[pltpu.SemaphoreType.DMA((len(moves),))],
        compiler_params=PARAMS,
        name="cut",
    )(*[pltpu.with_memory_space_constraint(a, pltpu.HBM) for a in sources])


def update_kernel(split, views, planes, *refs):
    est, out, rim = refs[-3:]
    for c, (p0, p1) in enumerate(planes):
        total = refs[2 * c][...] + refs[2 * c + 1][...]
        out[p0:p1] = est[p0:p1] * jnp.exp(total / views)
    n = rim.shape[0]
    rim[...] = out[pl.ds(split.side(True) * (out.shape[0] - n), n)]


def update(split, views, planes, sums, est):
    return pl.pallas_call(
        functools.partial(update_kernel, split, views, planes),
        out_shape=(
            jax.ShapeDtypeStruct(est.shape, F32),
            jax.ShapeDtypeStruct((2 * RADIUS, *est.shape[1:]), F32),
        ),
        in_specs=[VMEM] * (len(sums) + 1),
        out_specs=(VMEM,) * 2,
        compiler_params=PARAMS,
        name="update",
    )(*sums, est)


def finish_kernel(split, views, planes, mine, sibling, est, out):
    _, core = split.here()
    old = est[planes[0] : planes[1], split.rows(core), pl.ds(split.inner(), split.part)]
    out[...] = old * jnp.exp((mine[...] + sibling[...]) / views)


def finish(split, views, planes, mine, sibling, est):
    return pl.pallas_call(
        functools.partial(finish_kernel, split, views, planes),
        out_shape=jax.ShapeDtypeStruct(mine.shape, F32),
        in_specs=[VMEM] * 3,
        out_specs=VMEM,
        compiler_params=PARAMS,
        name="finish",
    )(mine, sibling, est)


GROUP = 8


def operators_kernel(nz, taps, t, last, w, wr, full):
    planes = ROWS // nz
    band = LANES + 3 * GROUP
    first = LANES - GROUP
    i = lax.broadcasted_iota(jnp.int32, (band, LANES), 0) + first
    o = lax.broadcasted_iota(jnp.int32, (band, LANES), 1)
    shift_y = i - o - (LANES - RADIUS)
    row = lax.broadcasted_iota(jnp.int32, (nz, 2 * ROWS), 0)
    col = lax.broadcasted_iota(jnp.int32, (nz, 2 * ROWS), 1)
    shift_x = col // nz
    shift_z = col % nz - row + RADIUS
    sums = []
    for d in range(3):
        value = taps[0, d, 0]
        for k in range(1, TAPS):
            value = value + taps[0, d, k]
        sums.append(value)
    full[...] = jnp.zeros_like(full)
    for mirrored in range(2):
        ty = jnp.zeros((band, LANES), F32)
        kx = jnp.zeros((nz, 2 * ROWS), F32)
        kz = jnp.zeros((nz, 2 * ROWS), F32)
        for k in range(TAPS):
            tap = TAPS - 1 - k if mirrored else k
            kx = jnp.where(shift_x == k, taps[0, 0, tap], kx)
            kz = jnp.where(shift_z == k, taps[0, 1, tap], kz)
            ty = jnp.where(shift_y == k, taps[0, 2, tap], ty)
        kx = kx / sums[0]
        kz = kz / sums[1]
        ty = ty / sums[2]
        for c0 in range(0, ROWS, LANES):
            full[first + c0 : first + c0 + band, c0 : c0 + LANES] = ty
        high, low = halves(full[LANES : LANES + ROWS, :])
        t[mirrored, :ROWS] = high
        t[mirrored, ROWS : 2 * ROWS] = high
        t[mirrored, 2 * ROWS : 3 * ROWS] = low
        right = full[LANES + ROWS : LANES + ROWS + GROUP, :]
        left = full[LANES - GROUP : LANES, :]
        right_high, left_high = right.astype(BF).astype(F32), left.astype(BF).astype(F32)
        none = jnp.zeros((2 * GROUP, ROWS), F32)
        corners = [
            right_high,
            none,
            left_high,
            right_high,
            none,
            left - left_high,
            right - right_high,
            none,
            none,
            none,
            left_high,
        ]
        t[mirrored, 3 * ROWS :] = jnp.concatenate(corners, 0).astype(BF)
        high, low = halves(full[:ROWS, :LANES])
        last[mirrored, :, :LANES] = high
        last[mirrored, :, LANES:] = low
        strip = kx * kz
        for p in range(planes):
            moved = pltpu.roll(strip, p * nz, 1) if p else strip
            rows = slice(p * nz, (p + 1) * nz)
            w[mirrored, 0, rows, :], w[mirrored, 1, rows, :] = halves(moved)
            if not mirrored:
                wr[0, 0, rows, :], wr[0, 1, rows, :] = halves(moved[:, :ROWS])
                back = (p - 2 * RADIUS) * nz % (2 * ROWS)
                moved = pltpu.roll(strip, back, 1)[:, :ROWS] if back else strip[:, :ROWS]
                wr[1, 0, rows, :], wr[1, 1, rows, :] = halves(moved)


class Operators(NamedTuple):
    t: jax.Array
    last: jax.Array
    w: jax.Array
    wr: jax.Array


def operators(taps, nz):
    out = pl.pallas_call(
        functools.partial(operators_kernel, nz),
        out_shape=(
            jax.ShapeDtypeStruct((2, 3 * ROWS + LANES, ROWS), BF),
            jax.ShapeDtypeStruct((2, ROWS, ROWS), BF),
            jax.ShapeDtypeStruct((2, 2, ROWS, 2 * ROWS), BF),
            jax.ShapeDtypeStruct((2, 2, ROWS, ROWS), BF),
        ),
        in_specs=[SMEM],
        out_specs=(VMEM,) * 4,
        scratch_shapes=[pltpu.VMEM((2 * ROWS, ROWS), F32)],
        compiler_params=PARAMS,
        name="operators",
    )(taps)
    return Operators(*out)


def blur_y(x, t, last, store):
    n, width = x.shape
    xh, xl = halves(x)
    lane = lax.broadcasted_iota(jnp.int32, (n, LANES), 1)
    for o0 in range(0, width, ROWS):
        size = min(ROWS, width - o0)
        if size == ROWS:
            end = o0 + ROWS
            at = slice(o0, end)
            corner = jnp.zeros((n, LANES), F32)
            if end < width:
                corner = jnp.where(lane < GROUP, x[:, end : end + LANES], corner)
            if o0:
                corner = jnp.where(lane >= LANES - GROUP, x[:, o0 - LANES : o0], corner)
            high = corner.astype(BF).astype(F32)
            low = pltpu.roll(corner - high, LANES // 4, 1)
            corner = (high + low + pltpu.roll(high, LANES // 2, 1)).astype(BF)
            out = dot(jnp.concatenate([xh[:, at], xl[:, at], xh[:, at], corner], 1), t[...])
        else:
            at = slice(o0 - LANES, o0 + LANES)
            both = dot(xh[:, at], last[...])
            out = both[:, :LANES] + (both[:, LANES:] + dot(xl[:, at], last[:, :LANES]))
        store(o0, size, out)


def product(w, dh, dl, rows, store):
    wh, wl = w
    width = dh.shape[1]
    for o0 in range(0, width, ROWS):
        size = min(ROWS, width - o0)
        at = slice(o0, o0 + size)
        if size == ROWS:
            out = dot(wh, dh[rows, at]) + (dot(wl, dh[rows, at]) + dot(wh, dl[rows, at]))
        else:
            both = dot(wh, jnp.concatenate([dh[rows, at], dl[rows, at]], 1))
            out = both[:, :size] + (both[:, size:] + dot(wl, dh[rows, at]))
        store(o0, size, out)


def blur_xz(dh, dl, w, nz, planes_out, store):
    step = ROWS // nz
    for p0 in range(0, planes_out, step):
        m = min(step, planes_out - p0) * nz
        k = min(2 * ROWS, (planes_out + 2 * RADIUS - p0) * nz)
        rows = slice(p0 * nz, p0 * nz + k)
        put = functools.partial(store, p0 * nz, m)
        product((w[0, :m, :k], w[1, :m, :k]), dh, dl, rows, put)


def to_halves(dh, dl, rows):
    def store(o0, size, value):
        h, l = halves(value)
        dh[rows, o0 : o0 + size] = h
        dl[rows, o0 : o0 + size] = l

    return store


def chunks(rows, step=128):
    return [(r, min(step, rows - r)) for r in range(0, rows, step)]


def own_kernel(est, t, last, w, wr, blurred, dh, dl):
    planes, nz, width = est.shape
    step = LANES // nz
    for p in range(0, planes, step):
        n = min(step, planes - p)
        x = est[p : p + n].reshape(n * nz, width)
        blur_y(x, t.at[0], last.at[0], to_halves(dh, dl, slice(p * nz, (p + n) * nz)))
    total = planes + 2 * RADIUS
    step = ROWS // nz
    for p0 in range(0, total, step):
        out = min(step, total - p0)
        first = max(0, p0 - 2 * RADIUS)
        stop = min(planes, p0 + out)
        k = (stop - first) * nz
        m = out * nz
        if p0 < 2 * RADIUS:
            assert p0 == 0
            block = wr[1, 0, :m, :k], wr[1, 1, :m, :k]
        else:
            first = p0 - 2 * RADIUS
            block = w[0, 0, :m, :k], w[0, 1, :m, :k]

        def store(o0, size, value):
            blurred[p0 * nz : p0 * nz + m, o0 : o0 + size] = value

        product(block, dh, dl, slice(first * nz, stop * nz), store)


def own_share(est, ops):
    planes, nz, width = est.shape
    half = pltpu.VMEM((planes * nz, width), BF)
    return pl.pallas_call(
        own_kernel,
        out_shape=jax.ShapeDtypeStruct(((planes + 2 * RADIUS) * nz, width), F32),
        in_specs=[VMEM] * 5,
        out_specs=VMEM,
        scratch_shapes=[half, half],
        compiler_params=PARAMS,
        name="own_share",
    )(est, *ops)


def rim_kernel(split, mine, views, rim, *refs):
    planes, nz, width = rim.shape
    n = planes * nz
    side = split.side(mine)
    flat = rim[...].reshape(n, width) * split.inside(side)
    befores, refs = refs[:views], refs[views:]
    ops, refs = refs[: 3 * views], refs[3 * views :]
    blurreds, halves_of = refs[:views], refs[views:]
    for r in range(views):
        t, last, wr = ops[3 * r : 3 * r + 3]
        dh, dl = halves_of[2 * r : 2 * r + 2]
        for r0, count in chunks(n, 112):
            rows = slice(r0, r0 + count)
            blur_y(flat[rows, :], t.at[0], last.at[0], to_halves(dh, dl, rows))
    for r in range(views):
        wr = ops[3 * r + 2]
        before, blurred = befores[r], blurreds[r]
        dh, dl = halves_of[2 * r : 2 * r + 2]
        rows = pl.ds(pl.multiple_of(side * (blurred.shape[0] - n), nz), n)

        def store(o0, size, value):
            blurred[rows, o0 : o0 + size] = before[rows, o0 : o0 + size] + value

        product((wr[side, 0, :n, :n], wr[side, 1, :n, :n]), dh, dl, slice(0, n), store)


def rim_share(split, mine, befores, rim, ops):
    planes, nz, width = rim.shape
    half = pltpu.VMEM((planes * nz, width), BF)
    views = len(befores)
    return list(
        pl.pallas_call(
            functools.partial(rim_kernel, split, mine, views),
            out_shape=tuple(jax.ShapeDtypeStruct(b.shape, F32) for b in befores),
            in_specs=[VMEM] * (1 + 4 * views),
            out_specs=(VMEM,) * views,
            scratch_shapes=[half] * (2 * views),
            input_output_aliases={1 + r: r for r in range(views)},
            compiler_params=PARAMS,
            name="rim_share",
        )(rim, *befores, *[x for o in ops for x in (o.t, o.last, o.wr)])
    )


class Piece(NamedTuple):
    at: int
    rows: int
    odd: int
    odd_start: int
    even: int
    even_start: int
    outside: int | None = None

    def load(self, refs, odd, r0, n):
        if self.odd != self.even:
            a = refs[self.odd][self.odd_start + r0 : self.odd_start + r0 + n, :]
            b = refs[self.even][self.even_start + r0 : self.even_start + r0 + n, :]
            return jnp.where(odd == 1, a, b)
        start = self.even_start
        if self.odd_start != self.even_start:
            start = jnp.where(odd == 1, self.odd_start, self.even_start)
            start = pl.multiple_of(start, 8)
        return refs[self.odd][pl.ds(start + r0, n), :]


class Span(NamedTuple):
    planes: tuple
    blurred: tuple
    handed: bool
    hands_on: bool


def adjoint_kernel(nz, split, pieces, inputs, span, has_added, ends, *refs):
    refs = list(refs)
    take = lambda n: [refs.pop(0) for _ in range(n)]
    (blurred,), record, (t, last, w) = take(1), take(inputs), take(3)
    (added,) = take(1) if has_added else (None,)
    handed = take(2) if span.handed else None
    keep, send = take(2) if ends is not None else (None, None)
    (out,) = take(1) if ends is None else (None,)
    hands_on = take(2) if span.hands_on else None
    (out,) = take(1) if ends is not None else (out,)
    dh, dl = refs
    odd = split.odd()
    p0, p1 = span.planes
    base = p0 * nz
    q0, q1 = span.blurred[0] * nz, span.blurred[1] * nz
    if handed is not None:
        dh[: q0 - base, :] = handed[0][...]
        dl[: q0 - base, :] = handed[1][...]
    for piece in pieces:
        lo, hi = max(q0, piece.at), min(q1, piece.at + piece.rows)
        for r0, n in chunks(max(0, hi - lo)):
            at = lo + r0
            q = piece.load(record, odd, at - piece.at, n)
            if piece.outside is not None:
                q = q * split.inside(piece.outside)
            q = q / blurred[at : at + n, :]
            rows = slice(at - base, at - base + n)
            blur_y(q, t.at[1], last.at[1], to_halves(dh, dl, rows))
    if hands_on is not None:
        hands_on[0][...] = dh[(p1 - p0) * nz :, :]
        hands_on[1][...] = dl[(p1 - p0) * nz :, :]

    def store(r0, m, o0, size, value):
        log = jnp.log(value)
        planes = slice(r0 // nz, (r0 + m) // nz)
        log = log.reshape(m // nz, nz, size)
        if has_added:
            log = log + added[planes, :, o0 : o0 + size]
        out[planes, :, o0 : o0 + size] = log

    blur_xz(dh, dl, w.at[1], nz, p1 - p0, store)
    if ends is not None:
        _, core = split.here()
        lanes = slice(None) if ends == split.width else pl.ds(split.inner(), ends)
        keep[...] = out[:, split.rows(core), lanes]
        send[...] = out[:, split.rows(1 - core), lanes]


def adjoint(split, blurred, record, pieces, ops, span, added, handed, nz, ends=None):
    width = blurred.shape[1]
    planes = span.planes[1] - span.planes[0]
    args = [blurred, *record, *ops[:3]] + ([] if added is None else [added])
    args += [] if handed is None else list(handed)
    rows = (planes + 2 * RADIUS) * nz
    full = (planes, nz, width)
    shapes = [jax.ShapeDtypeStruct(full, F32)]
    scratch = [pltpu.VMEM((rows, width), BF), pltpu.VMEM((rows, width), BF)]
    if ends is not None:
        shapes = [jax.ShapeDtypeStruct((planes, split.half, ends), F32)] * 2
        scratch = [pltpu.VMEM(full, F32)] + scratch
    if span.hands_on:
        shapes += [jax.ShapeDtypeStruct((2 * RADIUS * nz, width), BF)] * 2
    kernel = functools.partial(
        adjoint_kernel, nz, split, pieces, len(record), span, added is not None, ends
    )
    out = pl.pallas_call(
        kernel,
        out_shape=tuple(shapes),
        in_specs=[VMEM] * len(args),
        out_specs=(VMEM,) * len(shapes),
        scratch_shapes=scratch,
        compiler_params=PARAMS,
        name="adjoint",
    )(*args)
    total = out[0] if ends is None else out[:2]
    return total, (out[-2:] if span.hands_on else None)


def spans(nx, count):
    out, done = [], 0
    for c in range(count):
        p0, p1 = c * nx // count, (c + 1) * nx // count
        q1 = p1 + 2 * RADIUS
        out.append(Span((p0, p1), (done, q1), c > 0, c < count - 1))
        done = q1
    return out


def join_kernel(split, places, *refs):
    parts, out, sem = refs[: len(places)], refs[-2], refs[-1]
    chip, core = split.here()
    copies = []
    for part, (p0, p1, r, mine) in zip(parts, places):
        owner = lax.rem(chip + split.chips - r, split.chips)
        lanes = pl.ds(pl.multiple_of(owner * split.part, LANES), split.part)
        to = out.at[p0:p1, split.rows(core if mine else 1 - core), lanes]
        copies.append(pltpu.make_async_copy(part, to, sem.at[len(copies)]))
        copies[-1].start()
    for copy in copies:
        copy.wait()


def join(split, pieces, out, nx, nz):
    places, parts = zip(*pieces)
    return pl.pallas_call(
        functools.partial(join_kernel, split, places),
        out_shape=jax.ShapeDtypeStruct((nx, nz, split.ny), F32),
        in_specs=[VMEM] * len(parts) + ([] if out is None else [ANY]),
        out_specs=ANY,
        scratch_shapes=[pltpu.SemaphoreType.DMA((len(parts),))],
        input_output_aliases={} if out is None else {len(parts): 0},
        compiler_params=PARAMS,
        name="join",
    )(*parts, *([] if out is None else [out]))


def steps(recorded, psf_taps, estimate):
    views = lax.axis_size("view")
    tiles = lax.axis_size("tile")
    nx, nz, ny = estimate.shape
    cores = 2
    chips = views // cores
    part = ny // chips
    width = min(ny, part + (LANES if chips <= 2 else 2 * LANES))
    split = Split(chips, cores, part, width, ny, nz // cores, tiles)
    assert 2 * RADIUS * ITERS <= LANES and nx >= 2 * RADIUS
    flat = lambda a: a.reshape(-1, a.shape[-1])

    def swap_core(values):
        pairs = [(v, v ^ 1) for v in range(views)]
        return lax.ppermute(values, "view", pairs)

    def to_chip(values, r):
        pairs = [(v, (v + r * cores) % views) for v in range(views)]
        return lax.ppermute(values, "view", pairs)

    slabs = lax.axis_size("slab")
    axes = ("slab", "tile", "view")

    def partner(s, t, pair_b):
        u = ((t + 1) ^ 1) - 1 if pair_b else t ^ 1
        return (s, u) if 0 <= u < tiles else (s ^ 1, t)

    def pairs_of(is_b):
        pairs = []
        for s in range(slabs):
            for t in range(tiles):
                for v in range(views):
                    to, u = partner(s, t, is_b(v))
                    if to < slabs:
                        here = (s * tiles + t) * views + v
                        pairs.append((here, (to * tiles + u) * views + v))
        return pairs

    def pair_up(a, b):
        b = lax.ppermute(b, axes, pairs_of(lambda v: True))
        a = lax.ppermute(a, axes, pairs_of(lambda v: False))
        return a, b

    def estimate_rims(values):
        mine = lax.ppermute(values, axes, pairs_of(lambda v: v % cores == 1))
        return mine, swap_core(mine)

    recorded = recorded[0]

    def to_a(n, by_core=False):
        return (nx - n, 0, n, by_core)

    def to_b(n):
        return (0, nx - n, n, False)

    rim, body = RADIUS * nz, (nx - 2 * RADIUS) * nz
    end = 2 * rim + body
    outs = [(0, r, (to_a(RADIUS), to_b(RADIUS))) for r in range(1, chips)]
    outs.append((1, 0, (to_a(2 * RADIUS, True),)))
    *cuts, est_rim = cut((recorded, estimate), split, outs)
    taps = [psf_taps] + [to_chip(psf_taps, r) for r in range(1, chips)]
    edges = [None] + [to_chip(cuts[r - 1], r) for r in range(1, chips)]

    outs = [(0, r, ((RADIUS, RADIUS, nx - 2 * RADIUS, False),)) for r in range(1, chips)]
    outs += [(0, 0, ((0, 0, nx, False),)), (0, 0, (to_a(RADIUS),)), (0, 0, (to_b(RADIUS),))]
    outs += [(1, 0, ((0, 0, nx, False),))]
    *cuts, own, own_a, own_b, est = cut((recorded, estimate), split, outs)
    middles = [None] + [to_chip(cuts[r - 1], r) for r in range(1, chips)]
    rims = estimate_rims(est_rim)
    own_a, own_b = pair_up(own_a, own_b)

    record = [tuple(flat(a) for a in (own_a, own_b, own))]
    before = Piece(0, rim, 0, 0, 1, 0, 0)
    after = Piece(rim + end, rim, 1, 0, 0, 0, 1)
    pieces = [(before, Piece(rim, end, 2, 0, 2, 0), after)]
    for r in range(1, chips):
        pair_a, pair_b = pair_up(edges[r][:RADIUS], edges[r][RADIUS:])
        record.append(tuple(flat(a) for a in (pair_a, pair_b, edges[r], middles[r])))
        first = Piece(rim, rim, 2, 0, 2, rim)
        inner = Piece(2 * rim, body, 3, 0, 3, 0)
        last = Piece(2 * rim + body, rim, 2, rim, 2, 0)
        pieces.append((before, first, inner, last, after))

    ops = []
    for k in taps:
        ops.append(operators(k, nz))

    for iteration in range(ITERS):
        final = iteration == ITERS - 1
        blurred = []
        for r in range(chips):
            blurred.append(own_share(est, ops[r]))
        for mine in (True, False):
            rim_planes = rims[0] if mine else rims[1]
            blurred = rim_share(split, mine, blurred, rim_planes, ops)
        plan = spans(nx, 2)
        handed = [None] * chips
        sums = []
        for span in plan:
            total = None
            for r in range(chips):
                ends = part if final and r == chips - 1 else None
                total, handed[r] = adjoint(
                    split,
                    blurred[r],
                    record[r],
                    pieces[r],
                    ops[r],
                    span,
                    total,
                    handed[r],
                    nz,
                    ends,
                )
            keep, send = total if final else (total, total)
            sums.append((keep, swap_core(send)))
        if not final:
            planes = [span.planes for span in plan]
            est, est_rim = update(split, views, planes, sum(sums, ()), est)
            rims = estimate_rims(est_rim)

    early, late = [], []
    for c, (span, pair) in enumerate(zip(plan, sums)):
        done = finish(split, views, span.planes, *pair, est)
        for r in range(chips):
            mine = to_chip(done, r) if r else done
            sibling = swap_core(mine)
            pieces = late if r and c == len(plan) - 1 else early
            pieces.append(((*span.planes, r, True), mine))
            pieces.append(((*span.planes, r, False), sibling))
    out = join(split, early, None, nx, nz)
    return join(split, late, out, nx, nz)


def solution(mesh):
    in_specs = (P("view", "tile", "slab", None), P("view", None, None), P("tile", "slab", None))
    out_specs = P("tile", "slab", None)
    return jax.shard_map(steps, mesh=mesh, in_specs=in_specs, out_specs=out_specs, check_vma=False)
```

```python
import functools
from typing import NamedTuple

import jax
import jax.numpy as jnp
from jax import lax
from jax.experimental import pallas as pl
from jax.experimental.pallas import tpu as pltpu
from jax.sharding import PartitionSpec as P


RADIUS = 7
ITERS = 2
TAPS = 2 * RADIUS + 1
LANES = 128
ROWS = 256
BF = jnp.bfloat16
F32 = jnp.float32
VMEM = pl.BlockSpec(memory_space=pltpu.VMEM)
SMEM = pl.BlockSpec(memory_space=pltpu.SMEM)
ANY = pl.BlockSpec(memory_space=pltpu.HBM)
PARAMS = pltpu.CompilerParams(vmem_limit_bytes=20 * 1024 * 1024)


def halves(value):
    high = value.astype(BF)
    return high, (value - high.astype(F32)).astype(BF)


def dot(a, b):
    return jnp.dot(a, b, preferred_element_type=F32)


class Split(NamedTuple):
    chips: int
    cores: int
    part: int
    width: int
    ny: int
    half: int
    tiles: int

    def start(self, chip):
        place = jnp.clip(chip * self.part - LANES, 0, self.ny - self.width)
        return pl.multiple_of(place, LANES)

    def here(self):
        place = lax.axis_index("view")
        return place // self.cores, lax.rem(place, self.cores)

    def inner(self, chip):
        return pl.multiple_of(chip * self.part - self.start(chip), LANES)

    def halo(self, chip):
        return pl.multiple_of(jnp.where(chip == 0, self.part, 0), LANES)

    def packs(self, planes, nz):
        padded = -(-planes * nz // LANES) * LANES
        one = self.chips == 2 and self.width == self.part + LANES
        return one and SLIVER // nz * padded <= self.part

    def rim(self, planes, nz):
        if self.packs(planes, nz):
            return (planes + 1, nz, self.part)
        return (planes, nz, self.width)

    def odd(self):
        return lax.rem(lax.axis_index("tile"), 2)

    def side(self, mine):
        _, core = self.here()
        own = 1 - lax.rem(self.odd() + core, 2)
        return own if mine else 1 - own

    def inside(self, side):
        tile = lax.axis_index("tile")
        return jnp.where(side == 0, tile > 0, tile < self.tiles - 1).astype(F32)

    def rows(self, core):
        return pl.ds(pl.multiple_of(core * self.half, self.half), self.half)


SLIVER = 32


def pack(split, chip, window, first, planes, out, to):
    nz = out.shape[1]
    at = pl.ds(first, planes)
    out[to : to + planes] = window[at, :, pl.ds(split.inner(chip), split.part)]
    rows = planes * nz
    padded = -(-rows // LANES) * LANES
    tile = window[at, :, pl.ds(split.halo(chip), LANES)].reshape(rows, LANES)
    if padded > rows:
        tile = jnp.concatenate([tile, jnp.zeros((padded - rows, LANES), F32)], 0)
    turned = tile.T
    kept = jnp.where(chip == 0, turned[:SLIVER], turned[LANES - SLIVER :])
    for g in range(SLIVER // nz):
        out[to + planes, :, g * padded : (g + 1) * padded] = kept[g * nz : (g + 1) * nz]
    rest = SLIVER // nz * padded
    if rest < split.part:
        out[to + planes, :, rest:] = jnp.zeros((nz, split.part - rest), F32)


def unpack(split, packed, first, planes, window, to):
    nz = packed.shape[1]
    chip, _ = split.here()
    rows = planes * nz
    padded = -(-rows // LANES) * LANES
    at = slice(to, to + rows)
    own = packed[first : first + planes].reshape(rows, split.part)
    window[at, pl.ds(split.inner(chip), split.part)] = own
    extra = first + planes
    kept = [packed[extra, :, g * padded : (g + 1) * padded] for g in range(SLIVER // nz)]
    none = jnp.ones((LANES - SLIVER, padded), F32)
    turned = jnp.where(
        chip == 0, jnp.concatenate([*kept, none], 0), jnp.concatenate([none, *kept], 0)
    )
    window[at, pl.ds(split.halo(chip), LANES)] = turned.T[:rows]


def unpack_kernel(split, packs, *refs):
    for packed, window, counts in zip(refs[: len(packs)], refs[len(packs) :], packs):
        first = to = 0
        for planes in counts:
            unpack(split, packed, first, planes, window, to)
            first, to = first + planes + 1, to + planes * packed.shape[1]


def unpacked(split, arrays, packs):
    nz = arrays[0].shape[1]
    if not split.packs(packs[0][0], nz):
        return tuple(a.reshape(-1, a.shape[-1]) for a in arrays)
    return pl.pallas_call(
        functools.partial(unpack_kernel, split, packs),
        out_shape=tuple(jax.ShapeDtypeStruct((sum(p) * nz, split.width), F32) for p in packs),
        in_specs=[VMEM] * len(arrays),
        out_specs=(VMEM,) * len(arrays),
        compiler_params=PARAMS,
        name="unpack",
    )(*arrays)


def cut_kernel(split, sources, moves, packed, *refs):
    outs, sem = list(refs[sources : len(refs) - 1 - len(packed)]), refs[-1]
    finals = [outs[k] for k, _, _ in packed]
    for (k, _, _), scratch in zip(packed, refs[len(refs) - 1 - len(packed) : -1]):
        outs[k] = scratch
    chip, _ = split.here()
    copies = []
    for source, ahead, out, at, even, odd, n, by_core in moves:
        lanes = pl.ds(split.start(lax.rem(chip + ahead, split.chips)), split.width)
        which = 1 - split.side(True) if by_core else split.odd()
        x0 = even if even == odd else jnp.where(which == 1, odd, even)
        copies.append(
            pltpu.make_async_copy(
                refs[source].at[pl.ds(x0, n), :, lanes],
                outs[out].at[pl.ds(at, n)],
                sem.at[len(copies)],
            )
        )
        copies[-1].start()
    for copy in copies:
        copy.wait()
    for (k, ahead, counts), final in zip(packed, finals):
        first = to = 0
        for planes in counts:
            pack(split, lax.rem(chip + ahead, split.chips), outs[k], first, planes, final, to)
            first, to = first + planes, to + planes + 1


def cut(sources, split, outs, whole):
    moves, shapes, scratch, packed = [], [], [], []
    for index, (source, ahead, ranges) in enumerate(outs):
        at = 0
        for even, odd, n, by_core in ranges:
            moves.append((source, ahead, index, at, even, odd, n, by_core))
            at += n
        nz = sources[source].shape[1]
        shape = (at, nz, split.width)
        counts = tuple(n for _, _, n, _ in ranges)
        if index not in whole and split.packs(max(counts), nz):
            scratch.append(pltpu.VMEM(shape, F32))
            packed.append((index, ahead, counts))
            shape = (at + len(counts), nz, split.part)
        shapes.append(jax.ShapeDtypeStruct(shape, F32))
    return pl.pallas_call(
        functools.partial(cut_kernel, split, len(sources), tuple(moves), tuple(packed)),
        out_shape=tuple(shapes),
        in_specs=[ANY] * len(sources),
        out_specs=(VMEM,) * len(shapes),
        scratch_shapes=[*scratch, pltpu.SemaphoreType.DMA((len(moves),))],
        compiler_params=PARAMS,
        name="cut",
    )(*[pltpu.with_memory_space_constraint(a, pltpu.HBM) for a in sources])


def update_kernel(split, views, planes, *refs):
    est, out, rim = refs[-3:]
    for c, (p0, p1) in enumerate(planes):
        total = refs[2 * c][...] + refs[2 * c + 1][...]
        out[p0:p1] = est[p0:p1] * jnp.exp(total / views)
    n = 2 * RADIUS
    first = split.side(True) * (out.shape[0] - n)
    if split.packs(n, out.shape[1]):
        pack(split, split.here()[0], out, first, n, rim, 0)
    else:
        rim[...] = out[pl.ds(first, n)]


def update(split, views, planes, sums, est):
    return pl.pallas_call(
        functools.partial(update_kernel, split, views, planes),
        out_shape=(
            jax.ShapeDtypeStruct(est.shape, F32),
            jax.ShapeDtypeStruct(split.rim(2 * RADIUS, est.shape[1]), F32),
        ),
        in_specs=[VMEM] * (len(sums) + 1),
        out_specs=(VMEM,) * 2,
        compiler_params=PARAMS,
        name="update",
    )(*sums, est)


def finish_kernel(split, views, planes, mine, sibling, est, out):
    chip, core = split.here()
    old = est[planes[0] : planes[1], split.rows(core), pl.ds(split.inner(chip), split.part)]
    out[...] = old * jnp.exp((mine[...] + sibling[...]) / views)


def finish(split, views, planes, mine, sibling, est):
    return pl.pallas_call(
        functools.partial(finish_kernel, split, views, planes),
        out_shape=jax.ShapeDtypeStruct(mine.shape, F32),
        in_specs=[VMEM] * 3,
        out_specs=VMEM,
        compiler_params=PARAMS,
        name="finish",
    )(mine, sibling, est)


GROUP = 8


def operators_kernel(nz, taps, t, last, w, wr, full):
    planes = ROWS // nz
    band = LANES + 3 * GROUP
    first = LANES - GROUP
    i = lax.broadcasted_iota(jnp.int32, (band, LANES), 0) + first
    o = lax.broadcasted_iota(jnp.int32, (band, LANES), 1)
    shift_y = i - o - (LANES - RADIUS)
    row = lax.broadcasted_iota(jnp.int32, (nz, 2 * ROWS), 0)
    col = lax.broadcasted_iota(jnp.int32, (nz, 2 * ROWS), 1)
    shift_x = col // nz
    shift_z = col % nz - row + RADIUS
    sums = []
    for d in range(3):
        value = taps[0, d, 0]
        for k in range(1, TAPS):
            value = value + taps[0, d, k]
        sums.append(value)
    full[...] = jnp.zeros_like(full)
    for mirrored in range(2):
        ty = jnp.zeros((band, LANES), F32)
        kx = jnp.zeros((nz, 2 * ROWS), F32)
        kz = jnp.zeros((nz, 2 * ROWS), F32)
        for k in range(TAPS):
            tap = TAPS - 1 - k if mirrored else k
            kx = jnp.where(shift_x == k, taps[0, 0, tap], kx)
            kz = jnp.where(shift_z == k, taps[0, 1, tap], kz)
            ty = jnp.where(shift_y == k, taps[0, 2, tap], ty)
        kx = kx / sums[0]
        kz = kz / sums[1]
        ty = ty / sums[2]
        for c0 in range(0, ROWS, LANES):
            full[first + c0 : first + c0 + band, c0 : c0 + LANES] = ty
        high, low = halves(full[LANES : LANES + ROWS, :])
        t[mirrored, :ROWS] = high
        t[mirrored, ROWS : 2 * ROWS] = high
        t[mirrored, 2 * ROWS : 3 * ROWS] = low
        right = full[LANES + ROWS : LANES + ROWS + GROUP, :]
        left = full[LANES - GROUP : LANES, :]
        right_high, left_high = right.astype(BF).astype(F32), left.astype(BF).astype(F32)
        none = jnp.zeros((2 * GROUP, ROWS), F32)
        corners = [
            right_high,
            none,
            left_high,
            right_high,
            none,
            left - left_high,
            right - right_high,
            none,
            none,
            none,
            left_high,
        ]
        t[mirrored, 3 * ROWS :] = jnp.concatenate(corners, 0).astype(BF)
        high, low = halves(full[:ROWS, :LANES])
        last[mirrored, :, :LANES] = high
        last[mirrored, :, LANES:] = low
        strip = kx * kz
        for p in range(planes):
            moved = pltpu.roll(strip, p * nz, 1) if p else strip
            rows = slice(p * nz, (p + 1) * nz)
            w[mirrored, 0, rows, :], w[mirrored, 1, rows, :] = halves(moved)
            if not mirrored:
                wr[0, 0, rows, :], wr[0, 1, rows, :] = halves(moved[:, :ROWS])
                back = (p - 2 * RADIUS) * nz % (2 * ROWS)
                moved = pltpu.roll(strip, back, 1)[:, :ROWS] if back else strip[:, :ROWS]
                wr[1, 0, rows, :], wr[1, 1, rows, :] = halves(moved)


class Operators(NamedTuple):
    t: jax.Array
    last: jax.Array
    w: jax.Array
    wr: jax.Array


def operators(taps, nz):
    out = pl.pallas_call(
        functools.partial(operators_kernel, nz),
        out_shape=(
            jax.ShapeDtypeStruct((2, 3 * ROWS + LANES, ROWS), BF),
            jax.ShapeDtypeStruct((2, ROWS, ROWS), BF),
            jax.ShapeDtypeStruct((2, 2, ROWS, 2 * ROWS), BF),
            jax.ShapeDtypeStruct((2, 2, ROWS, ROWS), BF),
        ),
        in_specs=[SMEM],
        out_specs=(VMEM,) * 4,
        scratch_shapes=[pltpu.VMEM((2 * ROWS, ROWS), F32)],
        compiler_params=PARAMS,
        name="operators",
    )(taps)
    return Operators(*out)


def blur_y(x, t, last, store):
    n, width = x.shape
    xh, xl = halves(x)
    lane = lax.broadcasted_iota(jnp.int32, (n, LANES), 1)
    for o0 in range(0, width, ROWS):
        size = min(ROWS, width - o0)
        if size == ROWS:
            end = o0 + ROWS
            at = slice(o0, end)
            corner = jnp.zeros((n, LANES), F32)
            if end < width:
                corner = jnp.where(lane < GROUP, x[:, end : end + LANES], corner)
            if o0:
                corner = jnp.where(lane >= LANES - GROUP, x[:, o0 - LANES : o0], corner)
            high = corner.astype(BF).astype(F32)
            low = pltpu.roll(corner - high, LANES // 4, 1)
            corner = (high + low + pltpu.roll(high, LANES // 2, 1)).astype(BF)
            out = dot(jnp.concatenate([xh[:, at], xl[:, at], xh[:, at], corner], 1), t[...])
        else:
            at = slice(o0 - LANES, o0 + LANES)
            both = dot(xh[:, at], last[...])
            out = both[:, :LANES] + (both[:, LANES:] + dot(xl[:, at], last[:, :LANES]))
        store(o0, size, out)


def product(w, dh, dl, rows, store):
    wh, wl = w
    width = dh.shape[1]
    for o0 in range(0, width, ROWS):
        size = min(ROWS, width - o0)
        at = slice(o0, o0 + size)
        if size == ROWS:
            out = dot(wh, dh[rows, at]) + (dot(wl, dh[rows, at]) + dot(wh, dl[rows, at]))
        else:
            both = dot(wh, jnp.concatenate([dh[rows, at], dl[rows, at]], 1))
            out = both[:, :size] + (both[:, size:] + dot(wl, dh[rows, at]))
        store(o0, size, out)


def blur_xz(dh, dl, w, nz, planes_out, store):
    step = ROWS // nz
    for p0 in range(0, planes_out, step):
        m = min(step, planes_out - p0) * nz
        k = min(2 * ROWS, (planes_out + 2 * RADIUS - p0) * nz)
        rows = slice(p0 * nz, p0 * nz + k)
        put = functools.partial(store, p0 * nz, m)
        product((w[0, :m, :k], w[1, :m, :k]), dh, dl, rows, put)


def to_halves(dh, dl, rows):
    def store(o0, size, value):
        h, l = halves(value)
        dh[rows, o0 : o0 + size] = h
        dl[rows, o0 : o0 + size] = l

    return store


def chunks(rows, step=128):
    return [(r, min(step, rows - r)) for r in range(0, rows, step)]


def own_kernel(est, t, last, w, wr, blurred, dh, dl):
    planes, nz, width = est.shape
    step = LANES // nz
    for p in range(0, planes, step):
        n = min(step, planes - p)
        x = est[p : p + n].reshape(n * nz, width)
        blur_y(x, t.at[0], last.at[0], to_halves(dh, dl, slice(p * nz, (p + n) * nz)))
    total = planes + 2 * RADIUS
    step = ROWS // nz
    for p0 in range(0, total, step):
        out = min(step, total - p0)
        first = max(0, p0 - 2 * RADIUS)
        stop = min(planes, p0 + out)
        k = (stop - first) * nz
        m = out * nz
        if p0 < 2 * RADIUS:
            assert p0 == 0
            block = wr[1, 0, :m, :k], wr[1, 1, :m, :k]
        else:
            first = p0 - 2 * RADIUS
            block = w[0, 0, :m, :k], w[0, 1, :m, :k]

        def store(o0, size, value):
            blurred[p0 * nz : p0 * nz + m, o0 : o0 + size] = value

        product(block, dh, dl, slice(first * nz, stop * nz), store)


def own_share(est, ops):
    planes, nz, width = est.shape
    half = pltpu.VMEM((planes * nz, width), BF)
    return pl.pallas_call(
        own_kernel,
        out_shape=jax.ShapeDtypeStruct(((planes + 2 * RADIUS) * nz, width), F32),
        in_specs=[VMEM] * 5,
        out_specs=VMEM,
        scratch_shapes=[half, half],
        compiler_params=PARAMS,
        name="own_share",
    )(est, *ops)


def rim_kernel(split, mine, views, rim, *refs):
    nz, width = rim.shape[1], split.width
    n = 2 * RADIUS * nz
    side = split.side(mine)
    if split.packs(2 * RADIUS, nz):
        *refs, window = refs
        unpack(split, rim, 0, 2 * RADIUS, window, 0)
        flat = window[...] * split.inside(side)
    else:
        flat = rim[...].reshape(n, width) * split.inside(side)
    befores, refs = refs[:views], refs[views:]
    ops, refs = refs[: 3 * views], refs[3 * views :]
    blurreds, halves_of = refs[:views], refs[views:]
    for r in range(views):
        t, last, wr = ops[3 * r : 3 * r + 3]
        dh, dl = halves_of[2 * r : 2 * r + 2]
        for r0, count in chunks(n, 112):
            rows = slice(r0, r0 + count)
            blur_y(flat[rows, :], t.at[0], last.at[0], to_halves(dh, dl, rows))
    for r in range(views):
        wr = ops[3 * r + 2]
        before, blurred = befores[r], blurreds[r]
        dh, dl = halves_of[2 * r : 2 * r + 2]
        rows = pl.ds(pl.multiple_of(side * (blurred.shape[0] - n), nz), n)

        def store(o0, size, value):
            blurred[rows, o0 : o0 + size] = before[rows, o0 : o0 + size] + value

        product((wr[side, 0, :n, :n], wr[side, 1, :n, :n]), dh, dl, slice(0, n), store)


def rim_share(split, mine, befores, rim, ops):
    rows, nz = 2 * RADIUS * rim.shape[1], rim.shape[1]
    half = pltpu.VMEM((rows, split.width), BF)
    window = [pltpu.VMEM((rows, split.width), F32)] if split.packs(2 * RADIUS, nz) else []
    views = len(befores)
    return list(
        pl.pallas_call(
            functools.partial(rim_kernel, split, mine, views),
            out_shape=tuple(jax.ShapeDtypeStruct(b.shape, F32) for b in befores),
            in_specs=[VMEM] * (1 + 4 * views),
            out_specs=(VMEM,) * views,
            scratch_shapes=[half] * (2 * views) + window,
            input_output_aliases={1 + r: r for r in range(views)},
            compiler_params=PARAMS,
            name="rim_share",
        )(rim, *befores, *[x for o in ops for x in (o.t, o.last, o.wr)])
    )


class Piece(NamedTuple):
    at: int
    rows: int
    odd: int
    odd_start: int
    even: int
    even_start: int
    outside: int | None = None

    def load(self, refs, odd, r0, n):
        if self.odd != self.even:
            a = refs[self.odd][self.odd_start + r0 : self.odd_start + r0 + n, :]
            b = refs[self.even][self.even_start + r0 : self.even_start + r0 + n, :]
            return jnp.where(odd == 1, a, b)
        start = self.even_start
        if self.odd_start != self.even_start:
            start = jnp.where(odd == 1, self.odd_start, self.even_start)
            start = pl.multiple_of(start, 8)
        return refs[self.odd][pl.ds(start + r0, n), :]


class Span(NamedTuple):
    planes: tuple
    blurred: tuple
    handed: bool
    hands_on: bool


def adjoint_kernel(nz, split, pieces, inputs, span, has_added, ends, *refs):
    refs = list(refs)
    take = lambda n: [refs.pop(0) for _ in range(n)]
    (blurred,), record, (t, last, w) = take(1), take(inputs), take(3)
    (added,) = take(1) if has_added else (None,)
    handed = take(2) if span.handed else None
    keep, send = take(2) if ends is not None else (None, None)
    (out,) = take(1) if ends is None else (None,)
    hands_on = take(2) if span.hands_on else None
    (out,) = take(1) if ends is not None else (out,)
    dh, dl = refs
    odd = split.odd()
    p0, p1 = span.planes
    base = p0 * nz
    q0, q1 = span.blurred[0] * nz, span.blurred[1] * nz
    if handed is not None:
        dh[: q0 - base, :] = handed[0][...]
        dl[: q0 - base, :] = handed[1][...]
    for piece in pieces:
        lo, hi = max(q0, piece.at), min(q1, piece.at + piece.rows)
        for r0, n in chunks(max(0, hi - lo)):
            at = lo + r0
            q = piece.load(record, odd, at - piece.at, n)
            if piece.outside is not None:
                q = q * split.inside(piece.outside)
            q = q / blurred[at : at + n, :]
            rows = slice(at - base, at - base + n)
            blur_y(q, t.at[1], last.at[1], to_halves(dh, dl, rows))
    if hands_on is not None:
        hands_on[0][...] = dh[(p1 - p0) * nz :, :]
        hands_on[1][...] = dl[(p1 - p0) * nz :, :]

    def store(r0, m, o0, size, value):
        log = jnp.log(value)
        planes = slice(r0 // nz, (r0 + m) // nz)
        log = log.reshape(m // nz, nz, size)
        if has_added:
            log = log + added[planes, :, o0 : o0 + size]
        out[planes, :, o0 : o0 + size] = log

    blur_xz(dh, dl, w.at[1], nz, p1 - p0, store)
    if ends is not None:
        chip, core = split.here()
        lanes = slice(None) if ends == split.width else pl.ds(split.inner(chip), ends)
        keep[...] = out[:, split.rows(core), lanes]
        send[...] = out[:, split.rows(1 - core), lanes]


def adjoint(split, blurred, record, pieces, ops, span, added, handed, nz, ends=None):
    width = blurred.shape[1]
    planes = span.planes[1] - span.planes[0]
    args = [blurred, *record, *ops[:3]] + ([] if added is None else [added])
    args += [] if handed is None else list(handed)
    rows = (planes + 2 * RADIUS) * nz
    full = (planes, nz, width)
    shapes = [jax.ShapeDtypeStruct(full, F32)]
    scratch = [pltpu.VMEM((rows, width), BF), pltpu.VMEM((rows, width), BF)]
    if ends is not None:
        shapes = [jax.ShapeDtypeStruct((planes, split.half, ends), F32)] * 2
        scratch = [pltpu.VMEM(full, F32)] + scratch
    if span.hands_on:
        shapes += [jax.ShapeDtypeStruct((2 * RADIUS * nz, width), BF)] * 2
    kernel = functools.partial(
        adjoint_kernel, nz, split, pieces, len(record), span, added is not None, ends
    )
    out = pl.pallas_call(
        kernel,
        out_shape=tuple(shapes),
        in_specs=[VMEM] * len(args),
        out_specs=(VMEM,) * len(shapes),
        scratch_shapes=scratch,
        compiler_params=PARAMS,
        name="adjoint",
    )(*args)
    total = out[0] if ends is None else out[:2]
    return total, (out[-2:] if span.hands_on else None)


def spans(nx, count):
    out, done = [], 0
    for c in range(count):
        p0, p1 = c * nx // count, (c + 1) * nx // count
        q1 = p1 + 2 * RADIUS
        out.append(Span((p0, p1), (done, q1), c > 0, c < count - 1))
        done = q1
    return out


def join_kernel(split, places, *refs):
    parts, out, sem = refs[: len(places)], refs[-2], refs[-1]
    chip, core = split.here()
    copies = []
    for part, (p0, p1, r, mine) in zip(parts, places):
        owner = lax.rem(chip + split.chips - r, split.chips)
        lanes = pl.ds(pl.multiple_of(owner * split.part, LANES), split.part)
        to = out.at[p0:p1, split.rows(core if mine else 1 - core), lanes]
        copies.append(pltpu.make_async_copy(part, to, sem.at[len(copies)]))
        copies[-1].start()
    for copy in copies:
        copy.wait()


def join(split, pieces, out, nx, nz):
    places, parts = zip(*pieces)
    return pl.pallas_call(
        functools.partial(join_kernel, split, places),
        out_shape=jax.ShapeDtypeStruct((nx, nz, split.ny), F32),
        in_specs=[VMEM] * len(parts) + ([] if out is None else [ANY]),
        out_specs=ANY,
        scratch_shapes=[pltpu.SemaphoreType.DMA((len(parts),))],
        input_output_aliases={} if out is None else {len(parts): 0},
        compiler_params=PARAMS,
        name="join",
    )(*parts, *([] if out is None else [out]))


def steps(recorded, psf_taps, estimate):
    views = lax.axis_size("view")
    tiles = lax.axis_size("tile")
    nx, nz, ny = estimate.shape
    cores = 2
    chips = views // cores
    part = ny // chips
    width = min(ny, part + (LANES if chips <= 2 else 2 * LANES))
    split = Split(chips, cores, part, width, ny, nz // cores, tiles)
    assert 2 * RADIUS * ITERS <= SLIVER and nx >= 2 * RADIUS
    flat = lambda a: a.reshape(-1, a.shape[-1])

    def swap_core(values):
        pairs = [(v, v ^ 1) for v in range(views)]
        return lax.ppermute(values, "view", pairs)

    def to_chip(values, r):
        pairs = [(v, (v + r * cores) % views) for v in range(views)]
        return lax.ppermute(values, "view", pairs)

    slabs = lax.axis_size("slab")
    axes = ("slab", "tile", "view")

    def partner(s, t, pair_b):
        u = ((t + 1) ^ 1) - 1 if pair_b else t ^ 1
        return (s, u) if 0 <= u < tiles else (s ^ 1, t)

    def pairs_of(is_b):
        pairs = []
        for s in range(slabs):
            for t in range(tiles):
                for v in range(views):
                    to, u = partner(s, t, is_b(v))
                    if to < slabs:
                        here = (s * tiles + t) * views + v
                        pairs.append((here, (to * tiles + u) * views + v))
        return pairs

    def pair_up(a, b):
        b = lax.ppermute(b, axes, pairs_of(lambda v: True))
        a = lax.ppermute(a, axes, pairs_of(lambda v: False))
        return a, b

    def estimate_rims(values):
        mine = lax.ppermute(values, axes, pairs_of(lambda v: v % cores == 1))
        return mine, swap_core(mine)

    recorded = recorded[0]

    def to_a(n, by_core=False):
        return (nx - n, 0, n, by_core)

    def to_b(n):
        return (0, nx - n, n, False)

    rim, body = RADIUS * nz, (nx - 2 * RADIUS) * nz
    end = 2 * rim + body
    outs = [(0, r, (to_a(RADIUS), to_b(RADIUS))) for r in range(1, chips)]
    outs.append((1, 0, (to_a(2 * RADIUS, True),)))
    *cuts, est_rim = cut((recorded, estimate), split, outs, ())
    taps = [psf_taps] + [to_chip(psf_taps, r) for r in range(1, chips)]
    edges = [None] + [to_chip(cuts[r - 1], r) for r in range(1, chips)]

    outs = [(0, r, ((RADIUS, RADIUS, nx - 2 * RADIUS, False),)) for r in range(1, chips)]
    outs += [(0, 0, ((0, 0, nx, False),)), (0, 0, (to_a(RADIUS),)), (0, 0, (to_b(RADIUS),))]
    outs += [(1, 0, ((0, 0, nx, False),))]
    whole = (chips - 1, chips + 2)
    *cuts, own, own_a, own_b, est = cut((recorded, estimate), split, outs, whole)
    middles = [None] + [to_chip(cuts[r - 1], r) for r in range(1, chips)]
    rims = estimate_rims(est_rim)
    own_a, own_b = pair_up(own_a, own_b)

    own_a, own_b = unpacked(split, (own_a, own_b), ((RADIUS,), (RADIUS,)))
    record = [(own_a, own_b, flat(own))]
    before = Piece(0, rim, 0, 0, 1, 0, 0)
    after = Piece(rim + end, rim, 1, 0, 0, 0, 1)
    pieces = [(before, Piece(rim, end, 2, 0, 2, 0), after)]
    for r in range(1, chips):
        one = edges[r].shape[0] // 2
        pair_a, pair_b = pair_up(edges[r][:one], edges[r][one:])
        arrays = (pair_a, pair_b, edges[r], middles[r])
        packs = ((RADIUS,), (RADIUS,), (RADIUS, RADIUS), (nx - 2 * RADIUS,))
        record.append(unpacked(split, arrays, packs))
        first = Piece(rim, rim, 2, 0, 2, rim)
        inner = Piece(2 * rim, body, 3, 0, 3, 0)
        last = Piece(2 * rim + body, rim, 2, rim, 2, 0)
        pieces.append((before, first, inner, last, after))

    ops = []
    for k in taps:
        ops.append(operators(k, nz))

    for iteration in range(ITERS):
        final = iteration == ITERS - 1
        blurred = []
        for r in range(chips):
            blurred.append(own_share(est, ops[r]))
        for mine in (True, False):
            rim_planes = rims[0] if mine else rims[1]
            blurred = rim_share(split, mine, blurred, rim_planes, ops)
        plan = spans(nx, 2)
        handed = [None] * chips
        sums = []
        for span in plan:
            total = None
            for r in range(chips):
                ends = part if final and r == chips - 1 else None
                total, handed[r] = adjoint(
                    split,
                    blurred[r],
                    record[r],
                    pieces[r],
                    ops[r],
                    span,
                    total,
                    handed[r],
                    nz,
                    ends,
                )
            keep, send = total if final else (total, total)
            sums.append((keep, swap_core(send)))
        if not final:
            planes = [span.planes for span in plan]
            est, est_rim = update(split, views, planes, sum(sums, ()), est)
            rims = estimate_rims(est_rim)

    early, late = [], []
    for c, (span, pair) in enumerate(zip(plan, sums)):
        done = finish(split, views, span.planes, *pair, est)
        for r in range(chips):
            mine = to_chip(done, r) if r else done
            sibling = swap_core(mine)
            pieces = late if r and c == len(plan) - 1 else early
            pieces.append(((*span.planes, r, True), mine))
            pieces.append(((*span.planes, r, False), sibling))
    out = join(split, early, None, nx, nz)
    return join(split, late, out, nx, nz)


def solution(mesh):
    in_specs = (P("view", "tile", "slab", None), P("view", None, None), P("tile", "slab", None))
    out_specs = P("tile", "slab", None)
    return jax.shard_map(steps, mesh=mesh, in_specs=in_specs, out_specs=out_specs, check_vma=False)
```

```python
import functools
from typing import NamedTuple

import jax
import jax.numpy as jnp
from jax import lax
from jax.experimental import pallas as pl
from jax.experimental.pallas import tpu as pltpu
from jax.sharding import PartitionSpec as P


RADIUS = 7
ITERS = 2
TAPS = 2 * RADIUS + 1
LANES = 128
ROWS = 256
BF = jnp.bfloat16
F32 = jnp.float32
VMEM = pl.BlockSpec(memory_space=pltpu.VMEM)
SMEM = pl.BlockSpec(memory_space=pltpu.SMEM)
ANY = pl.BlockSpec(memory_space=pltpu.HBM)
PARAMS = pltpu.CompilerParams(vmem_limit_bytes=20 * 1024 * 1024)


def halves(value):
    high = value.astype(BF)
    return high, (value - high.astype(F32)).astype(BF)


def dot(a, b):
    return jnp.dot(a, b, preferred_element_type=F32)


class Split(NamedTuple):
    chips: int
    cores: int
    part: int
    width: int
    ny: int
    half: int
    tiles: int

    def start(self, chip):
        place = jnp.clip(chip * self.part - LANES, 0, self.ny - self.width)
        return pl.multiple_of(place, LANES)

    def here(self):
        place = lax.axis_index("view")
        return place // self.cores, lax.rem(place, self.cores)

    def inner(self, chip):
        return pl.multiple_of(chip * self.part - self.start(chip), LANES)

    def halo(self, chip):
        return pl.multiple_of(jnp.where(chip == 0, self.part, 0), LANES)

    def packs(self, planes, nz):
        padded = -(-planes * nz // LANES) * LANES
        one = self.chips == 2 and self.width == self.part + LANES
        return one and SLIVER // nz * padded <= self.part

    def rim(self, planes, nz):
        if self.packs(planes, nz):
            return (planes + 1, nz, self.part)
        return (planes, nz, self.width)

    def odd(self):
        return lax.rem(lax.axis_index("tile"), 2)

    def side(self, mine):
        _, core = self.here()
        own = 1 - lax.rem(self.odd() + core, 2)
        return own if mine else 1 - own

    def inside(self, side):
        tile = lax.axis_index("tile")
        return jnp.where(side == 0, tile > 0, tile < self.tiles - 1).astype(F32)

    def rows(self, core):
        return pl.ds(pl.multiple_of(core * self.half, self.half), self.half)


SLIVER = 32


def pack(split, chip, window, first, planes, out, to):
    nz = out.shape[1]
    at = pl.ds(first, planes)
    out[to : to + planes] = window[at, :, pl.ds(split.inner(chip), split.part)]
    rows = planes * nz
    padded = -(-rows // LANES) * LANES
    tile = window[at, :, pl.ds(split.halo(chip), LANES)].reshape(rows, LANES)
    if padded > rows:
        tile = jnp.concatenate([tile, jnp.zeros((padded - rows, LANES), F32)], 0)
    turned = tile.T
    kept = jnp.where(chip == 0, turned[:SLIVER], turned[LANES - SLIVER :])
    for g in range(SLIVER // nz):
        out[to + planes, :, g * padded : (g + 1) * padded] = kept[g * nz : (g + 1) * nz]
    rest = SLIVER // nz * padded
    if rest < split.part:
        out[to + planes, :, rest:] = jnp.zeros((nz, split.part - rest), F32)


def unpack(split, packed, first, planes, window, to):
    nz = packed.shape[1]
    chip, _ = split.here()
    rows = planes * nz
    padded = -(-rows // LANES) * LANES
    at = slice(to, to + rows)
    own = packed[first : first + planes].reshape(rows, split.part)
    window[at, pl.ds(split.inner(chip), split.part)] = own
    extra = first + planes
    kept = [packed[extra, :, g * padded : (g + 1) * padded] for g in range(SLIVER // nz)]
    none = jnp.ones((LANES - SLIVER, padded), F32)
    turned = jnp.where(
        chip == 0, jnp.concatenate([*kept, none], 0), jnp.concatenate([none, *kept], 0)
    )
    window[at, pl.ds(split.halo(chip), LANES)] = turned.T[:rows]


def unpack_kernel(split, packs, *refs):
    for packed, window, counts in zip(refs[: len(packs)], refs[len(packs) :], packs):
        first = to = 0
        for planes in counts:
            unpack(split, packed, first, planes, window, to)
            first, to = first + planes + 1, to + planes * packed.shape[1]


def unpacked(split, arrays, packs):
    nz = arrays[0].shape[1]
    if not split.packs(packs[0][0], nz):
        return tuple(a.reshape(-1, a.shape[-1]) for a in arrays)
    return pl.pallas_call(
        functools.partial(unpack_kernel, split, packs),
        out_shape=tuple(jax.ShapeDtypeStruct((sum(p) * nz, split.width), F32) for p in packs),
        in_specs=[VMEM] * len(arrays),
        out_specs=(VMEM,) * len(arrays),
        compiler_params=PARAMS,
        name="unpack",
    )(*arrays)


def cut_kernel(split, sources, moves, packed, *refs):
    outs, sem = list(refs[sources : len(refs) - 1 - len(packed)]), refs[-1]
    finals = [outs[k] for k, _, _ in packed]
    for (k, _, _), scratch in zip(packed, refs[len(refs) - 1 - len(packed) : -1]):
        outs[k] = scratch
    chip, _ = split.here()
    copies = []
    for source, ahead, out, at, even, odd, n, by_core in moves:
        lanes = pl.ds(split.start(lax.rem(chip + ahead, split.chips)), split.width)
        which = 1 - split.side(True) if by_core else split.odd()
        x0 = even if even == odd else jnp.where(which == 1, odd, even)
        copies.append(
            pltpu.make_async_copy(
                refs[source].at[pl.ds(x0, n), :, lanes],
                outs[out].at[pl.ds(at, n)],
                sem.at[len(copies)],
            )
        )
        copies[-1].start()
    for copy in copies:
        copy.wait()
    for (k, ahead, counts), final in zip(packed, finals):
        first = to = 0
        for planes in counts:
            pack(split, lax.rem(chip + ahead, split.chips), outs[k], first, planes, final, to)
            first, to = first + planes, to + planes + 1


def cut(sources, split, outs, whole):
    moves, shapes, scratch, packed = [], [], [], []
    for index, (source, ahead, ranges) in enumerate(outs):
        at = 0
        for even, odd, n, by_core in ranges:
            moves.append((source, ahead, index, at, even, odd, n, by_core))
            at += n
        nz = sources[source].shape[1]
        shape = (at, nz, split.width)
        counts = tuple(n for _, _, n, _ in ranges)
        if index not in whole and split.packs(max(counts), nz):
            scratch.append(pltpu.VMEM(shape, F32))
            packed.append((index, ahead, counts))
            shape = (at + len(counts), nz, split.part)
        shapes.append(jax.ShapeDtypeStruct(shape, F32))
    return pl.pallas_call(
        functools.partial(cut_kernel, split, len(sources), tuple(moves), tuple(packed)),
        out_shape=tuple(shapes),
        in_specs=[ANY] * len(sources),
        out_specs=(VMEM,) * len(shapes),
        scratch_shapes=[*scratch, pltpu.SemaphoreType.DMA((len(moves),))],
        compiler_params=PARAMS,
        name="cut",
    )(*[pltpu.with_memory_space_constraint(a, pltpu.HBM) for a in sources])


def update_kernel(split, views, planes, *refs):
    est, out, rim = refs[-3:]
    for c, (p0, p1) in enumerate(planes):
        total = refs[2 * c][...] + refs[2 * c + 1][...]
        out[p0:p1] = est[p0:p1] * jnp.exp(total / views)
    n = 2 * RADIUS
    first = split.side(True) * (out.shape[0] - n)
    if split.packs(n, out.shape[1]):
        pack(split, split.here()[0], out, first, n, rim, 0)
    else:
        rim[...] = out[pl.ds(first, n)]


def update(split, views, planes, sums, est):
    return pl.pallas_call(
        functools.partial(update_kernel, split, views, planes),
        out_shape=(
            jax.ShapeDtypeStruct(est.shape, F32),
            jax.ShapeDtypeStruct(split.rim(2 * RADIUS, est.shape[1]), F32),
        ),
        in_specs=[VMEM] * (len(sums) + 1),
        out_specs=(VMEM,) * 2,
        compiler_params=PARAMS,
        name="update",
    )(*sums, est)


def finish_kernel(split, views, planes, mine, sibling, est, out):
    chip, core = split.here()
    old = est[planes[0] : planes[1], split.rows(core), pl.ds(split.inner(chip), split.part)]
    out[...] = old * jnp.exp((mine[...] + sibling[...]) / views)


def finish(split, views, planes, mine, sibling, est):
    return pl.pallas_call(
        functools.partial(finish_kernel, split, views, planes),
        out_shape=jax.ShapeDtypeStruct(mine.shape, F32),
        in_specs=[VMEM] * 3,
        out_specs=VMEM,
        compiler_params=PARAMS,
        name="finish",
    )(mine, sibling, est)


GROUP = 8


def operators_kernel(nz, taps, t, last, w, wr, full):
    planes = ROWS // nz
    band = LANES + 3 * GROUP
    first = LANES - GROUP
    i = lax.broadcasted_iota(jnp.int32, (band, LANES), 0) + first
    o = lax.broadcasted_iota(jnp.int32, (band, LANES), 1)
    shift_y = i - o - (LANES - RADIUS)
    row = lax.broadcasted_iota(jnp.int32, (nz, 2 * ROWS), 0)
    col = lax.broadcasted_iota(jnp.int32, (nz, 2 * ROWS), 1)
    shift_x = col // nz
    shift_z = col % nz - row + RADIUS
    sums = []
    for d in range(3):
        value = taps[0, d, 0]
        for k in range(1, TAPS):
            value = value + taps[0, d, k]
        sums.append(value)
    full[...] = jnp.zeros_like(full)
    for mirrored in range(2):
        ty = jnp.zeros((band, LANES), F32)
        kx = jnp.zeros((nz, 2 * ROWS), F32)
        kz = jnp.zeros((nz, 2 * ROWS), F32)
        for k in range(TAPS):
            tap = TAPS - 1 - k if mirrored else k
            kx = jnp.where(shift_x == k, taps[0, 0, tap], kx)
            kz = jnp.where(shift_z == k, taps[0, 1, tap], kz)
            ty = jnp.where(shift_y == k, taps[0, 2, tap], ty)
        kx = kx / sums[0]
        kz = kz / sums[1]
        ty = ty / sums[2]
        for c0 in range(0, ROWS, LANES):
            full[first + c0 : first + c0 + band, c0 : c0 + LANES] = ty
        high, low = halves(full[LANES : LANES + ROWS, :])
        t[mirrored, :ROWS] = high
        t[mirrored, ROWS : 2 * ROWS] = high
        t[mirrored, 2 * ROWS : 3 * ROWS] = low
        right = full[LANES + ROWS : LANES + ROWS + GROUP, :]
        left = full[LANES - GROUP : LANES, :]
        right_high, left_high = right.astype(BF).astype(F32), left.astype(BF).astype(F32)
        none = jnp.zeros((2 * GROUP, ROWS), F32)
        corners = [
            right_high,
            none,
            left_high,
            right_high,
            none,
            left - left_high,
            right - right_high,
            none,
            none,
            none,
            left_high,
        ]
        t[mirrored, 3 * ROWS :] = jnp.concatenate(corners, 0).astype(BF)
        high, low = halves(full[:ROWS, :LANES])
        last[mirrored, :, :LANES] = high
        last[mirrored, :, LANES:] = low
        strip = kx * kz
        for p in range(planes):
            moved = pltpu.roll(strip, p * nz, 1) if p else strip
            rows = slice(p * nz, (p + 1) * nz)
            w[mirrored, 0, rows, :], w[mirrored, 1, rows, :] = halves(moved)
            if not mirrored:
                wr[0, 0, rows, :], wr[0, 1, rows, :] = halves(moved[:, :ROWS])
                back = (p - 2 * RADIUS) * nz % (2 * ROWS)
                moved = pltpu.roll(strip, back, 1)[:, :ROWS] if back else strip[:, :ROWS]
                wr[1, 0, rows, :], wr[1, 1, rows, :] = halves(moved)


class Operators(NamedTuple):
    t: jax.Array
    last: jax.Array
    w: jax.Array
    wr: jax.Array


def operators(taps, nz):
    out = pl.pallas_call(
        functools.partial(operators_kernel, nz),
        out_shape=(
            jax.ShapeDtypeStruct((2, 3 * ROWS + LANES, ROWS), BF),
            jax.ShapeDtypeStruct((2, ROWS, ROWS), BF),
            jax.ShapeDtypeStruct((2, 2, ROWS, 2 * ROWS), BF),
            jax.ShapeDtypeStruct((2, 2, ROWS, ROWS), BF),
        ),
        in_specs=[SMEM],
        out_specs=(VMEM,) * 4,
        scratch_shapes=[pltpu.VMEM((2 * ROWS, ROWS), F32)],
        compiler_params=PARAMS,
        name="operators",
    )(taps)
    return Operators(*out)


def blur_y(x, t, last, store):
    n, width = x.shape
    xh, xl = halves(x)
    lane = lax.broadcasted_iota(jnp.int32, (n, LANES), 1)
    for o0 in range(0, width, ROWS):
        size = min(ROWS, width - o0)
        if size == ROWS:
            end = o0 + ROWS
            at = slice(o0, end)
            corner = jnp.zeros((n, LANES), F32)
            if end < width:
                corner = jnp.where(lane < GROUP, x[:, end : end + LANES], corner)
            if o0:
                corner = jnp.where(lane >= LANES - GROUP, x[:, o0 - LANES : o0], corner)
            high = corner.astype(BF).astype(F32)
            low = pltpu.roll(corner - high, LANES // 4, 1)
            corner = (high + low + pltpu.roll(high, LANES // 2, 1)).astype(BF)
            out = dot(jnp.concatenate([xh[:, at], xl[:, at], xh[:, at], corner], 1), t[...])
        else:
            at = slice(o0 - LANES, o0 + LANES)
            both = dot(xh[:, at], last[...])
            out = both[:, :LANES] + (both[:, LANES:] + dot(xl[:, at], last[:, :LANES]))
        store(o0, size, out)


def product(w, dh, dl, rows, store):
    wh, wl = w
    width = dh.shape[1]
    for o0 in range(0, width, ROWS):
        size = min(ROWS, width - o0)
        at = slice(o0, o0 + size)
        if size == ROWS:
            out = dot(wh, dh[rows, at]) + (dot(wl, dh[rows, at]) + dot(wh, dl[rows, at]))
        else:
            both = dot(wh, jnp.concatenate([dh[rows, at], dl[rows, at]], 1))
            out = both[:, :size] + (both[:, size:] + dot(wl, dh[rows, at]))
        store(o0, size, out)


def blur_xz(dh, dl, w, nz, planes_out, store):
    step = ROWS // nz
    for p0 in range(0, planes_out, step):
        m = min(step, planes_out - p0) * nz
        k = min(2 * ROWS, (planes_out + 2 * RADIUS - p0) * nz)
        rows = slice(p0 * nz, p0 * nz + k)
        put = functools.partial(store, p0 * nz, m)
        product((w[0, :m, :k], w[1, :m, :k]), dh, dl, rows, put)


def to_halves(dh, dl, rows):
    def store(o0, size, value):
        h, l = halves(value)
        dh[rows, o0 : o0 + size] = h
        dl[rows, o0 : o0 + size] = l

    return store


def chunks(rows, step=256):
    return [(r, min(step, rows - r)) for r in range(0, rows, step)]


def own_kernel(est, t, last, w, wr, blurred, dh, dl):
    planes, nz, width = est.shape
    step = LANES // nz
    for p in range(0, planes, step):
        n = min(step, planes - p)
        x = est[p : p + n].reshape(n * nz, width)
        blur_y(x, t.at[0], last.at[0], to_halves(dh, dl, slice(p * nz, (p + n) * nz)))
    total = planes + 2 * RADIUS
    step = ROWS // nz
    for p0 in range(0, total, step):
        out = min(step, total - p0)
        first = max(0, p0 - 2 * RADIUS)
        stop = min(planes, p0 + out)
        k = (stop - first) * nz
        m = out * nz
        if p0 < 2 * RADIUS:
            assert p0 == 0
            block = wr[1, 0, :m, :k], wr[1, 1, :m, :k]
        else:
            first = p0 - 2 * RADIUS
            block = w[0, 0, :m, :k], w[0, 1, :m, :k]

        def store(o0, size, value):
            blurred[p0 * nz : p0 * nz + m, o0 : o0 + size] = value

        product(block, dh, dl, slice(first * nz, stop * nz), store)


def own_share(est, ops):
    planes, nz, width = est.shape
    half = pltpu.VMEM((planes * nz, width), BF)
    return pl.pallas_call(
        own_kernel,
        out_shape=jax.ShapeDtypeStruct(((planes + 2 * RADIUS) * nz, width), F32),
        in_specs=[VMEM] * 5,
        out_specs=VMEM,
        scratch_shapes=[half, half],
        compiler_params=PARAMS,
        name="own_share",
    )(est, *ops)


def rim_kernel(split, mine, views, rim, *refs):
    nz, width = rim.shape[1], split.width
    n = 2 * RADIUS * nz
    side = split.side(mine)
    if split.packs(2 * RADIUS, nz):
        *refs, window = refs
        unpack(split, rim, 0, 2 * RADIUS, window, 0)
        flat = window[...] * split.inside(side)
    else:
        flat = rim[...].reshape(n, width) * split.inside(side)
    befores, refs = refs[:views], refs[views:]
    ops, refs = refs[: 3 * views], refs[3 * views :]
    blurreds, halves_of = refs[:views], refs[views:]
    for r in range(views):
        t, last, wr = ops[3 * r : 3 * r + 3]
        dh, dl = halves_of[2 * r : 2 * r + 2]
        for r0, count in chunks(n, 112):
            rows = slice(r0, r0 + count)
            blur_y(flat[rows, :], t.at[0], last.at[0], to_halves(dh, dl, rows))
    for r in range(views):
        wr = ops[3 * r + 2]
        before, blurred = befores[r], blurreds[r]
        dh, dl = halves_of[2 * r : 2 * r + 2]
        rows = pl.ds(pl.multiple_of(side * (blurred.shape[0] - n), nz), n)

        def store(o0, size, value):
            blurred[rows, o0 : o0 + size] = before[rows, o0 : o0 + size] + value

        product((wr[side, 0, :n, :n], wr[side, 1, :n, :n]), dh, dl, slice(0, n), store)


def rim_share(split, mine, befores, rim, ops):
    rows, nz = 2 * RADIUS * rim.shape[1], rim.shape[1]
    half = pltpu.VMEM((rows, split.width), BF)
    window = [pltpu.VMEM((rows, split.width), F32)] if split.packs(2 * RADIUS, nz) else []
    views = len(befores)
    return list(
        pl.pallas_call(
            functools.partial(rim_kernel, split, mine, views),
            out_shape=tuple(jax.ShapeDtypeStruct(b.shape, F32) for b in befores),
            in_specs=[VMEM] * (1 + 4 * views),
            out_specs=(VMEM,) * views,
            scratch_shapes=[half] * (2 * views) + window,
            input_output_aliases={1 + r: r for r in range(views)},
            compiler_params=PARAMS,
            name="rim_share",
        )(rim, *befores, *[x for o in ops for x in (o.t, o.last, o.wr)])
    )


class Piece(NamedTuple):
    at: int
    rows: int
    odd: int
    odd_start: int
    even: int
    even_start: int
    outside: int | None = None

    def load(self, refs, odd, r0, n):
        if self.odd != self.even:
            a = refs[self.odd][self.odd_start + r0 : self.odd_start + r0 + n, :]
            b = refs[self.even][self.even_start + r0 : self.even_start + r0 + n, :]
            return jnp.where(odd == 1, a, b)
        start = self.even_start
        if self.odd_start != self.even_start:
            start = jnp.where(odd == 1, self.odd_start, self.even_start)
            start = pl.multiple_of(start, 8)
        return refs[self.odd][pl.ds(start + r0, n), :]


class Span(NamedTuple):
    planes: tuple
    blurred: tuple
    handed: bool
    hands_on: bool


def adjoint_kernel(nz, split, pieces, inputs, span, has_added, ends, *refs):
    refs = list(refs)
    take = lambda n: [refs.pop(0) for _ in range(n)]
    (blurred,), record, (t, last, w) = take(1), take(inputs), take(3)
    (added,) = take(1) if has_added else (None,)
    handed = take(2) if span.handed else None
    keep, send = take(2) if ends is not None else (None, None)
    (out,) = take(1) if ends is None else (None,)
    hands_on = take(2) if span.hands_on else None
    (out,) = take(1) if ends is not None else (out,)
    dh, dl = refs
    odd = split.odd()
    p0, p1 = span.planes
    base = p0 * nz
    q0, q1 = span.blurred[0] * nz, span.blurred[1] * nz
    if handed is not None:
        dh[: q0 - base, :] = handed[0][...]
        dl[: q0 - base, :] = handed[1][...]
    for piece in pieces:
        lo, hi = max(q0, piece.at), min(q1, piece.at + piece.rows)
        for r0, n in chunks(max(0, hi - lo)):
            at = lo + r0
            q = piece.load(record, odd, at - piece.at, n)
            if piece.outside is not None:
                q = q * split.inside(piece.outside)
            q = q / blurred[at : at + n, :]
            rows = slice(at - base, at - base + n)
            blur_y(q, t.at[1], last.at[1], to_halves(dh, dl, rows))
    if hands_on is not None:
        hands_on[0][...] = dh[(p1 - p0) * nz :, :]
        hands_on[1][...] = dl[(p1 - p0) * nz :, :]

    def store(r0, m, o0, size, value):
        log = jnp.log(value)
        planes = slice(r0 // nz, (r0 + m) // nz)
        log = log.reshape(m // nz, nz, size)
        if has_added:
            log = log + added[planes, :, o0 : o0 + size]
        out[planes, :, o0 : o0 + size] = log

    blur_xz(dh, dl, w.at[1], nz, p1 - p0, store)
    if ends is not None:
        chip, core = split.here()
        lanes = slice(None) if ends == split.width else pl.ds(split.inner(chip), ends)
        keep[...] = out[:, split.rows(core), lanes]
        send[...] = out[:, split.rows(1 - core), lanes]


def adjoint(split, blurred, record, pieces, ops, span, added, handed, nz, ends=None):
    width = blurred.shape[1]
    planes = span.planes[1] - span.planes[0]
    args = [blurred, *record, *ops[:3]] + ([] if added is None else [added])
    args += [] if handed is None else list(handed)
    rows = (planes + 2 * RADIUS) * nz
    full = (planes, nz, width)
    shapes = [jax.ShapeDtypeStruct(full, F32)]
    scratch = [pltpu.VMEM((rows, width), BF), pltpu.VMEM((rows, width), BF)]
    if ends is not None:
        shapes = [jax.ShapeDtypeStruct((planes, split.half, ends), F32)] * 2
        scratch = [pltpu.VMEM(full, F32)] + scratch
    if span.hands_on:
        shapes += [jax.ShapeDtypeStruct((2 * RADIUS * nz, width), BF)] * 2
    kernel = functools.partial(
        adjoint_kernel, nz, split, pieces, len(record), span, added is not None, ends
    )
    out = pl.pallas_call(
        kernel,
        out_shape=tuple(shapes),
        in_specs=[VMEM] * len(args),
        out_specs=(VMEM,) * len(shapes),
        scratch_shapes=scratch,
        compiler_params=PARAMS,
        name="adjoint",
    )(*args)
    total = out[0] if ends is None else out[:2]
    return total, (out[-2:] if span.hands_on else None)


def spans(nx, cut):
    reach = cut + 2 * RADIUS
    return [
        Span((0, cut), (0, reach), False, True),
        Span((cut, nx), (reach, nx + 2 * RADIUS), True, False),
    ]


def join_kernel(split, places, *refs):
    parts, out, sem = refs[: len(places)], refs[-2], refs[-1]
    chip, core = split.here()
    copies = []
    for part, (p0, p1, r, mine) in zip(parts, places):
        owner = lax.rem(chip + split.chips - r, split.chips)
        lanes = pl.ds(pl.multiple_of(owner * split.part, LANES), split.part)
        to = out.at[p0:p1, split.rows(core if mine else 1 - core), lanes]
        copies.append(pltpu.make_async_copy(part, to, sem.at[len(copies)]))
        copies[-1].start()
    for copy in copies:
        copy.wait()


def join(split, pieces, out, nx, nz):
    places, parts = zip(*pieces)
    return pl.pallas_call(
        functools.partial(join_kernel, split, places),
        out_shape=jax.ShapeDtypeStruct((nx, nz, split.ny), F32),
        in_specs=[VMEM] * len(parts) + ([] if out is None else [ANY]),
        out_specs=ANY,
        scratch_shapes=[pltpu.SemaphoreType.DMA((len(parts),))],
        input_output_aliases={} if out is None else {len(parts): 0},
        compiler_params=PARAMS,
        name="join",
    )(*parts, *([] if out is None else [out]))


def steps(recorded, psf_taps, estimate):
    views = lax.axis_size("view")
    tiles = lax.axis_size("tile")
    nx, nz, ny = estimate.shape
    cores = 2
    chips = views // cores
    part = ny // chips
    width = min(ny, part + (LANES if chips <= 2 else 2 * LANES))
    split = Split(chips, cores, part, width, ny, nz // cores, tiles)
    assert 2 * RADIUS * ITERS <= SLIVER and nx >= 2 * RADIUS
    flat = lambda a: a.reshape(-1, a.shape[-1])

    def swap_core(values):
        pairs = [(v, v ^ 1) for v in range(views)]
        return lax.ppermute(values, "view", pairs)

    def to_chip(values, r):
        pairs = [(v, (v + r * cores) % views) for v in range(views)]
        return lax.ppermute(values, "view", pairs)

    slabs = lax.axis_size("slab")
    axes = ("slab", "tile", "view")

    def partner(s, t, pair_b):
        u = ((t + 1) ^ 1) - 1 if pair_b else t ^ 1
        return (s, u) if 0 <= u < tiles else (s ^ 1, t)

    def pairs_of(is_b):
        pairs = []
        for s in range(slabs):
            for t in range(tiles):
                for v in range(views):
                    to, u = partner(s, t, is_b(v))
                    if to < slabs:
                        here = (s * tiles + t) * views + v
                        pairs.append((here, (to * tiles + u) * views + v))
        return pairs

    def pair_up(a, b):
        b = lax.ppermute(b, axes, pairs_of(lambda v: True))
        a = lax.ppermute(a, axes, pairs_of(lambda v: False))
        return a, b

    def estimate_rims(values):
        mine = lax.ppermute(values, axes, pairs_of(lambda v: v % cores == 1))
        return mine, swap_core(mine)

    recorded = recorded[0]

    def to_a(n, by_core=False):
        return (nx - n, 0, n, by_core)

    def to_b(n):
        return (0, nx - n, n, False)

    rim, body = RADIUS * nz, (nx - 2 * RADIUS) * nz
    end = 2 * rim + body
    outs = [(0, r, (to_a(RADIUS), to_b(RADIUS))) for r in range(1, chips)]
    outs.append((1, 0, (to_a(2 * RADIUS, True),)))
    *cuts, est_rim = cut((recorded, estimate), split, outs, ())
    taps = [psf_taps] + [to_chip(psf_taps, r) for r in range(1, chips)]
    edges = [None] + [to_chip(cuts[r - 1], r) for r in range(1, chips)]

    outs = [(0, r, ((RADIUS, RADIUS, nx - 2 * RADIUS, False),)) for r in range(1, chips)]
    outs += [(0, 0, ((0, 0, nx, False),)), (0, 0, (to_a(RADIUS),)), (0, 0, (to_b(RADIUS),))]
    outs += [(1, 0, ((0, 0, nx, False),))]
    whole = (chips - 1, chips + 2)
    *cuts, own, own_a, own_b, est = cut((recorded, estimate), split, outs, whole)
    middles = [None] + [to_chip(cuts[r - 1], r) for r in range(1, chips)]
    rims = estimate_rims(est_rim)
    own_a, own_b = pair_up(own_a, own_b)

    own_a, own_b = unpacked(split, (own_a, own_b), ((RADIUS,), (RADIUS,)))
    record = [(own_a, own_b, flat(own))]
    before = Piece(0, rim, 0, 0, 1, 0, 0)
    after = Piece(rim + end, rim, 1, 0, 0, 0, 1)
    pieces = [(before, Piece(rim, end, 2, 0, 2, 0), after)]
    for r in range(1, chips):
        one = edges[r].shape[0] // 2
        pair_a, pair_b = pair_up(edges[r][:one], edges[r][one:])
        arrays = (pair_a, pair_b, edges[r], middles[r])
        packs = ((RADIUS,), (RADIUS,), (RADIUS, RADIUS), (nx - 2 * RADIUS,))
        record.append(unpacked(split, arrays, packs))
        first = Piece(rim, rim, 2, 0, 2, rim)
        inner = Piece(2 * rim, body, 3, 0, 3, 0)
        last = Piece(2 * rim + body, rim, 2, rim, 2, 0)
        pieces.append((before, first, inner, last, after))

    ops = []
    for k in taps:
        ops.append(operators(k, nz))

    for iteration in range(ITERS):
        final = iteration == ITERS - 1
        blurred = []
        for r in range(chips):
            blurred.append(own_share(est, ops[r]))
        for mine in (True, False):
            rim_planes = rims[0] if mine else rims[1]
            blurred = rim_share(split, mine, blurred, rim_planes, ops)
        plan = spans(nx, nx // 2 if final else 2 * nx // 3)
        handed = [None] * chips
        sums = []
        for span in plan:
            total = None
            for r in range(chips):
                ends = part if final and r == chips - 1 else None
                total, handed[r] = adjoint(
                    split,
                    blurred[r],
                    record[r],
                    pieces[r],
                    ops[r],
                    span,
                    total,
                    handed[r],
                    nz,
                    ends,
                )
            keep, send = total if final else (total, total)
            sums.append((keep, swap_core(send)))
        if not final:
            planes = [span.planes for span in plan]
            est, est_rim = update(split, views, planes, sum(sums, ()), est)
            rims = estimate_rims(est_rim)

    early, late = [], []
    for c, (span, pair) in enumerate(zip(plan, sums)):
        done = finish(split, views, span.planes, *pair, est)
        for r in range(chips):
            mine = to_chip(done, r) if r else done
            sibling = swap_core(mine)
            pieces = late if r and c == len(plan) - 1 else early
            pieces.append(((*span.planes, r, True), mine))
            pieces.append(((*span.planes, r, False), sibling))
    out = join(split, early, None, nx, nz)
    return join(split, late, out, nx, nz)


def solution(mesh):
    in_specs = (P("view", "tile", "slab", None), P("view", None, None), P("tile", "slab", None))
    out_specs = P("tile", "slab", None)
    return jax.shard_map(steps, mesh=mesh, in_specs=in_specs, out_specs=out_specs, check_vma=False)
```
